32 devices in a mesh: dp: 2 (over x), fsdp: 16 (over z, y, core).
Axes of the slice: x: 2, y: 2, z: 4, core: 2. Of those that a mesh axis runs over, the one named last changes fastest.
Arguments:
- text_a: bfloat16 [32, 48, 768], P(('dp', 'fsdp')), may hold values from -6 to 6
- visual_a: bfloat16 [32, 20, 768], P(('dp', 'fsdp')), may hold values from -6 to 6
- text_b: bfloat16 [32, 56, 768], P(('dp', 'fsdp')), may hold values from -6 to 6
- visual_b: bfloat16 [32, 28, 768], P(('dp', 'fsdp')), may hold values from -6 to 6
- text_len_a: int32 [32], P(('dp', 'fsdp')), may hold values from 24 to 48
- visual_len_a: int32 [32], P(('dp', 'fsdp')), may hold values from 10 to 20
- text_len_b: int32 [32], P(('dp', 'fsdp')), may hold values from 28 to 56
- visual_len_b: int32 [32], P(('dp', 'fsdp')), may hold values from 14 to 28
- cot_text_a: bfloat16 [32, 48, 768], P(('dp', 'fsdp')), may hold values from -6 to 6
- cot_visual_a: bfloat16 [32, 20, 768], P(('dp', 'fsdp')), may hold values from -6 to 6
- cot_text_b: bfloat16 [32, 56, 768], P(('dp', 'fsdp')), may hold values from -6 to 6
- cot_visual_b: bfloat16 [32, 28, 768], P(('dp', 'fsdp')), may hold values from -6 to 6
- attn_in: bfloat16 [2, 6, 768, 768], P(None, None, 'fsdp'), may hold values from -0.21875 to 0.21875
- attn_out: bfloat16 [2, 2, 768, 768], P(None, None, 'fsdp'), may hold values from -0.625 to 0.625
- ffn_up: bfloat16 [2, 768, 3072], P(None, 'fsdp'), may hold values from -0.21875 to 0.21875
- ffn_down: bfloat16 [2, 3072, 768], P(None, 'fsdp'), may hold values from -0.109375 to 0.109375
- norm_gain: bfloat16 [2, 3, 768], P(None, None, 'fsdp'), may hold values from 0.5 to 1.5
- norm_bias: bfloat16 [2, 3, 768], P(None, None, 'fsdp'), may hold values from -2 to 2
- gate_vector: bfloat16 [2, 768], P(None, 'fsdp'), may hold values from -0.21875 to 0.21875
Outputs:
- out_text_a: bfloat16 [32, 48, 768], P(('dp', 'fsdp'))
- out_visual_a: bfloat16 [32, 20, 768], P(('dp', 'fsdp'))
- out_text_b: bfloat16 [32, 56, 768], P(('dp', 'fsdp'))
- out_visual_b: bfloat16 [32, 28, 768], P(('dp', 'fsdp'))
- grad_text_a: bfloat16 [32, 48, 768], P(('dp', 'fsdp'))
- grad_visual_a: bfloat16 [32, 20, 768], P(('dp', 'fsdp'))
- grad_text_b: bfloat16 [32, 56, 768], P(('dp', 'fsdp'))
- grad_visual_b: bfloat16 [32, 28, 768], P(('dp', 'fsdp'))
- grad_attn_in: float32 [2, 6, 768, 768], P(None, None, 'fsdp')
- grad_attn_out: float32 [2, 2, 768, 768], P(None, None, 'fsdp')
- grad_ffn_up: float32 [2, 768, 3072], P(None, 'fsdp')
- grad_ffn_down: float32 [2, 3072, 768], P(None, 'fsdp')
- grad_norm_gain: float32 [2, 3, 768], P(None, None, 'fsdp')
- grad_norm_bias: float32 [2, 3, 768], P(None, None, 'fsdp')
- grad_gate_vector: float32 [2, 768], P(None, 'fsdp')
The draws below stay inside these ranges and needn't reach their ends.
All inputs are finite; a program needn't handle non-finite values.
Results may differ from the reference program's by a relative error of at most 0.019.
Values may be sent and summed in bfloat16 or wider, within the bound.
A program may use at most 320 MiB of HBM per device.

```python
import math
import jax
import jax.numpy as jnp
from jax import lax

D = 768
HEADS = 12
FF = 3072
HEAD_DIM = 64
LT_A = 48
LV_A = 20
LT_B = 56
LV_B = 28
PAGES = 32


def touch_ends(drawn, rng, low, largest):
    longest = drawn.shape.index(max(drawn.shape))
    spots = []
    for shift in (0, 1):
        where = [jax.random.randint(jax.random.fold_in(rng, axis), (), 0, length) for axis, length in enumerate(drawn.shape)]
        where[longest] = (where[longest] + shift) % drawn.shape[longest]
        spots.append(tuple(where))
    return drawn.at[spots[0]].set(low).at[spots[1]].set(largest)


def block_scale(rng, dims, split, smallest, largest):
    def one(position, shards_of):
        heights = jax.random.uniform(jax.random.fold_in(jax.random.fold_in(rng, 6), position), (shards_of,), jnp.float32, smallest / len(split), largest / len(split))
        return jnp.repeat(jnp.exp(heights), dims[position] // shards_of).reshape((-1,) + (1,) * (len(dims) - position - 1))

    loudness = one(*split[0])
    for cut in split[1:]:
        loudness = loudness * one(*cut)
    return loudness


def noise(key, shape, scale, reach, shards=(), kind=jnp.bfloat16):
    loudness = block_scale(key, shape, shards, -0.22, 0.18) if shards else 1.0
    entries = jax.random.normal(key, shape, jnp.float32) * scale * loudness
    return jnp.minimum(jnp.maximum(entries, -reach), reach).astype(kind)


def setup_inputs(seed: int = 0) -> dict:
    splits = jax.random.split(jax.random.key(seed), 20)
    text_a = noise(splits[0], (PAGES, LT_A, D), 1.0, 6.0, ((0, 32),))
    visual_a = noise(splits[1], (PAGES, LV_A, D), 1.0, 6.0, ((0, 32),))
    text_b = noise(splits[2], (PAGES, LT_B, D), 1.0, 6.0, ((0, 32),))
    visual_b = noise(splits[3], (PAGES, LV_B, D), 1.0, 6.0, ((0, 32),))
    text_len_a = touch_ends(jax.random.randint(splits[4], (PAGES,), LT_A // 2, LT_A + 1), jax.random.fold_in(splits[4], 1), LT_A // 2, LT_A).astype(jnp.int32)
    visual_len_a = touch_ends(jax.random.randint(splits[5], (PAGES,), LV_A // 2, LV_A + 1), jax.random.fold_in(splits[5], 1), LV_A // 2, LV_A).astype(jnp.int32)
    text_len_b = touch_ends(jax.random.randint(splits[6], (PAGES,), LT_B // 2, LT_B + 1), jax.random.fold_in(splits[6], 1), LT_B // 2, LT_B).astype(jnp.int32)
    visual_len_b = touch_ends(jax.random.randint(splits[7], (PAGES,), LV_B // 2, LV_B + 1), jax.random.fold_in(splits[7], 1), LV_B // 2, LV_B).astype(jnp.int32)
    cot_text_a = noise(splits[8], (PAGES, LT_A, D), 1.0, 6.0, ((0, 32),))
    cot_visual_a = noise(splits[9], (PAGES, LV_A, D), 1.0, 6.0, ((0, 32),))
    cot_text_b = noise(splits[10], (PAGES, LT_B, D), 1.0, 6.0, ((0, 32),))
    cot_visual_b = noise(splits[11], (PAGES, LV_B, D), 1.0, 6.0, ((0, 32),))
    attn_in = noise(splits[12], (2, 6, D, D), D ** -0.5, 0.21875, ((2, 16),))
    attn_out = noise(splits[13], (2, 2, D, D), (D // 8) ** -0.5, 0.625, ((2, 16),))
    ffn_up = noise(splits[14], (2, D, FF), D ** -0.5, 0.21875, ((1, 16),))
    ffn_down = noise(splits[15], (2, FF, D), FF ** -0.5, 0.109375, ((1, 16),))
    norm_gain = jnp.clip(1.0 + 0.1 * jax.random.normal(splits[16], (2, 3, D), jnp.float32), 0.5, 1.5).astype(jnp.bfloat16)
    norm_bias = noise(splits[17], (2, 3, D), 0.3, 2.0, ((2, 16),))
    gate_vector = noise(splits[18], (2, D), D ** -0.5, 0.21875, ((1, 16),))
    return {"text_a": text_a, "visual_a": visual_a, "text_b": text_b, "visual_b": visual_b, "text_len_a": text_len_a, "visual_len_a": visual_len_a, "text_len_b": text_len_b, "visual_len_b": visual_len_b, "cot_text_a": cot_text_a, "cot_visual_a": cot_visual_a, "cot_text_b": cot_text_b, "cot_visual_b": cot_visual_b, "attn_in": attn_in, "attn_out": attn_out, "ffn_up": ffn_up, "ffn_down": ffn_down, "norm_gain": norm_gain, "norm_bias": norm_bias, "gate_vector": gate_vector}


@jax.custom_vjp
def low(v):
    return lax.optimization_barrier(v.astype(jnp.bfloat16)).astype(jnp.float32)

@jax.custom_vjp
def low_back(v):
    return v

def low_keep(v):
    return (low(v), None)

def low_pass(kept, grad):
    return (grad,)

def back_keep(v):
    return (v, None)

def back_low(kept, grad):
    return (low(grad),)
low.defvjp(low_keep, low_pass)
low_back.defvjp(back_keep, back_low)

def rounded_both(value):
    return low_back(low(value))

def project(rows, matrix):
    return jnp.einsum('pld,de->ple', rows, matrix, precision=lax.Precision.HIGHEST)

def layer_norm(resid, gain_row, bias_row):
    centre = resid - lax.optimization_barrier(jnp.mean(resid, axis=-1, keepdims=True))
    spread = lax.optimization_barrier(jnp.mean(centre * centre, axis=-1, keepdims=True))
    return centre * lax.rsqrt(spread + 1e-05) * gain_row + bias_row

def split_heads(rows):
    return rows.reshape(rows.shape[0], rows.shape[1], HEADS, HEAD_DIM)

def attend(queries, key_rows, value_rows, key_mask):
    score_scale = 1.0 / math.sqrt(HEAD_DIM)
    raw_scores = jnp.einsum('plhe,pmhe->phlm', split_heads(queries), split_heads(key_rows), precision=lax.Precision.HIGHEST)
    scores = low_back(raw_scores * score_scale)
    masked = jnp.where(key_mask[:, None, None, :], scores, -1000000000.0)
    probs_low = low(jax.nn.softmax(masked, axis=-1))
    mixed = jnp.einsum('phlm,pmhe->plhe', probs_low, split_heads(value_rows), precision=lax.Precision.HIGHEST)
    return rounded_both(mixed.reshape(queries.shape))

def stream_layer(own_rows, other_rows, own_keys, other_keys, row_mask, params):
    attn_in, attn_out, ffn_up, ffn_down, norm_gain, norm_bias, gate_row = params
    query_cross = rounded_both(project(own_rows, attn_in[0]))
    key_cross = rounded_both(project(other_rows, attn_in[1]))
    value_cross = rounded_both(project(other_rows, attn_in[2]))
    cross_out = low_back(project(attend(query_cross, key_cross, value_cross, other_keys), attn_out[0]))
    hidden_one = layer_norm(own_rows + cross_out, norm_gain[0], norm_bias[0])
    hidden_low = low(hidden_one)
    query_self = rounded_both(project(hidden_low, attn_in[3]))
    key_self = rounded_both(project(hidden_low, attn_in[4]))
    value_self = rounded_both(project(hidden_low, attn_in[5]))
    self_out = low_back(project(attend(query_self, key_self, value_self, own_keys), attn_out[1]))
    hidden_two = layer_norm(hidden_one + self_out, norm_gain[1], norm_bias[1])
    ffn_in = low(hidden_two)
    upward = low_back(project(ffn_in, ffn_up))
    active = low(jax.nn.gelu(upward, approximate=False))
    downward = low_back(project(active, ffn_down))
    hidden_three = layer_norm(hidden_two + downward, norm_gain[2], norm_bias[2])
    logit = jnp.einsum('pld,d->pl', hidden_three, gate_row, precision=lax.Precision.HIGHEST)
    return hidden_three * (jax.nn.sigmoid(logit) * row_mask)[..., None]

def page_pair(params, text_rows, visual_rows, text_keys, visual_keys):
    text_mask = text_keys.astype(jnp.float32)
    visual_mask = visual_keys.astype(jnp.float32)
    text_params = tuple((item[0] for item in params))
    visual_params = tuple((item[1] for item in params))
    text_out = stream_layer(text_rows, visual_rows, text_keys, visual_keys, text_mask, text_params)
    visual_out = stream_layer(visual_rows, text_rows, visual_keys, text_keys, visual_mask, visual_params)
    return (text_out, visual_out)

def run_layout(params, text_rows, visual_rows, text_len, visual_len, cot_text, cot_visual):
    page_total = text_rows.shape[0]
    group_size = math.gcd(page_total, 16)
    step_count = page_total // group_size

    def regroup(array):
        return array.reshape((step_count, group_size) + array.shape[1:])

    def step_fn(carry, batch):
        rows_text, rows_visual, len_text, len_visual, grad_in_text, grad_in_visual = batch
        text_keys = jnp.arange(rows_text.shape[1], dtype=jnp.int32)[None, :] < len_text[:, None]
        visual_keys = jnp.arange(rows_visual.shape[1], dtype=jnp.int32)[None, :] < len_visual[:, None]

        def forward_fn(weights, text_f, visual_f):
            return page_pair(weights, text_f, visual_f, text_keys, visual_keys)
        outputs, pull_back = jax.vjp(forward_fn, params, rows_text.astype(jnp.float32), rows_visual.astype(jnp.float32))
        weight_grads, grad_text, grad_visual = pull_back((grad_in_text.astype(jnp.float32), grad_in_visual.astype(jnp.float32)))
        carry = jax.tree.map(jnp.add, carry, weight_grads)
        return (carry, (outputs[0].astype(jnp.bfloat16), outputs[1].astype(jnp.bfloat16), grad_text.astype(jnp.bfloat16), grad_visual.astype(jnp.bfloat16)))
    initial = jax.tree.map(jnp.zeros_like, params)
    totals, stacked = lax.scan(step_fn, initial, (regroup(text_rows), regroup(visual_rows), regroup(text_len), regroup(visual_len), regroup(cot_text), regroup(cot_visual)))
    flat = tuple((item.reshape((page_total,) + item.shape[2:]) for item in stacked))
    return (totals, flat)

def reference(text_a, visual_a, text_b, visual_b, text_len_a, visual_len_a, text_len_b, visual_len_b, cot_text_a, cot_visual_a, cot_text_b, cot_visual_b, attn_in, attn_out, ffn_up, ffn_down, norm_gain, norm_bias, gate_vector):
    params = (attn_in.astype(jnp.float32), attn_out.astype(jnp.float32), ffn_up.astype(jnp.float32), ffn_down.astype(jnp.float32), norm_gain.astype(jnp.float32), norm_bias.astype(jnp.float32), gate_vector.astype(jnp.float32))
    grads_first, rows_first = run_layout(params, text_a, visual_a, text_len_a, visual_len_a, cot_text_a, cot_visual_a)
    grads_second, rows_second = run_layout(params, text_b, visual_b, text_len_b, visual_len_b, cot_text_b, cot_visual_b)
    return (rows_first[0], rows_first[1], rows_second[0], rows_second[1], rows_first[2], rows_first[3], rows_second[2], rows_second[3], grads_first[0] + grads_second[0], grads_first[1] + grads_second[1], grads_first[2] + grads_second[2], grads_first[3] + grads_second[3], grads_first[4] + grads_second[4], grads_first[5] + grads_second[5], grads_first[6] + grads_second[6])
```

```python
from functools import partial
import math

import jax
import jax.numpy as jnp
from jax import lax
from jax.sharding import PartitionSpec as P

HEADS = 12


def project(rows, matrix):
    return jnp.einsum("pld,de->ple", rows, matrix, preferred_element_type=jnp.float32)


def project_back(grads, matrix):
    return jnp.einsum("ple,de->pld", grads, matrix, preferred_element_type=jnp.float32)


def weight_grad(rows, grads):
    return jnp.einsum("pld,ple->de", rows, grads, preferred_element_type=jnp.float32)


def layer_norm(resid, gain_row, bias_row):
    centre = resid - jnp.mean(resid, axis=-1, keepdims=True)
    spread = jnp.mean(centre * centre, axis=-1, keepdims=True)
    return centre * lax.rsqrt(spread + 1e-05) * gain_row + bias_row


def gate_tail(resid, gain_row, bias_row, gate_row, row_mask):
    hidden_three = layer_norm(resid, gain_row, bias_row)
    logit = jnp.einsum("pld,d->pl", hidden_three, gate_row, precision=lax.Precision.HIGHEST)
    return hidden_three * (jax.nn.sigmoid(logit) * row_mask)[..., None]


def exact_gelu(upward):
    return jax.nn.gelu(upward, approximate=False)


def split_heads(rows):
    return rows.reshape(rows.shape[0], rows.shape[1], HEADS, rows.shape[2] // HEADS)


def masked_scores(queries, key_rows, key_mask):
    score_scale = 1.0 / math.sqrt(queries.shape[2] // HEADS)
    scores = (
        jnp.einsum(
            "plhe,pmhe->phlm",
            split_heads(queries),
            split_heads(key_rows),
            preferred_element_type=jnp.float32,
        )
        * score_scale
    )
    return jnp.where(key_mask[:, None, None, :], scores, -1000000000.0)


def attend_forward(queries, key_rows, value_rows, key_mask):
    masked = masked_scores(queries, key_rows, key_mask)
    row_max = jnp.max(masked, axis=-1, keepdims=True)
    expon = jnp.exp(masked - row_max)
    row_sum = jnp.sum(expon, axis=-1, keepdims=True)
    probs = expon / row_sum
    log_total = row_max + jnp.log(row_sum)
    mixed = jnp.einsum(
        "phlm,pmhe->plhe",
        probs.astype(jnp.bfloat16),
        split_heads(value_rows),
        preferred_element_type=jnp.float32,
    )
    return (mixed.reshape(queries.shape).astype(jnp.bfloat16), log_total)


def attend_backward(queries, key_rows, value_rows, key_mask, log_total, grad_mixed):
    score_scale = 1.0 / math.sqrt(queries.shape[2] // HEADS)
    masked = masked_scores(queries, key_rows, key_mask)
    probs = jnp.where(key_mask[:, None, None, :], jnp.exp(masked - log_total), 0.0)
    grad_heads = split_heads(grad_mixed)
    grad_probs = jnp.einsum(
        "plhe,pmhe->phlm", grad_heads, split_heads(value_rows), preferred_element_type=jnp.float32
    )
    grad_scores = (
        probs * (grad_probs - jnp.sum(grad_probs * probs, axis=-1, keepdims=True))
    ).astype(jnp.bfloat16)
    grad_query = (
        jnp.einsum(
            "phlm,pmhe->plhe",
            grad_scores,
            split_heads(key_rows),
            preferred_element_type=jnp.float32,
        )
        * score_scale
    )
    grad_key = (
        jnp.einsum(
            "phlm,plhe->pmhe", grad_scores, split_heads(queries), preferred_element_type=jnp.float32
        )
        * score_scale
    )
    grad_value = jnp.einsum(
        "phlm,plhe->pmhe",
        probs.astype(jnp.bfloat16),
        grad_heads,
        preferred_element_type=jnp.float32,
    )
    return (
        grad_query.reshape(queries.shape).astype(jnp.bfloat16),
        grad_key.reshape(key_rows.shape).astype(jnp.bfloat16),
        grad_value.reshape(value_rows.shape).astype(jnp.bfloat16),
    )


def cross_forward(own_rows, other_rows, other_keys, attn_in):
    cross_query = project(own_rows, attn_in[0]).astype(jnp.bfloat16)
    cross_key = project(other_rows, attn_in[1]).astype(jnp.bfloat16)
    cross_value = project(other_rows, attn_in[2]).astype(jnp.bfloat16)
    cross_mixed, cross_total = attend_forward(cross_query, cross_key, cross_value, other_keys)
    return ((cross_query, cross_key, cross_value), cross_mixed, cross_total)


def stream_forward(own_rows, other_rows, own_keys, other_keys, row_mask, params):
    attn_in, attn_out, ffn_up, ffn_down, gains, biases, gate_row = params
    _, cross_mixed, _ = cross_forward(own_rows, other_rows, other_keys, attn_in)
    resid_one = own_rows.astype(jnp.float32) + project(cross_mixed, attn_out[0])
    hidden_one = layer_norm(resid_one, gains[0], biases[0])
    hidden_low = hidden_one.astype(jnp.bfloat16)
    self_query = project(hidden_low, attn_in[3]).astype(jnp.bfloat16)
    self_key = project(hidden_low, attn_in[4]).astype(jnp.bfloat16)
    self_value = project(hidden_low, attn_in[5]).astype(jnp.bfloat16)
    self_mixed, self_total = attend_forward(self_query, self_key, self_value, own_keys)
    resid_two = hidden_one + project(self_mixed, attn_out[1])
    hidden_two = layer_norm(resid_two, gains[1], biases[1])
    ffn_in = hidden_two.astype(jnp.bfloat16)
    upward = project(ffn_in, ffn_up)
    active = exact_gelu(upward).astype(jnp.bfloat16)
    resid_three = hidden_two + project(active, ffn_down)
    output = gate_tail(resid_three, gains[2], biases[2], gate_row, row_mask)
    saved_rows = (
        resid_one,
        hidden_low,
        self_query,
        self_key,
        self_value,
        self_total,
        self_mixed,
        resid_two,
        ffn_in,
        upward,
        active,
        resid_three,
    )
    return (output, saved_rows)


def stream_backward(
    own_rows, other_rows, own_keys, other_keys, row_mask, params, saved_rows, grad_out
):
    attn_in, attn_out, ffn_up, ffn_down, gains, biases, gate_row = params
    (
        resid_one,
        hidden_low,
        self_query,
        self_key,
        self_value,
        self_total,
        self_mixed,
        resid_two,
        ffn_in,
        upward,
        active,
        resid_three,
    ) = saved_rows
    _, tail_pull = jax.vjp(
        partial(gate_tail, row_mask=row_mask), resid_three, gains[2], biases[2], gate_row
    )
    grad_three, gain_three, bias_three, grad_gate = tail_pull(grad_out)
    grad_down_in = grad_three.astype(jnp.bfloat16)
    down_grad = weight_grad(active, grad_down_in)
    grad_active = project_back(grad_down_in, ffn_down)
    _, gelu_pull = jax.vjp(exact_gelu, upward)
    grad_upward = gelu_pull(grad_active)[0].astype(jnp.bfloat16)
    up_grad = weight_grad(ffn_in, grad_upward)
    grad_two = grad_three + project_back(grad_upward, ffn_up)
    _, norm_two_pull = jax.vjp(layer_norm, resid_two, gains[1], biases[1])
    grad_resid_two, gain_two, bias_two = norm_two_pull(grad_two)
    grad_self_out = grad_resid_two.astype(jnp.bfloat16)
    self_out_grad = weight_grad(self_mixed, grad_self_out)
    grad_self_mixed = project_back(grad_self_out, attn_out[1]).astype(jnp.bfloat16)
    grad_self_query, grad_self_key, grad_self_value = attend_backward(
        self_query, self_key, self_value, own_keys, self_total, grad_self_mixed
    )
    grad_one = (
        grad_resid_two
        + project_back(grad_self_query, attn_in[3])
        + project_back(grad_self_key, attn_in[4])
        + project_back(grad_self_value, attn_in[5])
    )
    _, norm_one_pull = jax.vjp(layer_norm, resid_one, gains[0], biases[0])
    grad_resid_one, gain_one, bias_one = norm_one_pull(grad_one)
    grad_cross_out = grad_resid_one.astype(jnp.bfloat16)
    (cross_query, cross_key, cross_value), cross_mixed, cross_total = cross_forward(
        own_rows, other_rows, other_keys, attn_in
    )
    cross_out_grad = weight_grad(cross_mixed, grad_cross_out)
    grad_cross_mixed = project_back(grad_cross_out, attn_out[0]).astype(jnp.bfloat16)
    grad_cross_query, grad_cross_key, grad_cross_value = attend_backward(
        cross_query, cross_key, cross_value, other_keys, cross_total, grad_cross_mixed
    )
    grad_own = grad_resid_one + project_back(grad_cross_query, attn_in[0])
    grad_other = project_back(grad_cross_key, attn_in[1]) + project_back(
        grad_cross_value, attn_in[2]
    )
    in_grads = jnp.stack(
        [
            weight_grad(own_rows, grad_cross_query),
            weight_grad(other_rows, grad_cross_key),
            weight_grad(other_rows, grad_cross_value),
            weight_grad(hidden_low, grad_self_query),
            weight_grad(hidden_low, grad_self_key),
            weight_grad(hidden_low, grad_self_value),
        ]
    )
    out_grads = jnp.stack([cross_out_grad, self_out_grad])
    gain_grads = jnp.stack([gain_one, gain_two, gain_three])
    bias_grads = jnp.stack([bias_one, bias_two, bias_three])
    return (
        grad_own,
        grad_other,
        (in_grads, out_grads, up_grad, down_grad, gain_grads, bias_grads, grad_gate),
    )


def stream_params(gathered, stream):
    return (
        gathered[0][stream],
        gathered[1][stream],
        gathered[2][stream],
        gathered[3][stream],
        gathered[4][stream].astype(jnp.float32),
        gathered[5][stream].astype(jnp.float32),
        gathered[6][stream].astype(jnp.float32),
    )


def per_device(
    text_a,
    visual_a,
    text_b,
    visual_b,
    text_len_a,
    visual_len_a,
    text_len_b,
    visual_len_b,
    cot_text_a,
    cot_visual_a,
    cot_text_b,
    cot_visual_b,
    attn_in,
    attn_out,
    ffn_up,
    ffn_down,
    norm_gain,
    norm_bias,
    gate_vector,
):
    gathered = (
        lax.all_gather(attn_in, "fsdp", axis=2, tiled=True),
        lax.all_gather(attn_out, "fsdp", axis=2, tiled=True),
        lax.all_gather(ffn_up, "fsdp", axis=1, tiled=True),
        lax.all_gather(ffn_down, "fsdp", axis=1, tiled=True),
        lax.all_gather(norm_gain, "fsdp", axis=2, tiled=True),
        lax.all_gather(norm_bias, "fsdp", axis=2, tiled=True),
        lax.all_gather(gate_vector, "fsdp", axis=1, tiled=True),
    )
    layouts = []
    for rows_text, rows_visual, len_text, len_visual, cot_text, cot_visual in (
        (text_a, visual_a, text_len_a, visual_len_a, cot_text_a, cot_visual_a),
        (text_b, visual_b, text_len_b, visual_len_b, cot_text_b, cot_visual_b),
    ):
        keys_text = jnp.arange(rows_text.shape[1], dtype=jnp.int32)[None, :] < len_text[:, None]
        keys_visual = (
            jnp.arange(rows_visual.shape[1], dtype=jnp.int32)[None, :] < len_visual[:, None]
        )
        stream_rows = (rows_text, rows_visual)
        stream_keys = (keys_text, keys_visual)
        stream_masks = (keys_text.astype(jnp.float32), keys_visual.astype(jnp.float32))
        outputs = []
        saved_list = []
        for stream in (0, 1):
            other_side = 1 - stream
            output, saved_rows = stream_forward(
                stream_rows[stream],
                stream_rows[other_side],
                stream_keys[stream],
                stream_keys[other_side],
                stream_masks[stream],
                stream_params(gathered, stream),
            )
            outputs.append(output.astype(jnp.bfloat16))
            saved_list.append(saved_rows)
        layouts.append(
            (stream_rows, stream_keys, stream_masks, (cot_text, cot_visual), outputs, saved_list)
        )
    back_weights = gathered
    input_grads = [[None, None], [None, None]]
    stream_grads = []
    for stream in (0, 1):
        other_side = 1 - stream
        params = stream_params(back_weights, stream)
        summed = None
        for layout_index in (0, 1):
            stream_rows, stream_keys, stream_masks, cotangents, outputs, saved_list = layouts[
                layout_index
            ]
            grad_own, grad_other, grads_here = stream_backward(
                stream_rows[stream],
                stream_rows[other_side],
                stream_keys[stream],
                stream_keys[other_side],
                stream_masks[stream],
                params,
                saved_list[stream],
                cotangents[stream].astype(jnp.float32),
            )
            for target, piece in ((stream, grad_own), (other_side, grad_other)):
                if input_grads[layout_index][target] is None:
                    input_grads[layout_index][target] = piece
                else:
                    input_grads[layout_index][target] = input_grads[layout_index][target] + piece
            if summed is None:
                summed = grads_here
            else:
                summed = tuple((left + right for left, right in zip(summed, grads_here)))
        stream_grads.append(summed)
    text_grads = stream_grads[0]
    visual_grads = stream_grads[1]
    row_dims = (1, 1, 0, 0, 1, 1, 0)
    packed = tuple(
        (
            jnp.concatenate([text_grads[index], visual_grads[index]], axis=row_dims[index])
            for index in range(7)
        )
    )
    axes = ("dp", "fsdp")
    shares = tuple(
        lax.psum_scatter(
            packed[index].astype(jnp.bfloat16), axes, scatter_dimension=row_dims[index], tiled=True
        )
        for index in range(7)
    )
    joined = tuple(
        lax.all_gather(shares[index], "dp", axis=row_dims[index], tiled=True).astype(jnp.float32)
        for index in range(7)
    )
    finals = tuple(
        (jnp.stack(jnp.split(joined[index], 2, axis=row_dims[index])) for index in range(7))
    )
    first_outputs = layouts[0][4]
    second_outputs = layouts[1][4]
    return (
        first_outputs[0],
        first_outputs[1],
        second_outputs[0],
        second_outputs[1],
        input_grads[0][0].astype(jnp.bfloat16),
        input_grads[0][1].astype(jnp.bfloat16),
        input_grads[1][0].astype(jnp.bfloat16),
        input_grads[1][1].astype(jnp.bfloat16),
        finals[0],
        finals[1],
        finals[2],
        finals[3],
        finals[4],
        finals[5],
        finals[6],
    )


def solution(mesh):
    in_specs = (
        P(("dp", "fsdp"), None, None),
        P(("dp", "fsdp"), None, None),
        P(("dp", "fsdp"), None, None),
        P(("dp", "fsdp"), None, None),
        P(("dp", "fsdp")),
        P(("dp", "fsdp")),
        P(("dp", "fsdp")),
        P(("dp", "fsdp")),
        P(("dp", "fsdp"), None, None),
        P(("dp", "fsdp"), None, None),
        P(("dp", "fsdp"), None, None),
        P(("dp", "fsdp"), None, None),
        P(None, None, "fsdp", None),
        P(None, None, "fsdp", None),
        P(None, "fsdp", None),
        P(None, "fsdp", None),
        P(None, None, "fsdp"),
        P(None, None, "fsdp"),
        P(None, "fsdp"),
    )
    out_specs = (
        P(("dp", "fsdp"), None, None),
        P(("dp", "fsdp"), None, None),
        P(("dp", "fsdp"), None, None),
        P(("dp", "fsdp"), None, None),
        P(("dp", "fsdp"), None, None),
        P(("dp", "fsdp"), None, None),
        P(("dp", "fsdp"), None, None),
        P(("dp", "fsdp"), None, None),
        P(None, None, "fsdp", None),
        P(None, None, "fsdp", None),
        P(None, "fsdp", None),
        P(None, "fsdp", None),
        P(None, None, "fsdp"),
        P(None, None, "fsdp"),
        P(None, "fsdp"),
    )
    return jax.shard_map(
        per_device, mesh=mesh, in_specs=in_specs, out_specs=out_specs, check_vma=False
    )
```

```python
from functools import partial
import math

import jax
import jax.numpy as jnp
from jax import lax
from jax.experimental import pallas as pl
from jax.experimental.pallas import tpu as pltpu
from jax.sharding import PartitionSpec as P

HEADS = 12
BF = jnp.bfloat16
F32 = jnp.float32
MESH_ID = pl.DeviceIdType.MESH
NEG = -1000000000.0


def dot(a, b):
    return lax.dot_general(a, b, (((1,), (0,)), ((), ())), preferred_element_type=F32)


def dot_rt(a, b):
    return lax.dot_general(a, b, (((1,), (1,)), ((), ())), preferred_element_type=F32)


def dot_lt(a, b):
    return lax.dot_general(a, b, (((0,), (0,)), ((), ())), preferred_element_type=F32)


def loop(count, body):
    def step(index, carry):
        body(index)
        return carry

    lax.fori_loop(0, count, step, 0)


def cols(index, size):
    return pl.ds(pl.multiple_of(index * size, size), size)


def erf_of(value):
    x = jnp.minimum(jnp.maximum(value, -3.832506856900711), 3.832506856900711)
    y = x * x
    top = jnp.full_like(y, 0.00022905065861350646)
    for c in (0.0034082910107109506, 0.050955695062380861, 0.18520832239976145, 1.128379143519084):
        top = top * y + c
    low = jnp.full_like(y, -1.1791602954361697e-7)
    for c in (
        0.000023547966471313185,
        0.0010179625278914885,
        0.014070470171167667,
        0.11098505178285362,
        0.49746925110067538,
        1.0,
    ):
        low = low * y + c
    return x * top / low


def project(rows, matrix):
    return jnp.einsum("pld,de->ple", rows, matrix, preferred_element_type=jnp.float32)


def project_back(grads, matrix):
    return jnp.einsum("ple,de->pld", grads, matrix, preferred_element_type=jnp.float32)


def weight_grad(rows, grads):
    return jnp.einsum("pld,ple->de", rows, grads, preferred_element_type=jnp.float32)


def layer_norm(resid, gain_row, bias_row):
    centre = resid - jnp.mean(resid, axis=-1, keepdims=True)
    spread = jnp.mean(centre * centre, axis=-1, keepdims=True)
    return centre * lax.rsqrt(spread + 1e-05) * gain_row + bias_row


def gate_tail(resid, gain_row, bias_row, gate_row, row_mask):
    hidden_three = layer_norm(resid, gain_row, bias_row)
    logit = jnp.einsum("pld,d->pl", hidden_three, gate_row, precision=lax.Precision.HIGHEST)
    return hidden_three * (jax.nn.sigmoid(logit) * row_mask)[..., None]


def exact_gelu(upward):
    return jax.nn.gelu(upward, approximate=False)


def split_heads(rows):
    return rows.reshape(rows.shape[0], rows.shape[1], HEADS, rows.shape[2] // HEADS)


def masked_scores(queries, key_rows, key_mask):
    score_scale = 1.0 / math.sqrt(queries.shape[2] // HEADS)
    scores = (
        jnp.einsum(
            "plhe,pmhe->phlm",
            split_heads(queries),
            split_heads(key_rows),
            preferred_element_type=jnp.float32,
        )
        * score_scale
    )
    return jnp.where(key_mask[:, None, None, :], scores, -1000000000.0)


def attend_forward(queries, key_rows, value_rows, key_mask):
    masked = masked_scores(queries, key_rows, key_mask)
    row_max = jnp.max(masked, axis=-1, keepdims=True)
    expon = jnp.exp(masked - row_max)
    row_sum = jnp.sum(expon, axis=-1, keepdims=True)
    probs = expon / row_sum
    log_total = row_max + jnp.log(row_sum)
    mixed = jnp.einsum(
        "phlm,pmhe->plhe",
        probs.astype(jnp.bfloat16),
        split_heads(value_rows),
        preferred_element_type=jnp.float32,
    )
    return (mixed.reshape(queries.shape).astype(jnp.bfloat16), log_total)


def attend_backward(queries, key_rows, value_rows, key_mask, log_total, grad_mixed):
    score_scale = 1.0 / math.sqrt(queries.shape[2] // HEADS)
    masked = masked_scores(queries, key_rows, key_mask)
    probs = jnp.where(key_mask[:, None, None, :], jnp.exp(masked - log_total), 0.0)
    grad_heads = split_heads(grad_mixed)
    grad_probs = jnp.einsum(
        "plhe,pmhe->phlm", grad_heads, split_heads(value_rows), preferred_element_type=jnp.float32
    )
    grad_scores = (
        probs * (grad_probs - jnp.sum(grad_probs * probs, axis=-1, keepdims=True))
    ).astype(jnp.bfloat16)
    grad_query = (
        jnp.einsum(
            "phlm,pmhe->plhe",
            grad_scores,
            split_heads(key_rows),
            preferred_element_type=jnp.float32,
        )
        * score_scale
    )
    grad_key = (
        jnp.einsum(
            "phlm,plhe->pmhe", grad_scores, split_heads(queries), preferred_element_type=jnp.float32
        )
        * score_scale
    )
    grad_value = jnp.einsum(
        "phlm,plhe->pmhe",
        probs.astype(jnp.bfloat16),
        grad_heads,
        preferred_element_type=jnp.float32,
    )
    return (
        grad_query.reshape(queries.shape).astype(jnp.bfloat16),
        grad_key.reshape(key_rows.shape).astype(jnp.bfloat16),
        grad_value.reshape(value_rows.shape).astype(jnp.bfloat16),
    )


def cross_forward(own_rows, other_rows, other_keys, attn_in):
    cross_query = project(own_rows, attn_in[0]).astype(jnp.bfloat16)
    cross_key = project(other_rows, attn_in[1]).astype(jnp.bfloat16)
    cross_value = project(other_rows, attn_in[2]).astype(jnp.bfloat16)
    cross_mixed, cross_total = attend_forward(cross_query, cross_key, cross_value, other_keys)
    return ((cross_query, cross_key, cross_value), cross_mixed, cross_total)


def stream_forward(own_rows, other_rows, own_keys, other_keys, row_mask, params):
    attn_in, attn_out, ffn_up, ffn_down, gains, biases, gate_row = params
    _, cross_mixed, _ = cross_forward(own_rows, other_rows, other_keys, attn_in)
    resid_one = own_rows.astype(jnp.float32) + project(cross_mixed, attn_out[0])
    hidden_one = layer_norm(resid_one, gains[0], biases[0])
    hidden_low = hidden_one.astype(jnp.bfloat16)
    self_query = project(hidden_low, attn_in[3]).astype(jnp.bfloat16)
    self_key = project(hidden_low, attn_in[4]).astype(jnp.bfloat16)
    self_value = project(hidden_low, attn_in[5]).astype(jnp.bfloat16)
    self_mixed, self_total = attend_forward(self_query, self_key, self_value, own_keys)
    resid_two = hidden_one + project(self_mixed, attn_out[1])
    hidden_two = layer_norm(resid_two, gains[1], biases[1])
    ffn_in = hidden_two.astype(jnp.bfloat16)
    upward = project(ffn_in, ffn_up)
    active = exact_gelu(upward).astype(jnp.bfloat16)
    resid_three = hidden_two + project(active, ffn_down)
    output = gate_tail(resid_three, gains[2], biases[2], gate_row, row_mask)
    saved_rows = (
        resid_one,
        hidden_low,
        self_query,
        self_key,
        self_value,
        self_total,
        self_mixed,
        resid_two,
        ffn_in,
        upward,
        active,
        resid_three,
    )
    return (output, saved_rows)


def stream_backward(
    own_rows, other_rows, own_keys, other_keys, row_mask, params, saved_rows, grad_out
):
    attn_in, attn_out, ffn_up, ffn_down, gains, biases, gate_row = params
    (
        resid_one,
        hidden_low,
        self_query,
        self_key,
        self_value,
        self_total,
        self_mixed,
        resid_two,
        ffn_in,
        upward,
        active,
        resid_three,
    ) = saved_rows
    _, tail_pull = jax.vjp(
        partial(gate_tail, row_mask=row_mask), resid_three, gains[2], biases[2], gate_row
    )
    grad_three, gain_three, bias_three, grad_gate = tail_pull(grad_out)
    grad_down_in = grad_three.astype(jnp.bfloat16)
    down_grad = weight_grad(active, grad_down_in)
    grad_active = project_back(grad_down_in, ffn_down)
    _, gelu_pull = jax.vjp(exact_gelu, upward)
    grad_upward = gelu_pull(grad_active)[0].astype(jnp.bfloat16)
    up_grad = weight_grad(ffn_in, grad_upward)
    grad_two = grad_three + project_back(grad_upward, ffn_up)
    _, norm_two_pull = jax.vjp(layer_norm, resid_two, gains[1], biases[1])
    grad_resid_two, gain_two, bias_two = norm_two_pull(grad_two)
    grad_self_out = grad_resid_two.astype(jnp.bfloat16)
    self_out_grad = weight_grad(self_mixed, grad_self_out)
    grad_self_mixed = project_back(grad_self_out, attn_out[1]).astype(jnp.bfloat16)
    grad_self_query, grad_self_key, grad_self_value = attend_backward(
        self_query, self_key, self_value, own_keys, self_total, grad_self_mixed
    )
    grad_one = (
        grad_resid_two
        + project_back(grad_self_query, attn_in[3])
        + project_back(grad_self_key, attn_in[4])
        + project_back(grad_self_value, attn_in[5])
    )
    _, norm_one_pull = jax.vjp(layer_norm, resid_one, gains[0], biases[0])
    grad_resid_one, gain_one, bias_one = norm_one_pull(grad_one)
    grad_cross_out = grad_resid_one.astype(jnp.bfloat16)
    (cross_query, cross_key, cross_value), cross_mixed, cross_total = cross_forward(
        own_rows, other_rows, other_keys, attn_in
    )
    cross_out_grad = weight_grad(cross_mixed, grad_cross_out)
    grad_cross_mixed = project_back(grad_cross_out, attn_out[0]).astype(jnp.bfloat16)
    grad_cross_query, grad_cross_key, grad_cross_value = attend_backward(
        cross_query, cross_key, cross_value, other_keys, cross_total, grad_cross_mixed
    )
    grad_own = grad_resid_one + project_back(grad_cross_query, attn_in[0])
    grad_other = project_back(grad_cross_key, attn_in[1]) + project_back(
        grad_cross_value, attn_in[2]
    )
    in_grads = jnp.stack(
        [
            weight_grad(own_rows, grad_cross_query),
            weight_grad(other_rows, grad_cross_key),
            weight_grad(other_rows, grad_cross_value),
            weight_grad(hidden_low, grad_self_query),
            weight_grad(hidden_low, grad_self_key),
            weight_grad(hidden_low, grad_self_value),
        ]
    )
    out_grads = jnp.stack([cross_out_grad, self_out_grad])
    gain_grads = jnp.stack([gain_one, gain_two, gain_three])
    bias_grads = jnp.stack([bias_one, bias_two, bias_three])
    return (
        grad_own,
        grad_other,
        (in_grads, out_grads, up_grad, down_grad, gain_grads, bias_grads, grad_gate),
    )


def stream_params(gathered, stream):
    return (
        gathered[0][stream],
        gathered[1][stream],
        gathered[2][stream],
        gathered[3][stream],
        gathered[4][stream].astype(jnp.float32),
        gathered[5][stream].astype(jnp.float32),
        gathered[6][stream].astype(jnp.float32),
    )


def plain_path(
    text_a,
    visual_a,
    text_b,
    visual_b,
    text_len_a,
    visual_len_a,
    text_len_b,
    visual_len_b,
    cot_text_a,
    cot_visual_a,
    cot_text_b,
    cot_visual_b,
    attn_in,
    attn_out,
    ffn_up,
    ffn_down,
    norm_gain,
    norm_bias,
    gate_vector,
):
    gathered = (
        lax.all_gather(attn_in, "fsdp", axis=2, tiled=True),
        lax.all_gather(attn_out, "fsdp", axis=2, tiled=True),
        lax.all_gather(ffn_up, "fsdp", axis=1, tiled=True),
        lax.all_gather(ffn_down, "fsdp", axis=1, tiled=True),
        lax.all_gather(norm_gain, "fsdp", axis=2, tiled=True),
        lax.all_gather(norm_bias, "fsdp", axis=2, tiled=True),
        lax.all_gather(gate_vector, "fsdp", axis=1, tiled=True),
    )
    layouts = []
    for rows_text, rows_visual, len_text, len_visual, cot_text, cot_visual in (
        (text_a, visual_a, text_len_a, visual_len_a, cot_text_a, cot_visual_a),
        (text_b, visual_b, text_len_b, visual_len_b, cot_text_b, cot_visual_b),
    ):
        keys_text = jnp.arange(rows_text.shape[1], dtype=jnp.int32)[None, :] < len_text[:, None]
        keys_visual = (
            jnp.arange(rows_visual.shape[1], dtype=jnp.int32)[None, :] < len_visual[:, None]
        )
        stream_rows = (rows_text, rows_visual)
        stream_keys = (keys_text, keys_visual)
        stream_masks = (keys_text.astype(jnp.float32), keys_visual.astype(jnp.float32))
        outputs = []
        saved_list = []
        for stream in (0, 1):
            other_side = 1 - stream
            output, saved_rows = stream_forward(
                stream_rows[stream],
                stream_rows[other_side],
                stream_keys[stream],
                stream_keys[other_side],
                stream_masks[stream],
                stream_params(gathered, stream),
            )
            outputs.append(output.astype(jnp.bfloat16))
            saved_list.append(saved_rows)
        layouts.append(
            (stream_rows, stream_keys, stream_masks, (cot_text, cot_visual), outputs, saved_list)
        )
    back_weights = gathered
    input_grads = [[None, None], [None, None]]
    stream_grads = []
    for stream in (0, 1):
        other_side = 1 - stream
        params = stream_params(back_weights, stream)
        summed = None
        for layout_index in (0, 1):
            stream_rows, stream_keys, stream_masks, cotangents, outputs, saved_list = layouts[
                layout_index
            ]
            grad_own, grad_other, grads_here = stream_backward(
                stream_rows[stream],
                stream_rows[other_side],
                stream_keys[stream],
                stream_keys[other_side],
                stream_masks[stream],
                params,
                saved_list[stream],
                cotangents[stream].astype(jnp.float32),
            )
            for target, piece in ((stream, grad_own), (other_side, grad_other)):
                if input_grads[layout_index][target] is None:
                    input_grads[layout_index][target] = piece
                else:
                    input_grads[layout_index][target] = input_grads[layout_index][target] + piece
            if summed is None:
                summed = grads_here
            else:
                summed = tuple((left + right for left, right in zip(summed, grads_here)))
        stream_grads.append(summed)
    text_grads = stream_grads[0]
    visual_grads = stream_grads[1]
    row_dims = (1, 1, 0, 0, 1, 1, 0)
    packed = tuple(
        (
            jnp.concatenate([text_grads[index], visual_grads[index]], axis=row_dims[index])
            for index in range(7)
        )
    )
    shares = (
        lax.psum_scatter(packed[0], ("dp", "fsdp"), scatter_dimension=1, tiled=True),
        lax.psum_scatter(packed[1], ("dp", "fsdp"), scatter_dimension=1, tiled=True),
        lax.psum_scatter(packed[2], ("dp", "fsdp"), scatter_dimension=0, tiled=True),
        lax.psum_scatter(packed[3], ("dp", "fsdp"), scatter_dimension=0, tiled=True),
        lax.psum_scatter(packed[4], ("dp", "fsdp"), scatter_dimension=1, tiled=True),
        lax.psum_scatter(packed[5], ("dp", "fsdp"), scatter_dimension=1, tiled=True),
        lax.psum_scatter(packed[6], ("dp", "fsdp"), scatter_dimension=0, tiled=True),
    )
    joined = (
        lax.all_gather(shares[0].astype(jnp.bfloat16), "dp", axis=1, tiled=True).astype(
            jnp.float32
        ),
        lax.all_gather(shares[1].astype(jnp.bfloat16), "dp", axis=1, tiled=True).astype(
            jnp.float32
        ),
        lax.all_gather(shares[2].astype(jnp.bfloat16), "dp", axis=0, tiled=True).astype(
            jnp.float32
        ),
        lax.all_gather(shares[3].astype(jnp.bfloat16), "dp", axis=0, tiled=True).astype(
            jnp.float32
        ),
        lax.all_gather(shares[4].astype(jnp.bfloat16), "dp", axis=1, tiled=True).astype(
            jnp.float32
        ),
        lax.all_gather(shares[5].astype(jnp.bfloat16), "dp", axis=1, tiled=True).astype(
            jnp.float32
        ),
        lax.all_gather(shares[6].astype(jnp.bfloat16), "dp", axis=0, tiled=True).astype(
            jnp.float32
        ),
    )
    finals = tuple(
        (jnp.stack(jnp.split(joined[index], 2, axis=row_dims[index])) for index in range(7))
    )
    first_outputs = layouts[0][4]
    second_outputs = layouts[1][4]
    return (
        first_outputs[0],
        first_outputs[1],
        second_outputs[0],
        second_outputs[1],
        input_grads[0][0].astype(jnp.bfloat16),
        input_grads[0][1].astype(jnp.bfloat16),
        input_grads[1][0].astype(jnp.bfloat16),
        input_grads[1][1].astype(jnp.bfloat16),
        finals[0],
        finals[1],
        finals[2],
        finals[3],
        finals[4],
        finals[5],
        finals[6],
    )


class Geometry:
    def __init__(self, mesh, shapes):
        self.dp = mesh.shape["dp"]
        self.fsdp = mesh.shape["fsdp"]
        (self.la, self.lva), (self.lb, self.lvb) = (
            (shapes[0][1], shapes[1][1]),
            (shapes[2][1], shapes[3][1]),
        )
        self.d = shapes[0][2]
        self.rows = self.d // self.fsdp
        self.ff = shapes[14][2]
        self.pages = shapes[0][0]
        self.t0 = -(-(self.la + self.lb) // 16) * 16
        self.t1 = -(-(self.lva + self.lvb) // 16) * 16
        self.t = self.t0 + self.t1
        self.nz = self.fsdp // 4

    def fits(self):
        return (
            self.dp == 2
            and self.fsdp == 16
            and self.pages == 1
            and self.d == 16 * 48
            and self.ff == 4 * self.d
            and self.t0 >= self.t1
            and self.d == 64 * HEADS
        )


def layer_kernel(g, *refs):
    D, FF, R, T0, T1, T, NZ = g.d, g.ff, g.rows, g.t0, g.t1, g.t, g.nz
    ZR = D // NZ
    it = iter(refs)
    take = lambda n: [next(it) for _ in range(n)]
    lens = take(4)
    rows_in = take(4)
    cots_in = take(4)
    w_parts = take(4)
    (vec_in,) = take(1)
    outs = take(4)
    grads = take(4)
    ga, gu, gd, vec_out = take(4)
    ra, rg, rfa, rfg = take(4)
    W, VEC, vecs = take(3)
    S, A, DU, CQ, SQ, DO = take(6)
    RES, HID, DR, XH, RSTD, GP = take(6)
    p_refs = take(4)
    RZ, FB, VG, VR, VZ = take(5)
    (s_loc, s_vec, r_vec, sz, rz, sy, ry, sx, rx, sc, rc) = take(11)
    (s_ex, r_ex, s_own, s_st, s_zr, r_zr, s_rd, r_rd, s_vg, r_vg, s_vz, r_vz) = take(12)

    X, H1, OC, OS, H2 = 0, 1, 2, 3, 4
    DQC, DKC, DVC, DQS, DKS, DVS, DC, DS, DF = range(5, 14)
    span = (slice(0, T0), slice(T0, T))
    size = (T0, T1)

    x = lax.axis_index("dp")
    f = lax.axis_index("fsdp")
    z, y, c = f // 4, (f // 2) % 2, f % 2
    me = x * 4 + y * 2 + c

    def device(xx, zz, yy, cc):
        return (xx, zz * 4 + yy * 2 + cc)

    def role_device(r):
        return device(r // 4, z, (r // 2) % 2, r % 2)

    def remote(src, dst, send, recv, dev):
        return pltpu.make_async_remote_copy(
            src_ref=src, dst_ref=dst, send_sem=send, recv_sem=recv, device_id=dev,
            device_id_type=MESH_ID,
        )

    barrier = pltpu.get_barrier_semaphore()
    for step in range(1, g.fsdp):
        pl.semaphore_signal(
            barrier, inc=1, device_id=(x, (f + step) % g.fsdp), device_id_type=MESH_ID
        )
    for r in range(4):
        pl.semaphore_signal(
            barrier, inc=1, device_id=device(1 - x, z, r // 2, r % 2), device_id_type=MESH_ID
        )
    pl.semaphore_wait(barrier, g.fsdp + 3)

    def wref(k, ff, r0, n):
        down = k // 12
        unit = k + down * (12 + (4 * R * ff) // D - k)
        row = R * ff + down * ((4 * R * ff) % D + R * (k - 12) - R * ff) + r0
        return W.at[:, unit, pl.ds(pl.multiple_of(row, 16), n)]

    def local_part(k):
        w_in, w_out, w_up, w_dn = w_parts
        if k in (3, 7):
            return w_out.at[:, (k - 3) // 4]
        if k < 8:
            return w_in.at[:, (0, 1, 2, None, 3, 4, 5)[k]]
        if k < 12:
            return w_up.at[:, :, pl.ds(D * (k - 8), D)]
        return w_dn.at[:, pl.ds(R * (k - 12), R)]

    third = R // 3
    local = []
    for k in range(16):
        cp = pltpu.make_async_copy(local_part(k), wref(k, f, 0, R), s_loc.at[k])
        cp.start()
        local.append(cp)

    def vec_copy(step):
        return remote(
            vec_in, VEC.at[f], s_vec.at[step - 1], r_vec.at[step - 1],
            (x, (f + step) % g.fsdp),
        )

    def vec_wait(step):
        ref = VEC.at[(f + g.fsdp - step) % g.fsdp]
        remote(ref, ref, s_vec.at[step - 1], r_vec.at[step - 1], (x, f)).wait_recv()

    for step in range(1, g.fsdp):
        vec_copy(step).start()
    own_vec = pltpu.make_async_copy(vec_in, VEC.at[f], s_loc.at[16])
    own_vec.start()

    def shard(zz, yy):
        return zz * 4 + yy * 2 + c

    def z_copy(k, d):
        ref = wref(k, f, third * x, 2 * third)
        return remote(ref, ref, sz.at[k, d - 1], rz.at[k, d - 1], device(x, (z + d) % NZ, y, c))

    def z_wait(k, d):
        ref = wref(k, shard((z + NZ - d) % NZ, y), third * x, 2 * third)
        remote(ref, ref, sz.at[k, d - 1], rz.at[k, d - 1], device(x, (z + d) % NZ, y, c)).wait_recv()

    def y_copy(k, d):
        ref = wref(k, shard((z + NZ - d) % NZ, y), third * x, 2 * third)
        return remote(ref, ref, sy.at[k, d], ry.at[k, d], device(x, z, 1 - y, c))

    def y_wait(k, d):
        ref = wref(k, shard((z + NZ - d) % NZ, 1 - y), third * x, 2 * third)
        remote(ref, ref, sy.at[k, d], ry.at[k, d], device(x, z, 1 - y, c)).wait_recv()

    def x_copy(k, d, e):
        ref = wref(k, shard((z + NZ - d) % NZ, (y + e) % 2), 2 * third * x, third)
        return remote(ref, ref, sx.at[k, 2 * d + e], rx.at[k, 2 * d + e], device(1 - x, z, y, c))

    def x_wait(k, d, e):
        ref = wref(k, shard((z + NZ - d) % NZ, (y + e) % 2), 2 * third * (1 - x), third)
        remote(ref, ref, sx.at[k, 2 * d + e], rx.at[k, 2 * d + e], device(1 - x, z, y, c)).wait_recv()

    def c_copy(k, d, e):
        ref = wref(k, shard((z + NZ - d) % NZ, (y + e) % 2), 0, R)
        return remote(ref, ref, sc.at[k, 2 * d + e], rc.at[k, 2 * d + e], device(x, z, y, 1 - c))

    def c_wait(k, d, e):
        other = ((z + NZ - d) % NZ) * 4 + ((y + e) % 2) * 2 + 1 - c
        ref = wref(k, other, 0, R)
        remote(ref, ref, sc.at[k, 2 * d + e], rc.at[k, 2 * d + e], device(x, z, y, 1 - c)).wait_recv()

    for k in range(16):
        local[k].wait()
        for d in range(1, NZ):
            z_copy(k, d).start()
        y_copy(k, 0).start()
        c_copy(k, 0, 0).start()

    def gather_step(t):
        @pl.when(t < 16)
        def _():
            for d in range(1, NZ):
                z_wait(t, d)
                y_copy(t, d).start()
                x_copy(t, d, 0).start()

        @pl.when((t >= 1) & (t < 17))
        def _():
            for d in range(NZ):
                y_wait(t - 1, d)
                x_copy(t - 1, d, 1).start()

        @pl.when((t >= 2) & (t < 18))
        def _():
            for e in range(2):
                for d in range(NZ):
                    if d or e:
                        x_wait(t - 2, d, e)
                        c_copy(t - 2, d, e).start()

        @pl.when(t >= 3)
        def _():
            for e in range(2):
                for d in range(NZ):
                    c_wait(t - 3, d, e)

    def gather_steps(lo, hi):
        def step(t, carry):
            gather_step(t)
            return carry

        lax.fori_loop(lo, hi, step, 0)

    la, lva = g.la, g.lva

    def assemble(dst, parts):
        ta, va, tb, vb = parts
        dst[0:la] = ta[0].astype(F32)
        dst[la : la + g.lb] = tb[0].astype(F32)
        if T0 > la + g.lb:
            dst[la + g.lb : T0] = jnp.zeros((T0 - la - g.lb, D), F32)
        dst[T0 : T0 + lva] = va[0].astype(F32)
        dst[T0 + lva : T0 + lva + g.lvb] = vb[0].astype(F32)
        if T1 > lva + g.lvb:
            dst[T0 + lva + g.lvb : T] = jnp.zeros((T1 - lva - g.lvb, D), F32)

    assemble(HID, rows_in)
    S[X] = HID[...].astype(BF)
    assemble(DR, cots_in)

    def live(index, s):
        first, second = (la, g.lb) if s == 0 else (lva, g.lvb)
        na, nb = lens[s][0], lens[2 + s][0]
        return ((index < first) & (index < na)) | (
            (index >= first) & (index - first < nb) & (index - first < second)
        )

    def key_mask(qs, ks):
        shape = (size[qs], size[ks])
        qi = lax.broadcasted_iota(jnp.int32, shape, 0)
        ki = lax.broadcasted_iota(jnp.int32, shape, 1)
        q_first = la if qs == 0 else lva
        k_first = la if ks == 0 else lva
        same = ((qi < q_first) & (ki < k_first)) | ((qi >= q_first) & (ki >= k_first))
        return same & live(ki, ks)

    UA = (0, 1, 2, 4, 5, 6)
    UB = (3, 7)

    def wtile(s, u, i):
        return W[s, u, :, cols(i, 256)]

    def wrows(s, u, i):
        return W[s, u, cols(i, 256), :]

    NT = D // 256

    def cross_project():
        for s in (0, 1):
            own, other = span[s], span[1 - s]

            def q_tile(i):
                CQ[0, own, cols(i, 256)] = dot(S[X, own], wtile(s, UA[0], i)).astype(BF)

            loop(NT, q_tile)

            def kv_tile(i):
                m = 1 + i // NT
                j = i % NT
                CQ[m, other, cols(j, 256)] = dot(S[X, other], wtile(s, m, j)).astype(BF)

            loop(2 * NT, kv_tile)

    def self_project():
        for s in (0, 1):
            own = span[s]

            def tile(i):
                m = i // NT
                j = i % NT
                SQ[m, own, cols(j, 256)] = dot(S[H1, own], wtile(s, 4 + m, j)).astype(BF)

            loop(3 * NT, tile)

    def attend(src, s, ks, p_ref, o_index):
        own, keys = span[s], span[ks]

        def pair(p):
            lanes = cols(p, 128)
            mask = key_mask(s, ks)
            q, k, v = src[0, own, lanes], src[1, keys, lanes], src[2, keys, lanes]
            low = lax.broadcasted_iota(jnp.int32, q.shape, 1) < 64
            high = lax.broadcasted_iota(jnp.int32, q.shape, 1) >= 64
            mixed = []
            for half in range(2):
                qh = jnp.where(low if half == 0 else high, q, jnp.zeros_like(q))
                scores = jnp.where(mask, dot_rt(qh, k) * 0.125, NEG)
                top = jnp.max(scores, axis=-1, keepdims=True)
                expon = jnp.exp(scores - top)
                probs = expon / jnp.sum(expon, axis=-1, keepdims=True)
                p_ref[2 * p + half] = probs
                mixed.append(dot(probs.astype(BF), v))
            S[o_index, own, lanes] = jnp.where(low, mixed[0], mixed[1]).astype(BF)

        loop(HEADS // 2, pair)

    def attend_back(src, s, ks, p_ref, gq, gk, gv):
        own, keys = span[s], span[ks]

        def pair(p):
            lanes = cols(p, 128)
            q, k, v = src[0, own, lanes], src[1, keys, lanes], src[2, keys, lanes]
            do = DO[own, lanes]
            low_q = lax.broadcasted_iota(jnp.int32, q.shape, 1) < 64
            high_q = lax.broadcasted_iota(jnp.int32, q.shape, 1) >= 64
            low_k = lax.broadcasted_iota(jnp.int32, k.shape, 1) < 64
            dq, dk, dv = [], [], []
            for half in range(2):
                doh = jnp.where(low_q if half == 0 else high_q, do, jnp.zeros_like(do))
                probs = p_ref[2 * p + half]
                dp = dot_rt(doh, v)
                ds = (probs * (dp - jnp.sum(dp * probs, axis=-1, keepdims=True))).astype(BF)
                dq.append(dot(ds, k))
                dk.append(dot_lt(ds, q))
                dv.append(dot_lt(probs.astype(BF), do))
            S[gq, own, lanes] = (jnp.where(low_q, dq[0], dq[1]) * 0.125).astype(BF)
            S[gk, keys, lanes] = (jnp.where(low_k, dk[0], dk[1]) * 0.125).astype(BF)
            S[gv, keys, lanes] = jnp.where(low_k, dv[0], dv[1]).astype(BF)

        loop(HEADS // 2, pair)

    def out_project(o_index, which):
        for s in (0, 1):
            own = span[s]

            def tile(i):
                RES[own, cols(i, 256)] = HID[own, cols(i, 256)] + dot(
                    S[o_index, own], wtile(s, UB[which], i)
                )

            loop(NT, tile)

    RB = 16
    NB0 = T0 // RB
    mean = lambda v: jnp.sum(v, axis=-1, keepdims=True) * (1.0 / D)

    def normalize(i, r):
        resid = RES[r]
        centre = resid - mean(resid)
        rstd = lax.rsqrt(mean(centre * centre) + 1e-05)
        return centre * rstd, rstd

    def row_of(i, s):
        return vecs[pl.ds(s * 3 + i, 1), :]

    def norm_forward(i, h_index):
        def block(b):
            s = b // NB0
            r = cols(b, RB)
            xh, rstd = normalize(i, r)
            XH[i, r] = xh
            RSTD[i, r] = rstd
            hidden = xh * vecs[pl.ds(s * 3 + i, 1), :] + vecs[pl.ds(6 + s * 3 + i, 1), :]
            HID[r] = hidden
            S[h_index, r] = hidden.astype(BF)

        loop(T // RB, block)

    def add_row(row, value):
        VG[pl.ds(row, 1), :] += jnp.sum(value, axis=0, keepdims=True)

    def norm_pull(i, s, r, dh, xh, rstd):
        add_row(s * 3 + i, dh * xh)
        add_row(6 + s * 3 + i, dh)
        dx = dh * vecs[pl.ds(s * 3 + i, 1), :]
        return rstd * (dx - mean(dx) - xh * mean(dx * xh))

    def norm_backward(i, g_index):
        def block(b):
            s = b // NB0
            r = cols(b, RB)
            dr = norm_pull(i, s, r, DR[r], XH[i, r], RSTD[i, r])
            DR[r] = dr
            S[g_index, r] = dr.astype(BF)

        loop(T // RB, block)

    def tail():
        def block(b):
            s = b // NB0
            r = cols(b, RB)
            xh, rstd = normalize(2, r)
            gain = vecs[pl.ds(s * 3 + 2, 1), :]
            h3 = xh * gain + vecs[pl.ds(6 + s * 3 + 2, 1), :]
            gate = vecs[pl.ds(12 + s, 1), :]
            logit = jnp.sum(h3 * gate, axis=-1, keepdims=True)
            sig = 1.0 / (1.0 + jnp.exp(-logit))
            index = lax.broadcasted_iota(jnp.int32, (RB, 1), 0) + b * RB
            text = index < T0
            mask = (text & live(index, 0)) | ((index >= T0) & live(index - T0, 1))
            mask = jnp.where(mask, 1.0, 0.0)
            weight = sig * mask
            HID[r] = h3 * weight
            dout = DR[r]
            dlogit = jnp.sum(dout * h3, axis=-1, keepdims=True) * weight * (1.0 - sig)
            add_row(12 + s, h3 * dlogit)
            dr = norm_pull(2, s, r, dout * weight + dlogit * gate, xh, rstd)
            DR[r] = dr
            S[DF, r] = dr.astype(BF)

        loop(T // RB, block)
        o_ta, o_va, o_tb, o_vb = outs
        o_ta[0] = HID[0:la].astype(BF)
        o_tb[0] = HID[la : la + g.lb].astype(BF)
        o_va[0] = HID[T0 : T0 + lva].astype(BF)
        o_vb[0] = HID[T0 + lva : T0 + lva + g.lvb].astype(BF)

    def ffn_up(q):
        for s in (0, 1):
            own = span[s]

            def tile(i):
                j = q * NT + i
                u = dot(S[H2, own], wtile(s, 8 + q, i))
                cdf = 0.5 + 0.5 * erf_of(u * 0.7071067811865476)
                A[own, cols(j, 256)] = (u * cdf).astype(BF)
                GP[own, cols(j, 256)] = cdf + u * (
                    jnp.exp(u * u * -0.5) * 0.3989422804014327
                )

            loop(NT, tile)

    def ffn_down():
        for s in (0, 1):
            own = span[s]

            def tile(i):
                total = HID[own, cols(i, 256)]
                for q in range(4):
                    total = total + dot(A[own, D * q : D * q + D], wtile(s, 12 + q, i))
                RES[own, cols(i, 256)] = total

            loop(NT, tile)

    def ffn_down_back():
        for s in (0, 1):
            own = span[s]

            def tile(j):
                da = dot_rt(S[DF, own], wrows(s, 12 + j // NT, j % NT))
                DU[own, cols(j, 256)] = (GP[own, cols(j, 256)] * da).astype(BF)

            loop(4 * NT, tile)

    def ffn_up_back():
        for s in (0, 1):
            own = span[s]

            def tile(i):
                total = DR[own, cols(i, 256)]
                for q in range(4):
                    total = total + dot_rt(DU[own, D * q : D * q + D], wrows(s, 8 + q, i))
                DR[own, cols(i, 256)] = total

            loop(NT, tile)

    def out_back(g_index, which):
        for s in (0, 1):
            own = span[s]

            def tile(i):
                DO[own, cols(i, 256)] = dot_rt(
                    S[g_index, own], wrows(s, UB[which], i)
                ).astype(BF)

            loop(NT, tile)

    def self_back():
        for s in (0, 1):
            own = span[s]

            def tile(i):
                total = DR[own, cols(i, 256)]
                for m, gi in enumerate((DQS, DKS, DVS)):
                    total = total + dot_rt(S[gi, own], wrows(s, 4 + m, i))
                DR[own, cols(i, 256)] = total

            loop(NT, tile)

    def cross_back():
        for s in (0, 1):
            own = span[s]

            def tile(i):
                total = DR[own, cols(i, 256)] + dot_rt(S[DQC, own], wrows(s, 0, i))
                total = total + dot_rt(S[DKC, own], wrows(1 - s, 1, i))
                total = total + dot_rt(S[DVC, own], wrows(1 - s, 2, i))
                DR[own, cols(i, 256)] = total

            loop(NT, tile)
        g_ta, g_va, g_tb, g_vb = grads
        g_ta[0] = DR[0:la].astype(BF)
        g_tb[0] = DR[la : la + g.lb].astype(BF)
        g_va[0] = DR[T0 : T0 + lva].astype(BF)
        g_vb[0] = DR[T0 + lva : T0 + lva + g.lvb].astype(BF)

    sends = []

    def plane_send(r, src, dst, slot):
        @pl.when(me != r)
        def _():
            remote(src, dst, s_ex.at[slot, r], r_ex.at[slot, me], role_device(r)).start()

        @pl.when(me == r)
        def _():
            pltpu.make_async_copy(src, dst, s_own.at[slot]).start()

        sends.append((r, src, dst, slot))

    def finish_sends():
        for r, src, dst, slot in sends:

            @pl.when(me != r)
            def _():
                remote(src, dst, s_ex.at[slot, r], r_ex.at[slot, me], role_device(r)).wait_send()

    def plane_wait(slot, pick):
        for p in range(8):
            ref = pick(p)

            @pl.when(me != p)
            def _():
                remote(ref, ref, s_ex.at[slot, p], r_ex.at[slot, p], role_device(p)).wait_recv()

            @pl.when(me == p)
            def _():
                pltpu.make_async_copy(ref, ref, s_own.at[slot]).wait()

    A_OF = (X, X, X, H1, H1, H1, OC, OS)
    G_OF = (DQC, DKC, DVC, DQS, DKS, DVS, DC, DS)
    HB = D // 2

    def send_left(r):
        plane_send(r, S.at[A_OF[r]], ra.at[me], 0)

    def send_right(r):
        plane_send(r, S.at[G_OF[r]], rg.at[me], 1)

    def send_ffn_left(r):
        if r < 4:
            plane_send(r, S.at[H2], rfa.at[me, :, pl.ds(0, D)], 3)
        else:
            yy = (r - 4) // 2
            for q in range(4):
                plane_send(
                    r, A.at[:, pl.ds(D * q + HB * yy, HB)], rfa.at[me, :, pl.ds(HB * q, HB)],
                    3 + q,
                )

    def send_ffn_right(r):
        if r < 4:
            plane_send(r, DU.at[:, pl.ds(D * r, D)], rfg.at[me], 2)
        else:
            hh = (r - 4) % 2
            plane_send(r, S.at[DF, :, pl.ds(HB * hh, HB)], rfg.at[me, :, pl.ds(0, HB)], 2)

    st = [0]

    def stage(src, dst_unit, col, width, dcol):
        copies = []
        for half in range(2):
            for p in range(4):
                cp = pltpu.make_async_copy(
                    src.at[4 * half + p, :, pl.ds(col, width)],
                    W.at[half, dst_unit, pl.ds(T * p, T), pl.ds(dcol, width)],
                    s_st.at[st[0]],
                )
                st[0] += 1
                cp.start()
                copies.append(cp)
        return copies

    def stacked(unit, rs, lanes):
        first, count = (0, T0) if rs == 0 else (T0, T1)
        return jnp.concatenate(
            [
                W[half, unit, T * p + first : T * p + first + count, lanes]
                for half in range(2)
                for p in range(4)
            ],
            axis=0,
        )

    def weight_grad(left, right, dst):
        for rs in range(2):

            def tile(i):
                W[rs, dst, cols(i, 256), :] = dot_lt(
                    stacked(left, rs, cols(i, 256)), stacked(right, rs, slice(0, D))
                ).astype(BF)

            loop(NT, tile)

    def weight_grad_down(right, dst):
        for rs in range(2):

            def tile(q):
                left_unit = 10 + q // 2
                out = dot_lt(
                    stacked(left_unit, rs, cols(q % 2, HB)), stacked(right, rs, slice(0, HB))
                ).astype(BF)
                W[rs, dst, pl.ds(pl.multiple_of(q * ZR, ZR), ZR), 0:HB] = out[0:ZR]
                W[rs, dst, pl.ds(pl.multiple_of(q * ZR, ZR), ZR), HB:D] = out[ZR : 2 * ZR]

            loop(4, tile)

    def z_send(n, unit, d):
        zz = (z + d) % NZ
        src = W.at[:, unit, pl.ds(pl.multiple_of(zz * ZR, ZR), ZR)]
        return remote(src, RZ.at[n, d - 1], s_zr.at[n, d - 1], r_zr.at[n, d - 1], device(x, zz, y, c))

    def z_collect(n, unit):
        for d in range(1, NZ):
            z_send(n, unit, d).wait_recv()
        for rs in range(2):

            def block(i):
                total = W[rs, unit, pl.ds(pl.multiple_of(z * ZR + i * 16, 16), 16)].astype(F32)
                for d in range(NZ - 1):
                    total = total + RZ[n, d, rs, cols(i, 16)].astype(F32)
                FB[n, rs, cols(i, 16)] = total.astype(BF)

            loop(ZR // 16, block)

    flip = (((me + 1) // 2) % 2) * (1 - (me // 3 + 1) // 2)

    def attn_blocks(r):
        yy, cc = (r // 2) % 2, r % 2
        for rs in range(2):
            src = FB.at[0, rs, pl.ds(R * (2 * yy + cc), R)]
            s = rs + flip - 2 * rs * flip
            yield rs, src, ga.at[s, me]

    def up_blocks(r):
        yy, cc = (r // 2) % 2, r % 2
        for rs in range(2):
            src = FB.at[1, rs, pl.ds(R * (2 * yy + cc), R)]
            yield 2 + rs, src, gu.at[rs, :, pl.ds(pl.multiple_of(D * (me % 4), 128), D)]

    def down_blocks(r):
        cc = r % 2
        for rs in range(2):
            src = FB.at[1, rs, :, pl.ds(HB * cc, HB)]
            yield 2 + rs, src, gd.at[rs, :, pl.ds(pl.multiple_of(HB * (me % 2), 128), HB)]

    def spread(r, blocks, cond, act):
        for n, src, dst in blocks(r):

            @pl.when(cond & (me != r))
            def _():
                cp = remote(src, dst, s_rd.at[n, r], r_rd.at[n, me], role_device(r))
                cp.start() if act == "start" else cp.wait_send()

            @pl.when(cond & (me == r))
            def _():
                cp = pltpu.make_async_copy(src, dst, s_own.at[8 + n])
                cp.start() if act == "start" else cp.wait()

    def spread_all(n, act):
        for r in range(8):
            if n == 0:
                spread(r, attn_blocks, me >= 0, act)
            else:
                spread(r, up_blocks, me < 4, act)
                spread(r, down_blocks, (me // 2 == 2 + (r // 2) % 2), act)

    def spread_wait():
        for p in range(8):

            @pl.when(me != p)
            def _():
                for rs in range(2):
                    ref = ga.at[rs, p]
                    remote(ref, ref, s_rd.at[rs, p], r_rd.at[rs, p], role_device(p)).wait_recv()
                    if p < 4:
                        ref = gu.at[rs, :, pl.ds(D * p, D)]
                        remote(
                            ref, ref, s_rd.at[2 + rs, p], r_rd.at[2 + rs, p], role_device(p)
                        ).wait_recv()

            if p >= 4:

                @pl.when((me != p) & (y == (p - 4) // 2))
                def _():
                    for rs in range(2):
                        ref = gd.at[rs, :, pl.ds(HB * (p % 2), HB)]
                        remote(
                            ref, ref, s_rd.at[2 + rs, p], r_rd.at[2 + rs, p], role_device(p)
                        ).wait_recv()

    VG[...] = jnp.zeros_like(VG)
    for step in range(1, g.fsdp):
        vec_wait(step)
    own_vec.wait()
    total = jnp.zeros((16, D), F32)
    lane = lax.broadcasted_iota(jnp.int32, (128, D), 0)
    col = lax.broadcasted_iota(jnp.int32, (128, D), 1)
    for ff in range(g.fsdp):
        pick = ((col == lane + R * ff) & (lane < R)).astype(F32).astype(BF)
        total = total + dot(VEC[ff], pick)
    vecs[...] = total

    gather_steps(0, 7)
    cross_project()
    gather_steps(7, 8)
    attend(CQ, 0, 1, p_refs[0], OC)
    attend(CQ, 1, 0, p_refs[1], OC)
    gather_steps(8, 9)
    out_project(OC, 0)
    norm_forward(0, H1)
    gather_steps(9, 11)
    self_project()
    gather_steps(11, 12)
    attend(SQ, 0, 0, p_refs[2], OS)
    attend(SQ, 1, 1, p_refs[3], OS)
    gather_steps(12, 13)
    out_project(OS, 1)
    norm_forward(1, H2)
    gather_steps(13, 15)
    for q in range(4):
        gather_steps(15 + q, 16 + q)
        ffn_up(q)

    def gather_sent(k):
        for d in range(1, NZ):
            z_copy(k, d).wait_send()
        for d in range(NZ):
            y_copy(k, d).wait_send()
            for e in range(2):
                c_copy(k, d, e).wait_send()
                if d or e:
                    x_copy(k, d, e).wait_send()

    loop(16, gather_sent)
    for r in range(8):
        send_ffn_left(r)
    for r in range(8):
        send_left(r)
    ffn_down()
    tail()
    for r in range(4, 8):
        send_ffn_right(r)
    ffn_down_back()
    for r in range(4):
        send_ffn_right(r)
    ffn_up_back()
    norm_backward(1, DS)
    send_right(7)
    out_back(DS, 1)
    attend_back(SQ, 0, 0, p_refs[2], DQS, DKS, DVS)
    attend_back(SQ, 1, 1, p_refs[3], DQS, DKS, DVS)
    for r in (3, 4, 5):
        send_right(r)
    self_back()
    norm_backward(0, DC)
    send_right(6)
    out_back(DC, 0)
    attend_back(CQ, 0, 1, p_refs[0], DQC, DKC, DVC)
    attend_back(CQ, 1, 0, p_refs[1], DQC, DKC, DVC)
    for r in (0, 1, 2):
        send_right(r)

    def vg_copy(r):
        return remote(VG, VR.at[me], s_vg.at[r], r_vg.at[me], role_device(r))

    for r in range(8):

        @pl.when(me != r)
        def _():
            vg_copy(r).start()

    VR[me] = VG[...]
    cross_back()

    @pl.when(me < 4)
    def _():
        plane_wait(2, lambda p: rfg.at[p])
        plane_wait(3, lambda p: rfa.at[p, :, pl.ds(0, D)])

    @pl.when(me >= 4)
    def _():
        plane_wait(2, lambda p: rfg.at[p, :, pl.ds(0, HB)])
        for q in range(4):
            plane_wait(3 + q, lambda p: rfa.at[p, :, pl.ds(HB * q, HB)])

    copies = stage(rfg, 12, 0, D, 0) + stage(rfa, 10, 0, D, 0) + stage(rfa, 11, D, D, 0)
    for cp in copies:
        cp.wait()

    @pl.when(me < 4)
    def _():
        weight_grad(10, 12, 15)

    @pl.when(me >= 4)
    def _():
        weight_grad_down(12, 15)

    for d in range(1, NZ):
        z_send(1, 15, d).start()

    plane_wait(0, lambda p: ra.at[p])
    plane_wait(1, lambda p: rg.at[p])
    copies = stage(ra, 8, 0, D, 0) + stage(rg, 9, 0, D, 0)
    for cp in copies:
        cp.wait()
    weight_grad(8, 9, 14)
    for d in range(1, NZ):
        z_send(0, 14, d).start()

    for p in range(8):

        @pl.when(me != p)
        def _():
            ref = VR.at[p]
            remote(ref, ref, s_vg.at[p], r_vg.at[p], role_device(p)).wait_recv()

    total = VR[0]
    for p in range(1, 8):
        total = total + VR[p]
    VZ[z] = total

    def vz_copy(d):
        return remote(
            VZ.at[z], VZ.at[z], s_vz.at[d - 1], r_vz.at[d - 1], device(x, (z + d) % NZ, y, c)
        )

    for d in range(1, NZ):
        vz_copy(d).start()
    z_collect(1, 15)
    spread_all(1, "start")
    for d in range(1, NZ):
        ref = VZ.at[(z + NZ - d) % NZ]
        remote(ref, ref, s_vz.at[d - 1], r_vz.at[d - 1], device(x, z, y, c)).wait_recv()
    total = VZ[0]
    for zz in range(1, NZ):
        total = total + VZ[zz]
    vec_out[...] = total
    z_collect(0, 14)
    spread_all(0, "start")

    for step in range(1, g.fsdp):
        vec_copy(step).wait_send()
    finish_sends()
    for r in range(8):

        @pl.when(me != r)
        def _():
            vg_copy(r).wait_send()

    for d in range(1, NZ):
        vz_copy(d).wait_send()
        z_send(0, 14, d).wait_send()
        z_send(1, 15, d).wait_send()
    spread_wait()
    spread_all(1, "wait")
    spread_all(0, "wait")


def kernel_path(g, *args):
    rows, lens, cots = args[0:4], args[4:8], args[8:12]
    weights = args[12:16]
    gain, bias, gate = args[16:19]
    D, FF, R, T, T0, T1, NZ = g.d, g.ff, g.rows, g.t, g.t0, g.t1, g.nz
    vec = jnp.concatenate([gain.reshape(6, R), bias.reshape(6, R), gate], axis=0)
    vec = jnp.pad(vec, ((0, 2), (0, 128 - R)))
    vmem = lambda *shape: pltpu.VMEM(shape[:-1], shape[-1])
    dma = lambda *shape: pltpu.SemaphoreType.DMA(shape)
    in_vmem = pl.BlockSpec(memory_space=pltpu.VMEM)
    in_any = pl.BlockSpec(memory_space=pl.ANY)
    in_smem = pl.BlockSpec(memory_space=pltpu.SMEM)
    row_shapes = [jax.ShapeDtypeStruct(r.shape, BF) for r in rows]
    out_shape = row_shapes * 2 + [
        jax.ShapeDtypeStruct((2, 8, R, D), BF),
        jax.ShapeDtypeStruct((2, R, FF), BF),
        jax.ShapeDtypeStruct((2, 4 * R, D), BF),
        jax.ShapeDtypeStruct((16, D), F32),
        jax.ShapeDtypeStruct((8, T, D), BF),
        jax.ShapeDtypeStruct((8, T, D), BF),
        jax.ShapeDtypeStruct((8, T, 2 * D), BF),
        jax.ShapeDtypeStruct((8, T, D), BF),
    ]
    scratch = [
        vmem(2, 16, D, D, BF),
        vmem(g.fsdp, 16, 128, BF),
        vmem(16, D, F32),
        vmem(14, T, D, BF),
        vmem(T, FF, BF),
        vmem(T, FF, BF),
        vmem(3, T, D, BF),
        vmem(3, T, D, BF),
        vmem(T, D, BF),
        vmem(T, D, F32),
        vmem(T, D, F32),
        vmem(T, D, F32),
        vmem(3, T, D, F32),
        vmem(3, T, 1, F32),
        vmem(T, FF, F32),
        vmem(HEADS, T0, T1, F32),
        vmem(HEADS, T1, T0, F32),
        vmem(HEADS, T0, T0, F32),
        vmem(HEADS, T1, T1, F32),
        vmem(2, NZ - 1, 2, D // NZ, D, BF),
        vmem(2, 2, D // NZ, D, BF),
        vmem(16, D, F32),
        vmem(8, 16, D, F32),
        vmem(NZ, 16, D, F32),
        dma(17),
        dma(g.fsdp - 1),
        dma(g.fsdp - 1),
        dma(16, NZ - 1),
        dma(16, NZ - 1),
        dma(16, NZ),
        dma(16, NZ),
        dma(16, 2 * NZ),
        dma(16, 2 * NZ),
        dma(16, 2 * NZ),
        dma(16, 2 * NZ),
        dma(7, 8),
        dma(7, 8),
        dma(12),
        dma(40),
        dma(2, NZ - 1),
        dma(2, NZ - 1),
        dma(4, 8),
        dma(4, 8),
        dma(8),
        dma(8),
        dma(NZ - 1),
        dma(NZ - 1),
    ]
    results = pl.pallas_call(
        partial(layer_kernel, g),
        out_shape=out_shape,
        in_specs=[in_smem] * 4 + [in_vmem] * 8 + [in_any] * 5,
        out_specs=[in_vmem] * 8 + [in_any] * 3 + [in_vmem] + [in_any] * 4,
        scratch_shapes=scratch,
        compiler_params=pltpu.CompilerParams(
            collective_id=0, has_side_effects=True, vmem_limit_bytes=67043328
        ),
        name="layer",
    )(*lens, *rows, *cots, *weights, vec)
    ga, gu, gd, vectors = results[8:12]
    ga = ga.astype(F32)
    own = lax.dynamic_slice(vectors, (0, lax.axis_index("fsdp") * R), (16, R))
    return (
        *results[:8],
        ga[:, :6],
        ga[:, 6:],
        gu.astype(F32),
        gd.astype(F32),
        own[0:6].reshape(2, 3, R),
        own[6:12].reshape(2, 3, R),
        own[12:14],
    )


def solution(mesh):
    def per_device(*args):
        g = Geometry(mesh, [a.shape for a in args])
        return kernel_path(g, *args) if g.fits() else plain_path(*args)

    in_specs = (
        P(("dp", "fsdp"), None, None),
        P(("dp", "fsdp"), None, None),
        P(("dp", "fsdp"), None, None),
        P(("dp", "fsdp"), None, None),
        P(("dp", "fsdp")),
        P(("dp", "fsdp")),
        P(("dp", "fsdp")),
        P(("dp", "fsdp")),
        P(("dp", "fsdp"), None, None),
        P(("dp", "fsdp"), None, None),
        P(("dp", "fsdp"), None, None),
        P(("dp", "fsdp"), None, None),
        P(None, None, "fsdp", None),
        P(None, None, "fsdp", None),
        P(None, "fsdp", None),
        P(None, "fsdp", None),
        P(None, None, "fsdp"),
        P(None, None, "fsdp"),
        P(None, "fsdp"),
    )
    out_specs = (
        P(("dp", "fsdp"), None, None),
        P(("dp", "fsdp"), None, None),
        P(("dp", "fsdp"), None, None),
        P(("dp", "fsdp"), None, None),
        P(("dp", "fsdp"), None, None),
        P(("dp", "fsdp"), None, None),
        P(("dp", "fsdp"), None, None),
        P(("dp", "fsdp"), None, None),
        P(None, None, "fsdp", None),
        P(None, None, "fsdp", None),
        P(None, "fsdp", None),
        P(None, "fsdp", None),
        P(None, None, "fsdp"),
        P(None, None, "fsdp"),
        P(None, "fsdp"),
    )
    return jax.shard_map(
        per_device, mesh=mesh, in_specs=in_specs, out_specs=out_specs, check_vma=False
    )
```

```python
from functools import partial
import math

import jax
import jax.numpy as jnp
from jax import lax
from jax.experimental import pallas as pl
from jax.experimental.pallas import tpu as pltpu
from jax.sharding import PartitionSpec as P

HEADS = 12
BF = jnp.bfloat16
F32 = jnp.float32
MESH_ID = pl.DeviceIdType.MESH
NEG = -1000000000.0


def dot(a, b):
    return lax.dot_general(a, b, (((1,), (0,)), ((), ())), preferred_element_type=F32)


def dot_rt(a, b):
    return lax.dot_general(a, b, (((1,), (1,)), ((), ())), preferred_element_type=F32)


def dot_lt(a, b):
    return lax.dot_general(a, b, (((0,), (0,)), ((), ())), preferred_element_type=F32)


def loop(count, body):
    def step(index, carry):
        body(index)
        return carry

    lax.fori_loop(0, count, step, 0)


def cols(index, size):
    return pl.ds(pl.multiple_of(index * size, size), size)


def erf_of(value):
    x = jnp.minimum(jnp.maximum(value, -3.832506856900711), 3.832506856900711)
    y = x * x
    top = jnp.full_like(y, 0.00022905065861350646)
    for c in (0.0034082910107109506, 0.050955695062380861, 0.18520832239976145, 1.128379143519084):
        top = top * y + c
    low = jnp.full_like(y, -1.1791602954361697e-7)
    for c in (
        0.000023547966471313185,
        0.0010179625278914885,
        0.014070470171167667,
        0.11098505178285362,
        0.49746925110067538,
        1.0,
    ):
        low = low * y + c
    return x * top / low


def project(rows, matrix):
    return jnp.einsum("pld,de->ple", rows, matrix, preferred_element_type=jnp.float32)


def project_back(grads, matrix):
    return jnp.einsum("ple,de->pld", grads, matrix, preferred_element_type=jnp.float32)


def weight_grad(rows, grads):
    return jnp.einsum("pld,ple->de", rows, grads, preferred_element_type=jnp.float32)


def layer_norm(resid, gain_row, bias_row):
    centre = resid - jnp.mean(resid, axis=-1, keepdims=True)
    spread = jnp.mean(centre * centre, axis=-1, keepdims=True)
    return centre * lax.rsqrt(spread + 1e-05) * gain_row + bias_row


def gate_tail(resid, gain_row, bias_row, gate_row, row_mask):
    hidden_three = layer_norm(resid, gain_row, bias_row)
    logit = jnp.einsum("pld,d->pl", hidden_three, gate_row, precision=lax.Precision.HIGHEST)
    return hidden_three * (jax.nn.sigmoid(logit) * row_mask)[..., None]


def exact_gelu(upward):
    return jax.nn.gelu(upward, approximate=False)


def split_heads(rows):
    return rows.reshape(rows.shape[0], rows.shape[1], HEADS, rows.shape[2] // HEADS)


def masked_scores(queries, key_rows, key_mask):
    score_scale = 1.0 / math.sqrt(queries.shape[2] // HEADS)
    scores = (
        jnp.einsum(
            "plhe,pmhe->phlm",
            split_heads(queries),
            split_heads(key_rows),
            preferred_element_type=jnp.float32,
        )
        * score_scale
    )
    return jnp.where(key_mask[:, None, None, :], scores, -1000000000.0)


def attend_forward(queries, key_rows, value_rows, key_mask):
    masked = masked_scores(queries, key_rows, key_mask)
    row_max = jnp.max(masked, axis=-1, keepdims=True)
    expon = jnp.exp(masked - row_max)
    row_sum = jnp.sum(expon, axis=-1, keepdims=True)
    probs = expon / row_sum
    log_total = row_max + jnp.log(row_sum)
    mixed = jnp.einsum(
        "phlm,pmhe->plhe",
        probs.astype(jnp.bfloat16),
        split_heads(value_rows),
        preferred_element_type=jnp.float32,
    )
    return (mixed.reshape(queries.shape).astype(jnp.bfloat16), log_total)


def attend_backward(queries, key_rows, value_rows, key_mask, log_total, grad_mixed):
    score_scale = 1.0 / math.sqrt(queries.shape[2] // HEADS)
    masked = masked_scores(queries, key_rows, key_mask)
    probs = jnp.where(key_mask[:, None, None, :], jnp.exp(masked - log_total), 0.0)
    grad_heads = split_heads(grad_mixed)
    grad_probs = jnp.einsum(
        "plhe,pmhe->phlm", grad_heads, split_heads(value_rows), preferred_element_type=jnp.float32
    )
    grad_scores = (
        probs * (grad_probs - jnp.sum(grad_probs * probs, axis=-1, keepdims=True))
    ).astype(jnp.bfloat16)
    grad_query = (
        jnp.einsum(
            "phlm,pmhe->plhe",
            grad_scores,
            split_heads(key_rows),
            preferred_element_type=jnp.float32,
        )
        * score_scale
    )
    grad_key = (
        jnp.einsum(
            "phlm,plhe->pmhe", grad_scores, split_heads(queries), preferred_element_type=jnp.float32
        )
        * score_scale
    )
    grad_value = jnp.einsum(
        "phlm,plhe->pmhe",
        probs.astype(jnp.bfloat16),
        grad_heads,
        preferred_element_type=jnp.float32,
    )
    return (
        grad_query.reshape(queries.shape).astype(jnp.bfloat16),
        grad_key.reshape(key_rows.shape).astype(jnp.bfloat16),
        grad_value.reshape(value_rows.shape).astype(jnp.bfloat16),
    )


def cross_forward(own_rows, other_rows, other_keys, attn_in):
    cross_query = project(own_rows, attn_in[0]).astype(jnp.bfloat16)
    cross_key = project(other_rows, attn_in[1]).astype(jnp.bfloat16)
    cross_value = project(other_rows, attn_in[2]).astype(jnp.bfloat16)
    cross_mixed, cross_total = attend_forward(cross_query, cross_key, cross_value, other_keys)
    return ((cross_query, cross_key, cross_value), cross_mixed, cross_total)


def stream_forward(own_rows, other_rows, own_keys, other_keys, row_mask, params):
    attn_in, attn_out, ffn_up, ffn_down, gains, biases, gate_row = params
    _, cross_mixed, _ = cross_forward(own_rows, other_rows, other_keys, attn_in)
    resid_one = own_rows.astype(jnp.float32) + project(cross_mixed, attn_out[0])
    hidden_one = layer_norm(resid_one, gains[0], biases[0])
    hidden_low = hidden_one.astype(jnp.bfloat16)
    self_query = project(hidden_low, attn_in[3]).astype(jnp.bfloat16)
    self_key = project(hidden_low, attn_in[4]).astype(jnp.bfloat16)
    self_value = project(hidden_low, attn_in[5]).astype(jnp.bfloat16)
    self_mixed, self_total = attend_forward(self_query, self_key, self_value, own_keys)
    resid_two = hidden_one + project(self_mixed, attn_out[1])
    hidden_two = layer_norm(resid_two, gains[1], biases[1])
    ffn_in = hidden_two.astype(jnp.bfloat16)
    upward = project(ffn_in, ffn_up)
    active = exact_gelu(upward).astype(jnp.bfloat16)
    resid_three = hidden_two + project(active, ffn_down)
    output = gate_tail(resid_three, gains[2], biases[2], gate_row, row_mask)
    saved_rows = (
        resid_one,
        hidden_low,
        self_query,
        self_key,
        self_value,
        self_total,
        self_mixed,
        resid_two,
        ffn_in,
        upward,
        active,
        resid_three,
    )
    return (output, saved_rows)


def stream_backward(
    own_rows, other_rows, own_keys, other_keys, row_mask, params, saved_rows, grad_out
):
    attn_in, attn_out, ffn_up, ffn_down, gains, biases, gate_row = params
    (
        resid_one,
        hidden_low,
        self_query,
        self_key,
        self_value,
        self_total,
        self_mixed,
        resid_two,
        ffn_in,
        upward,
        active,
        resid_three,
    ) = saved_rows
    _, tail_pull = jax.vjp(
        partial(gate_tail, row_mask=row_mask), resid_three, gains[2], biases[2], gate_row
    )
    grad_three, gain_three, bias_three, grad_gate = tail_pull(grad_out)
    grad_down_in = grad_three.astype(jnp.bfloat16)
    down_grad = weight_grad(active, grad_down_in)
    grad_active = project_back(grad_down_in, ffn_down)
    _, gelu_pull = jax.vjp(exact_gelu, upward)
    grad_upward = gelu_pull(grad_active)[0].astype(jnp.bfloat16)
    up_grad = weight_grad(ffn_in, grad_upward)
    grad_two = grad_three + project_back(grad_upward, ffn_up)
    _, norm_two_pull = jax.vjp(layer_norm, resid_two, gains[1], biases[1])
    grad_resid_two, gain_two, bias_two = norm_two_pull(grad_two)
    grad_self_out = grad_resid_two.astype(jnp.bfloat16)
    self_out_grad = weight_grad(self_mixed, grad_self_out)
    grad_self_mixed = project_back(grad_self_out, attn_out[1]).astype(jnp.bfloat16)
    grad_self_query, grad_self_key, grad_self_value = attend_backward(
        self_query, self_key, self_value, own_keys, self_total, grad_self_mixed
    )
    grad_one = (
        grad_resid_two
        + project_back(grad_self_query, attn_in[3])
        + project_back(grad_self_key, attn_in[4])
        + project_back(grad_self_value, attn_in[5])
    )
    _, norm_one_pull = jax.vjp(layer_norm, resid_one, gains[0], biases[0])
    grad_resid_one, gain_one, bias_one = norm_one_pull(grad_one)
    grad_cross_out = grad_resid_one.astype(jnp.bfloat16)
    (cross_query, cross_key, cross_value), cross_mixed, cross_total = cross_forward(
        own_rows, other_rows, other_keys, attn_in
    )
    cross_out_grad = weight_grad(cross_mixed, grad_cross_out)
    grad_cross_mixed = project_back(grad_cross_out, attn_out[0]).astype(jnp.bfloat16)
    grad_cross_query, grad_cross_key, grad_cross_value = attend_backward(
        cross_query, cross_key, cross_value, other_keys, cross_total, grad_cross_mixed
    )
    grad_own = grad_resid_one + project_back(grad_cross_query, attn_in[0])
    grad_other = project_back(grad_cross_key, attn_in[1]) + project_back(
        grad_cross_value, attn_in[2]
    )
    in_grads = jnp.stack(
        [
            weight_grad(own_rows, grad_cross_query),
            weight_grad(other_rows, grad_cross_key),
            weight_grad(other_rows, grad_cross_value),
            weight_grad(hidden_low, grad_self_query),
            weight_grad(hidden_low, grad_self_key),
            weight_grad(hidden_low, grad_self_value),
        ]
    )
    out_grads = jnp.stack([cross_out_grad, self_out_grad])
    gain_grads = jnp.stack([gain_one, gain_two, gain_three])
    bias_grads = jnp.stack([bias_one, bias_two, bias_three])
    return (
        grad_own,
        grad_other,
        (in_grads, out_grads, up_grad, down_grad, gain_grads, bias_grads, grad_gate),
    )


def stream_params(gathered, stream):
    return (
        gathered[0][stream],
        gathered[1][stream],
        gathered[2][stream],
        gathered[3][stream],
        gathered[4][stream].astype(jnp.float32),
        gathered[5][stream].astype(jnp.float32),
        gathered[6][stream].astype(jnp.float32),
    )


def plain_path(
    text_a,
    visual_a,
    text_b,
    visual_b,
    text_len_a,
    visual_len_a,
    text_len_b,
    visual_len_b,
    cot_text_a,
    cot_visual_a,
    cot_text_b,
    cot_visual_b,
    attn_in,
    attn_out,
    ffn_up,
    ffn_down,
    norm_gain,
    norm_bias,
    gate_vector,
):
    gathered = (
        lax.all_gather(attn_in, "fsdp", axis=2, tiled=True),
        lax.all_gather(attn_out, "fsdp", axis=2, tiled=True),
        lax.all_gather(ffn_up, "fsdp", axis=1, tiled=True),
        lax.all_gather(ffn_down, "fsdp", axis=1, tiled=True),
        lax.all_gather(norm_gain, "fsdp", axis=2, tiled=True),
        lax.all_gather(norm_bias, "fsdp", axis=2, tiled=True),
        lax.all_gather(gate_vector, "fsdp", axis=1, tiled=True),
    )
    layouts = []
    for rows_text, rows_visual, len_text, len_visual, cot_text, cot_visual in (
        (text_a, visual_a, text_len_a, visual_len_a, cot_text_a, cot_visual_a),
        (text_b, visual_b, text_len_b, visual_len_b, cot_text_b, cot_visual_b),
    ):
        keys_text = jnp.arange(rows_text.shape[1], dtype=jnp.int32)[None, :] < len_text[:, None]
        keys_visual = (
            jnp.arange(rows_visual.shape[1], dtype=jnp.int32)[None, :] < len_visual[:, None]
        )
        stream_rows = (rows_text, rows_visual)
        stream_keys = (keys_text, keys_visual)
        stream_masks = (keys_text.astype(jnp.float32), keys_visual.astype(jnp.float32))
        outputs = []
        saved_list = []
        for stream in (0, 1):
            other_side = 1 - stream
            output, saved_rows = stream_forward(
                stream_rows[stream],
                stream_rows[other_side],
                stream_keys[stream],
                stream_keys[other_side],
                stream_masks[stream],
                stream_params(gathered, stream),
            )
            outputs.append(output.astype(jnp.bfloat16))
            saved_list.append(saved_rows)
        layouts.append(
            (stream_rows, stream_keys, stream_masks, (cot_text, cot_visual), outputs, saved_list)
        )
    back_weights = gathered
    input_grads = [[None, None], [None, None]]
    stream_grads = []
    for stream in (0, 1):
        other_side = 1 - stream
        params = stream_params(back_weights, stream)
        summed = None
        for layout_index in (0, 1):
            stream_rows, stream_keys, stream_masks, cotangents, outputs, saved_list = layouts[
                layout_index
            ]
            grad_own, grad_other, grads_here = stream_backward(
                stream_rows[stream],
                stream_rows[other_side],
                stream_keys[stream],
                stream_keys[other_side],
                stream_masks[stream],
                params,
                saved_list[stream],
                cotangents[stream].astype(jnp.float32),
            )
            for target, piece in ((stream, grad_own), (other_side, grad_other)):
                if input_grads[layout_index][target] is None:
                    input_grads[layout_index][target] = piece
                else:
                    input_grads[layout_index][target] = input_grads[layout_index][target] + piece
            if summed is None:
                summed = grads_here
            else:
                summed = tuple((left + right for left, right in zip(summed, grads_here)))
        stream_grads.append(summed)
    text_grads = stream_grads[0]
    visual_grads = stream_grads[1]
    row_dims = (1, 1, 0, 0, 1, 1, 0)
    packed = tuple(
        (
            jnp.concatenate([text_grads[index], visual_grads[index]], axis=row_dims[index])
            for index in range(7)
        )
    )
    shares = (
        lax.psum_scatter(packed[0], ("dp", "fsdp"), scatter_dimension=1, tiled=True),
        lax.psum_scatter(packed[1], ("dp", "fsdp"), scatter_dimension=1, tiled=True),
        lax.psum_scatter(packed[2], ("dp", "fsdp"), scatter_dimension=0, tiled=True),
        lax.psum_scatter(packed[3], ("dp", "fsdp"), scatter_dimension=0, tiled=True),
        lax.psum_scatter(packed[4], ("dp", "fsdp"), scatter_dimension=1, tiled=True),
        lax.psum_scatter(packed[5], ("dp", "fsdp"), scatter_dimension=1, tiled=True),
        lax.psum_scatter(packed[6], ("dp", "fsdp"), scatter_dimension=0, tiled=True),
    )
    joined = (
        lax.all_gather(shares[0].astype(jnp.bfloat16), "dp", axis=1, tiled=True).astype(
            jnp.float32
        ),
        lax.all_gather(shares[1].astype(jnp.bfloat16), "dp", axis=1, tiled=True).astype(
            jnp.float32
        ),
        lax.all_gather(shares[2].astype(jnp.bfloat16), "dp", axis=0, tiled=True).astype(
            jnp.float32
        ),
        lax.all_gather(shares[3].astype(jnp.bfloat16), "dp", axis=0, tiled=True).astype(
            jnp.float32
        ),
        lax.all_gather(shares[4].astype(jnp.bfloat16), "dp", axis=1, tiled=True).astype(
            jnp.float32
        ),
        lax.all_gather(shares[5].astype(jnp.bfloat16), "dp", axis=1, tiled=True).astype(
            jnp.float32
        ),
        lax.all_gather(shares[6].astype(jnp.bfloat16), "dp", axis=0, tiled=True).astype(
            jnp.float32
        ),
    )
    finals = tuple(
        (jnp.stack(jnp.split(joined[index], 2, axis=row_dims[index])) for index in range(7))
    )
    first_outputs = layouts[0][4]
    second_outputs = layouts[1][4]
    return (
        first_outputs[0],
        first_outputs[1],
        second_outputs[0],
        second_outputs[1],
        input_grads[0][0].astype(jnp.bfloat16),
        input_grads[0][1].astype(jnp.bfloat16),
        input_grads[1][0].astype(jnp.bfloat16),
        input_grads[1][1].astype(jnp.bfloat16),
        finals[0],
        finals[1],
        finals[2],
        finals[3],
        finals[4],
        finals[5],
        finals[6],
    )


class Geometry:
    def __init__(self, mesh, shapes):
        self.dp = mesh.shape["dp"]
        self.fsdp = mesh.shape["fsdp"]
        (self.la, self.lva), (self.lb, self.lvb) = (
            (shapes[0][1], shapes[1][1]),
            (shapes[2][1], shapes[3][1]),
        )
        self.d = shapes[0][2]
        self.rows = self.d // self.fsdp
        self.ff = shapes[14][2]
        self.pages = shapes[0][0]
        self.t0 = -(-(self.la + self.lb) // 16) * 16
        self.t1 = -(-(self.lva + self.lvb) // 16) * 16
        self.t = self.t0 + self.t1
        self.nz = self.fsdp // 4

    def fits(self):
        return (
            self.dp == 2
            and self.fsdp == 16
            and self.pages == 1
            and self.d == 16 * 48
            and self.ff == 4 * self.d
            and self.t0 >= self.t1
            and self.d == 64 * HEADS
        )


def layer_kernel(g, *refs):
    D, FF, R, T0, T1, T, NZ = g.d, g.ff, g.rows, g.t0, g.t1, g.t, g.nz
    ZR = D // NZ
    it = iter(refs)
    take = lambda n: [next(it) for _ in range(n)]
    lens = take(4)
    rows_in = take(4)
    cots_in = take(4)
    w_parts = take(4)
    (vec_in,) = take(1)
    outs = take(4)
    grads = take(4)
    ga, gu, gd, vec_out = take(4)
    ra, rg, rfa, rfg = take(4)
    W, VEC, vecs = take(3)
    S, A, DU, CQ, SQ, DO = take(6)
    RES, HID, DR, XH, RSTD, GP = take(6)
    p_refs = take(4)
    RZ, FB, VG, VR, VZ = take(5)
    (s_loc, s_vec, r_vec, sz, rz, sy, ry, sx, rx, sc, rc) = take(11)
    (s_ex, r_ex, s_own, s_st, s_zr, r_zr, s_rd, r_rd, s_vg, r_vg, s_vz, r_vz) = take(12)

    X, H1, OC, OS, H2 = 0, 1, 2, 3, 4
    DQC, DKC, DVC, DQS, DKS, DVS, DC, DS, DF = range(5, 14)
    span = (slice(0, T0), slice(T0, T))
    size = (T0, T1)

    x = lax.axis_index("dp")
    f = lax.axis_index("fsdp")
    z, y, c = f // 4, (f // 2) % 2, f % 2
    me = c * 4 + x * 2 + y

    def device(xx, zz, yy, cc):
        return (xx, zz * 4 + yy * 2 + cc)

    def role_device(r):
        return device((r // 2) % 2, z, r % 2, r // 4)

    def remote(src, dst, send, recv, dev):
        return pltpu.make_async_remote_copy(
            src_ref=src, dst_ref=dst, send_sem=send, recv_sem=recv, device_id=dev,
            device_id_type=MESH_ID,
        )

    barrier = pltpu.get_barrier_semaphore()
    for step in range(1, g.fsdp):
        pl.semaphore_signal(
            barrier, inc=1, device_id=(x, (f + step) % g.fsdp), device_id_type=MESH_ID
        )
    for r in range(4):
        pl.semaphore_signal(
            barrier, inc=1, device_id=device(1 - x, z, r // 2, r % 2), device_id_type=MESH_ID
        )
    pl.semaphore_wait(barrier, g.fsdp + 3)

    def wref(k, ff, r0, n):
        kk = k % 16
        down = kk // 12
        unit = kk + down * (12 + (4 * R * ff) // D - kk)
        row = R * ff + down * ((4 * R * ff) % D + R * (kk - 12) - R * ff) + r0
        return W.at[k // 16, unit, pl.ds(pl.multiple_of(row, 16), n)]

    def local_part(k):
        w_in, w_out, w_up, w_dn = w_parts
        s, k = k // 16, k % 16
        if k in (3, 7):
            return w_out.at[s, (k - 3) // 4]
        if k < 8:
            return w_in.at[s, (0, 1, 2, None, 3, 4, 5)[k]]
        if k < 12:
            return w_up.at[s, :, pl.ds(D * (k - 8), D)]
        return w_dn.at[s, pl.ds(R * (k - 12), R)]

    third = R // 3
    NK = 32
    local = []
    for k in range(NK):
        cp = pltpu.make_async_copy(local_part(k), wref(k, f, 0, R), s_loc.at[k])
        cp.start()
        local.append(cp)

    def vec_copy(step):
        return remote(
            vec_in, VEC.at[f], s_vec.at[step - 1], r_vec.at[step - 1],
            (x, (f + step) % g.fsdp),
        )

    def vec_wait(step):
        ref = VEC.at[(f + g.fsdp - step) % g.fsdp]
        remote(ref, ref, s_vec.at[step - 1], r_vec.at[step - 1], (x, f)).wait_recv()

    for step in range(1, g.fsdp):
        vec_copy(step).start()
    own_vec = pltpu.make_async_copy(vec_in, VEC.at[f], s_loc.at[NK])
    own_vec.start()

    def shard(zz, yy):
        return zz * 4 + yy * 2 + c

    def z_copy(k, d):
        ref = wref(k, f, third * x, 2 * third)
        return remote(ref, ref, sz.at[k, d - 1], rz.at[k, d - 1], device(x, (z + d) % NZ, y, c))

    def z_wait(k, d):
        ref = wref(k, shard((z + NZ - d) % NZ, y), third * x, 2 * third)
        remote(ref, ref, sz.at[k, d - 1], rz.at[k, d - 1], device(x, (z + d) % NZ, y, c)).wait_recv()

    def y_copy(k, d):
        ref = wref(k, shard((z + NZ - d) % NZ, y), third * x, 2 * third)
        return remote(ref, ref, sy.at[k, d], ry.at[k, d], device(x, z, 1 - y, c))

    def y_wait(k, d):
        ref = wref(k, shard((z + NZ - d) % NZ, 1 - y), third * x, 2 * third)
        remote(ref, ref, sy.at[k, d], ry.at[k, d], device(x, z, 1 - y, c)).wait_recv()

    def x_copy(k, d, e):
        ref = wref(k, shard((z + NZ - d) % NZ, (y + e) % 2), 2 * third * x, third)
        return remote(ref, ref, sx.at[k, 2 * d + e], rx.at[k, 2 * d + e], device(1 - x, z, y, c))

    def x_wait(k, d, e):
        ref = wref(k, shard((z + NZ - d) % NZ, (y + e) % 2), 2 * third * (1 - x), third)
        remote(ref, ref, sx.at[k, 2 * d + e], rx.at[k, 2 * d + e], device(1 - x, z, y, c)).wait_recv()

    def c_copy(k, d, e):
        ref = wref(k, shard((z + NZ - d) % NZ, (y + e) % 2), 0, R)
        return remote(ref, ref, sc.at[k, 2 * d + e], rc.at[k, 2 * d + e], device(x, z, y, 1 - c))

    def c_wait(k, d, e):
        other = ((z + NZ - d) % NZ) * 4 + ((y + e) % 2) * 2 + 1 - c
        ref = wref(k, other, 0, R)
        remote(ref, ref, sc.at[k, 2 * d + e], rc.at[k, 2 * d + e], device(x, z, y, 1 - c)).wait_recv()

    for k in range(NK):
        local[k].wait()
        for d in range(1, NZ):
            z_copy(k, d).start()
        y_copy(k, 0).start()
        c_copy(k, 0, 0).start()

    def gather_step(t):
        @pl.when(t < NK)
        def _():
            for d in range(1, NZ):
                z_wait(t, d)
                y_copy(t, d).start()
                x_copy(t, d, 0).start()

        @pl.when((t >= 1) & (t < NK + 1))
        def _():
            for d in range(NZ):
                y_wait(t - 1, d)
                x_copy(t - 1, d, 1).start()

        @pl.when((t >= 2) & (t < NK + 2))
        def _():
            for e in range(2):
                for d in range(NZ):
                    if d or e:
                        x_wait(t - 2, d, e)
                        c_copy(t - 2, d, e).start()

        @pl.when(t >= 3)
        def _():
            for e in range(2):
                for d in range(NZ):
                    c_wait(t - 3, d, e)

    def gather_steps(lo, hi):
        def step(t, carry):
            gather_step(t)
            return carry

        lax.fori_loop(lo, hi, step, 0)

    la, lva = g.la, g.lva

    def assemble(dst, parts):
        ta, va, tb, vb = parts
        dst[0:la] = ta[0].astype(F32)
        dst[la : la + g.lb] = tb[0].astype(F32)
        if T0 > la + g.lb:
            dst[la + g.lb : T0] = jnp.zeros((T0 - la - g.lb, D), F32)
        dst[T0 : T0 + lva] = va[0].astype(F32)
        dst[T0 + lva : T0 + lva + g.lvb] = vb[0].astype(F32)
        if T1 > lva + g.lvb:
            dst[T0 + lva + g.lvb : T] = jnp.zeros((T1 - lva - g.lvb, D), F32)

    assemble(HID, rows_in)
    S[X] = HID[...].astype(BF)
    assemble(DR, cots_in)

    def live(index, s):
        first, second = (la, g.lb) if s == 0 else (lva, g.lvb)
        na, nb = lens[s][0], lens[2 + s][0]
        return ((index < first) & (index < na)) | (
            (index >= first) & (index - first < nb) & (index - first < second)
        )

    def key_mask(qs, ks):
        shape = (size[qs], size[ks])
        qi = lax.broadcasted_iota(jnp.int32, shape, 0)
        ki = lax.broadcasted_iota(jnp.int32, shape, 1)
        q_first = la if qs == 0 else lva
        k_first = la if ks == 0 else lva
        same = ((qi < q_first) & (ki < k_first)) | ((qi >= q_first) & (ki >= k_first))
        return same & live(ki, ks)

    UA = (0, 1, 2, 4, 5, 6)
    UB = (3, 7)

    def wtile(s, u, i):
        return W[s, u, :, cols(i, 256)]

    def wrows(s, u, i):
        return W[s, u, cols(i, 256), :]

    NT = D // 256

    def cross_project(s):
        own, other = span[s], span[1 - s]

        def q_tile(i):
            CQ[0, own, cols(i, 256)] = dot(S[X, own], wtile(s, 0, i)).astype(BF)

        loop(NT, q_tile)

        def kv_tile(i):
            m = 1 + i // NT
            j = i % NT
            CQ[m, other, cols(j, 256)] = dot(S[X, other], wtile(s, m, j)).astype(BF)

        loop(2 * NT, kv_tile)

    def self_project(s):
        own = span[s]

        def tile(i):
            m = i // NT
            j = i % NT
            SQ[m, own, cols(j, 256)] = dot(S[H1, own], wtile(s, 4 + m, j)).astype(BF)

        loop(3 * NT, tile)

    def attend(src, base, s, ks, p_ref, o_index):
        own, keys = span[s], span[ks]

        def pair(p):
            lanes = cols(p, 128)
            mask = key_mask(s, ks)
            q, k, v = src[base, own, lanes], src[base + 1, keys, lanes], src[base + 2, keys, lanes]
            low = lax.broadcasted_iota(jnp.int32, q.shape, 1) < 64
            high = lax.broadcasted_iota(jnp.int32, q.shape, 1) >= 64
            mixed = []
            for half in range(2):
                qh = jnp.where(low if half == 0 else high, q, jnp.zeros_like(q))
                scores = jnp.where(mask, dot_rt(qh, k) * 0.125, NEG)
                top = jnp.max(scores, axis=-1, keepdims=True)
                expon = jnp.exp(scores - top)
                probs = expon / jnp.sum(expon, axis=-1, keepdims=True)
                p_ref[2 * p + half] = probs
                mixed.append(dot(probs.astype(BF), v))
            S[o_index, own, lanes] = jnp.where(low, mixed[0], mixed[1]).astype(BF)

        loop(HEADS // 2, pair)

    def attend_back(src, base, s, ks, p_ref, gq, gk, gv):
        own, keys = span[s], span[ks]

        def pair(p):
            lanes = cols(p, 128)
            q, k, v = src[base, own, lanes], src[base + 1, keys, lanes], src[base + 2, keys, lanes]
            do = DO[own, lanes]
            low_q = lax.broadcasted_iota(jnp.int32, q.shape, 1) < 64
            high_q = lax.broadcasted_iota(jnp.int32, q.shape, 1) >= 64
            low_k = lax.broadcasted_iota(jnp.int32, k.shape, 1) < 64
            dq, dk, dv = [], [], []
            for half in range(2):
                doh = jnp.where(low_q if half == 0 else high_q, do, jnp.zeros_like(do))
                probs = p_ref[2 * p + half]
                dp = dot_rt(doh, v)
                ds = (probs * (dp - jnp.sum(dp * probs, axis=-1, keepdims=True))).astype(BF)
                dq.append(dot(ds, k))
                dk.append(dot_lt(ds, q))
                dv.append(dot_lt(probs.astype(BF), do))
            S[gq, own, lanes] = (jnp.where(low_q, dq[0], dq[1]) * 0.125).astype(BF)
            S[gk, keys, lanes] = (jnp.where(low_k, dk[0], dk[1]) * 0.125).astype(BF)
            S[gv, keys, lanes] = jnp.where(low_k, dv[0], dv[1]).astype(BF)

        loop(HEADS // 2, pair)

    def out_project(o_index, which, s):
        own = span[s]

        def tile(i):
            RES[own, cols(i, 256)] = HID[own, cols(i, 256)] + dot(
                S[o_index, own], wtile(s, UB[which], i)
            )

        loop(NT, tile)

    RB = 16
    mean = lambda v: jnp.sum(v, axis=-1, keepdims=True) * (1.0 / D)

    def normalize(i, r):
        resid = RES[r]
        centre = resid - mean(resid)
        rstd = lax.rsqrt(mean(centre * centre) + 1e-05)
        return centre * rstd, rstd

    def rows_of(s, b):
        return pl.ds(pl.multiple_of((0, T0)[s] + b * RB, RB), RB)

    def norm_forward(i, h_index, s):
        def block(b):
            r = rows_of(s, b)
            xh, rstd = normalize(i, r)
            XH[i, r] = xh
            RSTD[i, r] = rstd
            hidden = xh * vecs[pl.ds(s * 3 + i, 1), :] + vecs[pl.ds(6 + s * 3 + i, 1), :]
            HID[r] = hidden
            S[h_index, r] = hidden.astype(BF)

        loop(size[s] // RB, block)

    def add_row(row, value):
        VG[pl.ds(row, 1), :] += jnp.sum(value, axis=0, keepdims=True)

    def norm_pull(i, s, r, dh, xh, rstd):
        add_row(s * 3 + i, dh * xh)
        add_row(6 + s * 3 + i, dh)
        dx = dh * vecs[pl.ds(s * 3 + i, 1), :]
        return rstd * (dx - mean(dx) - xh * mean(dx * xh))

    def norm_backward(i, g_index, s):
        def block(b):
            r = rows_of(s, b)
            dr = norm_pull(i, s, r, DR[r], XH[i, r], RSTD[i, r])
            DR[r] = dr
            S[g_index, r] = dr.astype(BF)

        loop(size[s] // RB, block)

    def tail(s):
        def block(b):
            r = rows_of(s, b)
            xh, rstd = normalize(2, r)
            gain = vecs[pl.ds(s * 3 + 2, 1), :]
            h3 = xh * gain + vecs[pl.ds(6 + s * 3 + 2, 1), :]
            gate = vecs[pl.ds(12 + s, 1), :]
            logit = jnp.sum(h3 * gate, axis=-1, keepdims=True)
            sig = 1.0 / (1.0 + jnp.exp(-logit))
            index = lax.broadcasted_iota(jnp.int32, (RB, 1), 0) + b * RB
            mask = jnp.where(live(index, s), 1.0, 0.0)
            weight = sig * mask
            HID[r] = h3 * weight
            dout = DR[r]
            dlogit = jnp.sum(dout * h3, axis=-1, keepdims=True) * weight * (1.0 - sig)
            add_row(12 + s, h3 * dlogit)
            dr = norm_pull(2, s, r, dout * weight + dlogit * gate, xh, rstd)
            DR[r] = dr
            S[DF, r] = dr.astype(BF)

        loop(size[s] // RB, block)
        o_ta, o_va, o_tb, o_vb = outs
        if s == 0:
            o_ta[0] = HID[0:la].astype(BF)
            o_tb[0] = HID[la : la + g.lb].astype(BF)
        else:
            o_va[0] = HID[T0 : T0 + lva].astype(BF)
            o_vb[0] = HID[T0 + lva : T0 + lva + g.lvb].astype(BF)

    def ffn_up(q, s):
        own = span[s]

        def tile(i):
            j = q * NT + i
            u = dot(S[H2, own], wtile(s, 8 + q, i))
            cdf = 0.5 + 0.5 * erf_of(u * 0.7071067811865476)
            A[own, cols(j, 256)] = (u * cdf).astype(BF)
            GP[own, cols(j, 256)] = cdf + u * (
                jnp.exp(u * u * -0.5) * 0.3989422804014327
            )

        loop(NT, tile)

    def ffn_down(s):
        own = span[s]

        def tile(i):
            total = HID[own, cols(i, 256)]
            for q in range(4):
                total = total + dot(A[own, D * q : D * q + D], wtile(s, 12 + q, i))
            RES[own, cols(i, 256)] = total

        loop(NT, tile)

    def ffn_down_back(s):
        own = span[s]

        def tile(j):
            da = dot_rt(S[DF, own], wrows(s, 12 + j // NT, j % NT))
            DU[own, cols(j, 256)] = (GP[own, cols(j, 256)] * da).astype(BF)

        loop(4 * NT, tile)

    def ffn_up_back(s):
        own = span[s]

        def tile(i):
            total = DR[own, cols(i, 256)]
            for q in range(4):
                total = total + dot_rt(DU[own, D * q : D * q + D], wrows(s, 8 + q, i))
            DR[own, cols(i, 256)] = total

        loop(NT, tile)

    def out_back(g_index, which, s):
        own = span[s]

        def tile(i):
            DO[own, cols(i, 256)] = dot_rt(
                S[g_index, own], wrows(s, UB[which], i)
            ).astype(BF)

        loop(NT, tile)

    def self_back(s):
        own = span[s]

        def tile(i):
            total = DR[own, cols(i, 256)]
            for m, gi in enumerate((DQS, DKS, DVS)):
                total = total + dot_rt(S[gi, own], wrows(s, 4 + m, i))
            DR[own, cols(i, 256)] = total

        loop(NT, tile)

    def cross_back(s):
        own = span[s]

        def tile(i):
            total = DR[own, cols(i, 256)] + dot_rt(S[DQC, own], wrows(s, 0, i))
            total = total + dot_rt(S[DKC, own], wrows(1 - s, 1, i))
            total = total + dot_rt(S[DVC, own], wrows(1 - s, 2, i))
            DR[own, cols(i, 256)] = total

        loop(NT, tile)
        g_ta, g_va, g_tb, g_vb = grads
        if s == 0:
            g_ta[0] = DR[0:la].astype(BF)
            g_tb[0] = DR[la : la + g.lb].astype(BF)
        else:
            g_va[0] = DR[T0 : T0 + lva].astype(BF)
            g_vb[0] = DR[T0 + lva : T0 + lva + g.lvb].astype(BF)

    sends = []

    def plane_send(r, src, dst, slot):
        @pl.when(me != r)
        def _():
            remote(src, dst, s_ex.at[slot, r], r_ex.at[slot, me], role_device(r)).start()

        @pl.when(me == r)
        def _():
            pltpu.make_async_copy(src, dst, s_own.at[slot]).start()

        sends.append((r, src, dst, slot))

    def finish_sends():
        for r, src, dst, slot in sends:

            @pl.when(me != r)
            def _():
                remote(src, dst, s_ex.at[slot, r], r_ex.at[slot, me], role_device(r)).wait_send()

    def plane_wait(slot, pick):
        for p in range(8):
            ref = pick(p)

            @pl.when(me != p)
            def _():
                remote(ref, ref, s_ex.at[slot, p], r_ex.at[slot, p], role_device(p)).wait_recv()

            @pl.when(me == p)
            def _():
                pltpu.make_async_copy(ref, ref, s_own.at[slot]).wait()

    A_OF = (X, X, X, OC, H1, H1, H1, OS)
    G_OF = (DQC, DKC, DVC, DC, DQS, DKS, DVS, DS)
    HB = D // 2

    def rows_for(r, s):
        t = 1 - s if r in (1, 2) else s
        return pl.ds((0, T0)[t], size[t])

    def send_left(r, s):
        rows = rows_for(r, s)
        plane_send(r, S.at[A_OF[r], rows], ra.at[me, rows], 7 * s)

    def send_right(r, s):
        rows = rows_for(r, s)
        plane_send(r, S.at[G_OF[r], rows], rg.at[me, rows], 7 * s + 1)

    def own_rows(s):
        return pl.ds((0, T0)[s], size[s])

    def send_ffn_left(r, q, s):
        rows = own_rows(s)
        if r < 4:
            plane_send(r, S.at[H2, rows], rfa.at[me, rows, pl.ds(0, D)], 7 * s + 3)
        else:
            plane_send(
                r, A.at[rows, pl.ds(D * q + HB * (r % 2), HB)],
                rfa.at[me, rows, pl.ds(HB * q, HB)], 7 * s + 3 + q,
            )

    def send_ffn_right(r, s):
        rows = own_rows(s)
        if r < 4:
            plane_send(r, DU.at[rows, pl.ds(D * r, D)], rfg.at[me, rows], 7 * s + 2)
        else:
            hh = (r // 2) % 2
            plane_send(
                r, S.at[DF, rows, pl.ds(HB * hh, HB)], rfg.at[me, rows, pl.ds(0, HB)], 7 * s + 2
            )

    flip = (((me + 1) // 2) % 2) * (1 - me // 4)

    def stage(s, rows, n, first, blocks):
        made = []
        for src, unit, col in blocks:
            for p in range(8):
                made.append(
                    pltpu.make_async_copy(
                        src.at[p, rows, pl.ds(col, D)],
                        W.at[s, unit + p // 4, pl.ds(n * (p % 4), n)],
                        s_st.at[first + len(made)],
                    )
                )
        for cp in made:
            cp.start()
        for cp in made:
            cp.wait()

    def stacked(s, unit, n, lanes):
        return jnp.concatenate(
            [W[s, unit + p // 4, n * (p % 4) : n * (p % 4) + n, lanes] for p in range(8)], axis=0
        )

    def weight_grad(s, n, dst):
        def tile(i):
            W[s, dst, cols(i, 256), :] = dot_lt(
                stacked(s, 8, n, cols(i, 256)), stacked(s, 12, n, slice(0, D))
            ).astype(BF)

        loop(NT, tile)

    def weight_grad_down(s, n, dst):
        def tile(q):
            out = dot_lt(
                stacked(s, 8 + 2 * (q // 2), n, cols(q % 2, HB)), stacked(s, 12, n, slice(0, HB))
            ).astype(BF)
            W[s, dst, pl.ds(pl.multiple_of(q * ZR, ZR), ZR), 0:HB] = out[0:ZR]
            W[s, dst, pl.ds(pl.multiple_of(q * ZR, ZR), ZR), HB:D] = out[ZR : 2 * ZR]

        loop(4, tile)

    def z_send(n, s, d):
        zz = (z + d) % NZ
        src = W.at[s, 14 + n, pl.ds(pl.multiple_of(zz * ZR, ZR), ZR)]
        return remote(
            src, RZ.at[n, s, d - 1], s_zr.at[n, s, d - 1], r_zr.at[n, s, d - 1],
            device(x, zz, y, c),
        )

    def z_collect(n, s):
        for d in range(1, NZ):
            z_send(n, s, d).wait_recv()

        def block(i):
            total = W[s, 14 + n, pl.ds(pl.multiple_of(z * ZR + i * 16, 16), 16)].astype(F32)
            for d in range(NZ - 1):
                total = total + RZ[n, s, d, cols(i, 16)].astype(F32)
            FB[n, s, cols(i, 16)] = total.astype(BF)

        loop(ZR // 16, block)

    def ffn_share(s):
        rows, n = own_rows(s), size[s]

        @pl.when(me < 4)
        def _():
            plane_wait(7 * s + 2, lambda p: rfg.at[p, rows])
            plane_wait(7 * s + 3, lambda p: rfa.at[p, rows, pl.ds(0, D)])

        @pl.when(me >= 4)
        def _():
            plane_wait(7 * s + 2, lambda p: rfg.at[p, rows, pl.ds(0, HB)])
            for q in range(4):
                plane_wait(7 * s + 3 + q, lambda p: rfa.at[p, rows, pl.ds(HB * q, HB)])

        stage(s, rows, n, 0, ((rfg, 12, 0), (rfa, 8, 0), (rfa, 10, D)))

        @pl.when(me < 4)
        def _():
            weight_grad(s, n, 15)

        @pl.when(me >= 4)
        def _():
            weight_grad_down(s, n, 15)

        for d in range(1, NZ):
            z_send(1, s, d).start()

    def attention_share(s):
        def branch(r):
            rows, n = rows_for(r, s), size[1 - s if r in (1, 2) else s]
            plane_wait(7 * s, lambda p: ra.at[p, rows])
            plane_wait(7 * s + 1, lambda p: rg.at[p, rows])
            stage(s, rows, n, 24, ((ra, 8, 0), (rg, 12, 0)))
            weight_grad(s, n, 14)

        @pl.when(flip == 0)
        def _():
            branch(0)

        @pl.when(flip == 1)
        def _():
            branch(1)

        for d in range(1, NZ):
            z_send(0, s, d).start()

    slot_of = me + 3 * (me // 3) * (1 - me // 4) - (me // 4) * (1 - me // 7)

    def attn_block(r, s):
        return FB.at[0, s, pl.ds(R * (2 * (r % 2) + r // 4), R)], ga.at[s, slot_of]

    def up_block(r, s):
        return (
            FB.at[1, s, pl.ds(R * (2 * (r % 2) + r // 4), R)],
            gu.at[s, :, pl.ds(pl.multiple_of(D * (me % 4), 128), D)],
        )

    def down_block(r, s):
        return (
            FB.at[1, s, :, pl.ds(HB * (r // 4), HB)],
            gd.at[s, :, pl.ds(pl.multiple_of(HB * ((me // 2) % 2), 128), HB)],
        )

    def spread(r, n, s, block, cond, act):
        src, dst = block(r, s)

        @pl.when(cond & (me != r))
        def _():
            cp = remote(src, dst, s_rd.at[2 * n + s, r], r_rd.at[2 * n + s, me], role_device(r))
            cp.start() if act == "start" else cp.wait_send()

        @pl.when(cond & (me == r))
        def _():
            cp = pltpu.make_async_copy(src, dst, s_own.at[14 + 2 * n + s])
            cp.start() if act == "start" else cp.wait()

    def spread_all(n, s, act):
        for r in range(8):
            if n == 0:
                spread(r, n, s, attn_block, me >= 0, act)
            else:
                spread(r, n, s, up_block, me < 4, act)
                spread(r, n, s, down_block, (me >= 4) & (me % 2 == r % 2), act)

    def spread_wait():
        def arrived(ref, n, s, p):
            remote(
                ref, ref, s_rd.at[2 * n + s, p], r_rd.at[2 * n + s, p], role_device(p)
            ).wait_recv()

        for p in range(8):

            @pl.when(me != p)
            def _():
                for s in range(2):
                    arrived(ga.at[s, p], 0, s, p)
                    if p < 4:
                        arrived(gu.at[s, :, pl.ds(D * p, D)], 1, s, p)

            if p >= 4:

                @pl.when((me != p) & (y == p % 2))
                def _():
                    for s in range(2):
                        arrived(gd.at[s, :, pl.ds(HB * (p % 2), HB)], 1, s, p)

    VG[...] = jnp.zeros_like(VG)
    for step in range(1, g.fsdp):
        vec_wait(step)
    own_vec.wait()
    total = jnp.zeros((16, D), F32)
    lane = lax.broadcasted_iota(jnp.int32, (128, D), 0)
    col = lax.broadcasted_iota(jnp.int32, (128, D), 1)
    for ff in range(g.fsdp):
        pick = ((col == lane + R * ff) & (lane < R)).astype(F32).astype(BF)
        total = total + dot(VEC[ff], pick)
    vecs[...] = total

    reached = [0]

    def gather_to(t):
        if t > reached[0]:
            gather_steps(reached[0], t)
            reached[0] = t

    def gather_more(n):
        gather_to(min(reached[0] + n, NK + 3))

    def gather_sent(k):
        for d in range(1, NZ):
            z_copy(k, d).wait_send()
        for d in range(NZ):
            y_copy(k, d).wait_send()
            for e in range(2):
                c_copy(k, d, e).wait_send()
                if d or e:
                    x_copy(k, d, e).wait_send()

    for s in range(2):
        base = 16 * s + 4
        gather_to(base + 2)
        cross_project(s)
        gather_to(base + 3)
        attend(CQ, 0, s, 1 - s, p_refs[s], OC)
        if s == 1:
            z_collect(1, 0)
            spread_all(1, 0, "start")
        gather_to(base + 4)
        out_project(OC, 0, s)
        norm_forward(0, H1, s)
        gather_to(base + 6)
        self_project(s)
        gather_to(base + 7)
        attend(SQ, 0, s, s, p_refs[2 + s], OS)
        if s == 1:
            z_collect(0, 0)
            spread_all(0, 0, "start")
        gather_to(base + 8)
        out_project(OS, 1, s)
        norm_forward(1, H2, s)
        for r in range(4):
            send_ffn_left(r, 0, s)
        for q in range(4):
            gather_to(base + 8 + q)
            ffn_up(q, s)
            for r in range(4, 8):
                send_ffn_left(r, q, s)
        gather_to(base + 15)
        ffn_down(s)
        gather_more(1)
        tail(s)
        for r in range(4, 8):
            send_ffn_right(r, s)
        gather_more(1)
        ffn_down_back(s)
        for r in range(4):
            send_ffn_right(r, s)
        for r in range(8):
            send_left(r, s)
        gather_more(1)
        ffn_up_back(s)
        norm_backward(1, DS, s)
        send_right(7, s)
        gather_more(1)
        out_back(DS, 1, s)
        attend_back(SQ, 0, s, s, p_refs[2 + s], DQS, DKS, DVS)
        for r in (4, 5, 6):
            send_right(r, s)
        gather_more(1)
        lax.fori_loop(16 * s, 16 * s + 16, lambda k, carry: (gather_sent(k), carry)[1], 0)
        ffn_share(s)
        gather_more(1)
        self_back(s)
        norm_backward(0, DC, s)
        send_right(3, s)
        gather_more(1)
        out_back(DC, 0, s)
        attend_back(CQ, 0, s, 1 - s, p_refs[s], DQC, DKC, DVC)
        for r in (0, 1, 2):
            send_right(r, s)
        gather_more(1)
        attention_share(s)

    def vg_copy(r):
        return remote(VG, VR.at[me], s_vg.at[r], r_vg.at[me], role_device(r))

    for r in range(8):

        @pl.when(me != r)
        def _():
            vg_copy(r).start()

    VR[me] = VG[...]
    cross_back(0)
    cross_back(1)

    for p in range(8):

        @pl.when(me != p)
        def _():
            ref = VR.at[p]
            remote(ref, ref, s_vg.at[p], r_vg.at[p], role_device(p)).wait_recv()

    total = VR[0]
    for p in range(1, 8):
        total = total + VR[p]
    VZ[z] = total

    def vz_copy(d):
        return remote(
            VZ.at[z], VZ.at[z], s_vz.at[d - 1], r_vz.at[d - 1], device(x, (z + d) % NZ, y, c)
        )

    for d in range(1, NZ):
        vz_copy(d).start()
    z_collect(1, 1)
    spread_all(1, 1, "start")
    for d in range(1, NZ):
        ref = VZ.at[(z + NZ - d) % NZ]
        remote(ref, ref, s_vz.at[d - 1], r_vz.at[d - 1], device(x, z, y, c)).wait_recv()
    total = VZ[0]
    for zz in range(1, NZ):
        total = total + VZ[zz]
    vec_out[...] = total
    z_collect(0, 1)
    spread_all(0, 1, "start")

    for step in range(1, g.fsdp):
        vec_copy(step).wait_send()
    finish_sends()
    for r in range(8):

        @pl.when(me != r)
        def _():
            vg_copy(r).wait_send()

    for d in range(1, NZ):
        vz_copy(d).wait_send()
        for n in range(2):
            for s in range(2):
                z_send(n, s, d).wait_send()
    spread_wait()
    for n in range(2):
        for s in range(2):
            spread_all(n, s, "wait")


def kernel_path(g, *args):
    rows, lens, cots = args[0:4], args[4:8], args[8:12]
    weights = args[12:16]
    gain, bias, gate = args[16:19]
    D, FF, R, T, T0, T1, NZ = g.d, g.ff, g.rows, g.t, g.t0, g.t1, g.nz
    vec = jnp.concatenate([gain.reshape(6, R), bias.reshape(6, R), gate], axis=0)
    vec = jnp.pad(vec, ((0, 2), (0, 128 - R)))
    vmem = lambda *shape: pltpu.VMEM(shape[:-1], shape[-1])
    dma = lambda *shape: pltpu.SemaphoreType.DMA(shape)
    in_vmem = pl.BlockSpec(memory_space=pltpu.VMEM)
    in_any = pl.BlockSpec(memory_space=pl.ANY)
    in_smem = pl.BlockSpec(memory_space=pltpu.SMEM)
    row_shapes = [jax.ShapeDtypeStruct(r.shape, BF) for r in rows]
    out_shape = row_shapes * 2 + [
        jax.ShapeDtypeStruct((2, 8, R, D), BF),
        jax.ShapeDtypeStruct((2, R, FF), BF),
        jax.ShapeDtypeStruct((2, 4 * R, D), BF),
        jax.ShapeDtypeStruct((16, D), F32),
        jax.ShapeDtypeStruct((8, T, D), BF),
        jax.ShapeDtypeStruct((8, T, D), BF),
        jax.ShapeDtypeStruct((8, T, 2 * D), BF),
        jax.ShapeDtypeStruct((8, T, D), BF),
    ]
    scratch = [
        vmem(2, 16, D, D, BF),
        vmem(g.fsdp, 16, 128, BF),
        vmem(16, D, F32),
        vmem(14, T, D, BF),
        vmem(T, FF, BF),
        vmem(T, FF, BF),
        vmem(3, T, D, BF),
        vmem(3, T, D, BF),
        vmem(T, D, BF),
        vmem(T, D, F32),
        vmem(T, D, F32),
        vmem(T, D, F32),
        vmem(3, T, D, F32),
        vmem(3, T, 1, F32),
        vmem(T, FF, F32),
        vmem(HEADS, T0, T1, F32),
        vmem(HEADS, T1, T0, F32),
        vmem(HEADS, T0, T0, F32),
        vmem(HEADS, T1, T1, F32),
        vmem(2, 2, NZ - 1, D // NZ, D, BF),
        vmem(2, 2, D // NZ, D, BF),
        vmem(16, D, F32),
        vmem(8, 16, D, F32),
        vmem(NZ, 16, D, F32),
        dma(33),
        dma(g.fsdp - 1),
        dma(g.fsdp - 1),
        dma(32, NZ - 1),
        dma(32, NZ - 1),
        dma(32, NZ),
        dma(32, NZ),
        dma(32, 2 * NZ),
        dma(32, 2 * NZ),
        dma(32, 2 * NZ),
        dma(32, 2 * NZ),
        dma(14, 8),
        dma(14, 8),
        dma(18),
        dma(40),
        dma(2, 2, NZ - 1),
        dma(2, 2, NZ - 1),
        dma(4, 8),
        dma(4, 8),
        dma(8),
        dma(8),
        dma(NZ - 1),
        dma(NZ - 1),
    ]
    results = pl.pallas_call(
        partial(layer_kernel, g),
        out_shape=out_shape,
        in_specs=[in_smem] * 4 + [in_vmem] * 8 + [in_any] * 5,
        out_specs=[in_vmem] * 8 + [in_any] * 3 + [in_vmem] + [in_any] * 4,
        scratch_shapes=scratch,
        compiler_params=pltpu.CompilerParams(
            collective_id=0, has_side_effects=True, vmem_limit_bytes=67043328
        ),
        name="layer",
    )(*lens, *rows, *cots, *weights, vec)
    ga, gu, gd, vectors = results[8:12]
    ga = ga.astype(F32)
    own = lax.dynamic_slice(vectors, (0, lax.axis_index("fsdp") * R), (16, R))
    return (
        *results[:8],
        ga[:, :6],
        ga[:, 6:],
        gu.astype(F32),
        gd.astype(F32),
        own[0:6].reshape(2, 3, R),
        own[6:12].reshape(2, 3, R),
        own[12:14],
    )


def solution(mesh):
    def per_device(*args):
        g = Geometry(mesh, [a.shape for a in args])
        return kernel_path(g, *args) if g.fits() else plain_path(*args)

    in_specs = (
        P(("dp", "fsdp"), None, None),
        P(("dp", "fsdp"), None, None),
        P(("dp", "fsdp"), None, None),
        P(("dp", "fsdp"), None, None),
        P(("dp", "fsdp")),
        P(("dp", "fsdp")),
        P(("dp", "fsdp")),
        P(("dp", "fsdp")),
        P(("dp", "fsdp"), None, None),
        P(("dp", "fsdp"), None, None),
        P(("dp", "fsdp"), None, None),
        P(("dp", "fsdp"), None, None),
        P(None, None, "fsdp", None),
        P(None, None, "fsdp", None),
        P(None, "fsdp", None),
        P(None, "fsdp", None),
        P(None, None, "fsdp"),
        P(None, None, "fsdp"),
        P(None, "fsdp"),
    )
    out_specs = (
        P(("dp", "fsdp"), None, None),
        P(("dp", "fsdp"), None, None),
        P(("dp", "fsdp"), None, None),
        P(("dp", "fsdp"), None, None),
        P(("dp", "fsdp"), None, None),
        P(("dp", "fsdp"), None, None),
        P(("dp", "fsdp"), None, None),
        P(("dp", "fsdp"), None, None),
        P(None, None, "fsdp", None),
        P(None, None, "fsdp", None),
        P(None, "fsdp", None),
        P(None, "fsdp", None),
        P(None, None, "fsdp"),
        P(None, None, "fsdp"),
        P(None, "fsdp"),
    )
    return jax.shard_map(
        per_device, mesh=mesh, in_specs=in_specs, out_specs=out_specs, check_vma=False
    )
```

```python
from functools import partial
import math

import jax
import jax.numpy as jnp
from jax import lax
from jax.experimental import pallas as pl
from jax.experimental.pallas import tpu as pltpu
from jax.sharding import PartitionSpec as P

HEADS = 12
BF = jnp.bfloat16
F32 = jnp.float32
MESH_ID = pl.DeviceIdType.MESH
NEG = -1000000000.0


def dot(a, b):
    return lax.dot_general(a, b, (((1,), (0,)), ((), ())), preferred_element_type=F32)


def dot_rt(a, b):
    return lax.dot_general(a, b, (((1,), (1,)), ((), ())), preferred_element_type=F32)


def dot_lt(a, b):
    return lax.dot_general(a, b, (((0,), (0,)), ((), ())), preferred_element_type=F32)


def loop(count, body):
    def step(index, carry):
        body(index)
        return carry

    lax.fori_loop(0, count, step, 0)


def cols(index, size):
    return pl.ds(pl.multiple_of(index * size, size), size)


def erf_of(value):
    x = jnp.minimum(jnp.maximum(value, -3.832506856900711), 3.832506856900711)
    y = x * x
    top = jnp.full_like(y, 0.00022905065861350646)
    for c in (0.0034082910107109506, 0.050955695062380861, 0.18520832239976145, 1.128379143519084):
        top = top * y + c
    low = jnp.full_like(y, -1.1791602954361697e-7)
    for c in (
        0.000023547966471313185,
        0.0010179625278914885,
        0.014070470171167667,
        0.11098505178285362,
        0.49746925110067538,
        1.0,
    ):
        low = low * y + c
    return x * top / low


def project(rows, matrix):
    return jnp.einsum("pld,de->ple", rows, matrix, preferred_element_type=jnp.float32)


def project_back(grads, matrix):
    return jnp.einsum("ple,de->pld", grads, matrix, preferred_element_type=jnp.float32)


def weight_grad(rows, grads):
    return jnp.einsum("pld,ple->de", rows, grads, preferred_element_type=jnp.float32)


def layer_norm(resid, gain_row, bias_row):
    centre = resid - jnp.mean(resid, axis=-1, keepdims=True)
    spread = jnp.mean(centre * centre, axis=-1, keepdims=True)
    return centre * lax.rsqrt(spread + 1e-05) * gain_row + bias_row


def gate_tail(resid, gain_row, bias_row, gate_row, row_mask):
    hidden_three = layer_norm(resid, gain_row, bias_row)
    logit = jnp.einsum("pld,d->pl", hidden_three, gate_row, precision=lax.Precision.HIGHEST)
    return hidden_three * (jax.nn.sigmoid(logit) * row_mask)[..., None]


def exact_gelu(upward):
    return jax.nn.gelu(upward, approximate=False)


def split_heads(rows):
    return rows.reshape(rows.shape[0], rows.shape[1], HEADS, rows.shape[2] // HEADS)


def masked_scores(queries, key_rows, key_mask):
    score_scale = 1.0 / math.sqrt(queries.shape[2] // HEADS)
    scores = (
        jnp.einsum(
            "plhe,pmhe->phlm",
            split_heads(queries),
            split_heads(key_rows),
            preferred_element_type=jnp.float32,
        )
        * score_scale
    )
    return jnp.where(key_mask[:, None, None, :], scores, -1000000000.0)


def attend_forward(queries, key_rows, value_rows, key_mask):
    masked = masked_scores(queries, key_rows, key_mask)
    row_max = jnp.max(masked, axis=-1, keepdims=True)
    expon = jnp.exp(masked - row_max)
    row_sum = jnp.sum(expon, axis=-1, keepdims=True)
    probs = expon / row_sum
    log_total = row_max + jnp.log(row_sum)
    mixed = jnp.einsum(
        "phlm,pmhe->plhe",
        probs.astype(jnp.bfloat16),
        split_heads(value_rows),
        preferred_element_type=jnp.float32,
    )
    return (mixed.reshape(queries.shape).astype(jnp.bfloat16), log_total)


def attend_backward(queries, key_rows, value_rows, key_mask, log_total, grad_mixed):
    score_scale = 1.0 / math.sqrt(queries.shape[2] // HEADS)
    masked = masked_scores(queries, key_rows, key_mask)
    probs = jnp.where(key_mask[:, None, None, :], jnp.exp(masked - log_total), 0.0)
    grad_heads = split_heads(grad_mixed)
    grad_probs = jnp.einsum(
        "plhe,pmhe->phlm", grad_heads, split_heads(value_rows), preferred_element_type=jnp.float32
    )
    grad_scores = (
        probs * (grad_probs - jnp.sum(grad_probs * probs, axis=-1, keepdims=True))
    ).astype(jnp.bfloat16)
    grad_query = (
        jnp.einsum(
            "phlm,pmhe->plhe",
            grad_scores,
            split_heads(key_rows),
            preferred_element_type=jnp.float32,
        )
        * score_scale
    )
    grad_key = (
        jnp.einsum(
            "phlm,plhe->pmhe", grad_scores, split_heads(queries), preferred_element_type=jnp.float32
        )
        * score_scale
    )
    grad_value = jnp.einsum(
        "phlm,plhe->pmhe",
        probs.astype(jnp.bfloat16),
        grad_heads,
        preferred_element_type=jnp.float32,
    )
    return (
        grad_query.reshape(queries.shape).astype(jnp.bfloat16),
        grad_key.reshape(key_rows.shape).astype(jnp.bfloat16),
        grad_value.reshape(value_rows.shape).astype(jnp.bfloat16),
    )


def cross_forward(own_rows, other_rows, other_keys, attn_in):
    cross_query = project(own_rows, attn_in[0]).astype(jnp.bfloat16)
    cross_key = project(other_rows, attn_in[1]).astype(jnp.bfloat16)
    cross_value = project(other_rows, attn_in[2]).astype(jnp.bfloat16)
    cross_mixed, cross_total = attend_forward(cross_query, cross_key, cross_value, other_keys)
    return ((cross_query, cross_key, cross_value), cross_mixed, cross_total)


def stream_forward(own_rows, other_rows, own_keys, other_keys, row_mask, params):
    attn_in, attn_out, ffn_up, ffn_down, gains, biases, gate_row = params
    _, cross_mixed, _ = cross_forward(own_rows, other_rows, other_keys, attn_in)
    resid_one = own_rows.astype(jnp.float32) + project(cross_mixed, attn_out[0])
    hidden_one = layer_norm(resid_one, gains[0], biases[0])
    hidden_low = hidden_one.astype(jnp.bfloat16)
    self_query = project(hidden_low, attn_in[3]).astype(jnp.bfloat16)
    self_key = project(hidden_low, attn_in[4]).astype(jnp.bfloat16)
    self_value = project(hidden_low, attn_in[5]).astype(jnp.bfloat16)
    self_mixed, self_total = attend_forward(self_query, self_key, self_value, own_keys)
    resid_two = hidden_one + project(self_mixed, attn_out[1])
    hidden_two = layer_norm(resid_two, gains[1], biases[1])
    ffn_in = hidden_two.astype(jnp.bfloat16)
    upward = project(ffn_in, ffn_up)
    active = exact_gelu(upward).astype(jnp.bfloat16)
    resid_three = hidden_two + project(active, ffn_down)
    output = gate_tail(resid_three, gains[2], biases[2], gate_row, row_mask)
    saved_rows = (
        resid_one,
        hidden_low,
        self_query,
        self_key,
        self_value,
        self_total,
        self_mixed,
        resid_two,
        ffn_in,
        upward,
        active,
        resid_three,
    )
    return (output, saved_rows)


def stream_backward(
    own_rows, other_rows, own_keys, other_keys, row_mask, params, saved_rows, grad_out
):
    attn_in, attn_out, ffn_up, ffn_down, gains, biases, gate_row = params
    (
        resid_one,
        hidden_low,
        self_query,
        self_key,
        self_value,
        self_total,
        self_mixed,
        resid_two,
        ffn_in,
        upward,
        active,
        resid_three,
    ) = saved_rows
    _, tail_pull = jax.vjp(
        partial(gate_tail, row_mask=row_mask), resid_three, gains[2], biases[2], gate_row
    )
    grad_three, gain_three, bias_three, grad_gate = tail_pull(grad_out)
    grad_down_in = grad_three.astype(jnp.bfloat16)
    down_grad = weight_grad(active, grad_down_in)
    grad_active = project_back(grad_down_in, ffn_down)
    _, gelu_pull = jax.vjp(exact_gelu, upward)
    grad_upward = gelu_pull(grad_active)[0].astype(jnp.bfloat16)
    up_grad = weight_grad(ffn_in, grad_upward)
    grad_two = grad_three + project_back(grad_upward, ffn_up)
    _, norm_two_pull = jax.vjp(layer_norm, resid_two, gains[1], biases[1])
    grad_resid_two, gain_two, bias_two = norm_two_pull(grad_two)
    grad_self_out = grad_resid_two.astype(jnp.bfloat16)
    self_out_grad = weight_grad(self_mixed, grad_self_out)
    grad_self_mixed = project_back(grad_self_out, attn_out[1]).astype(jnp.bfloat16)
    grad_self_query, grad_self_key, grad_self_value = attend_backward(
        self_query, self_key, self_value, own_keys, self_total, grad_self_mixed
    )
    grad_one = (
        grad_resid_two
        + project_back(grad_self_query, attn_in[3])
        + project_back(grad_self_key, attn_in[4])
        + project_back(grad_self_value, attn_in[5])
    )
    _, norm_one_pull = jax.vjp(layer_norm, resid_one, gains[0], biases[0])
    grad_resid_one, gain_one, bias_one = norm_one_pull(grad_one)
    grad_cross_out = grad_resid_one.astype(jnp.bfloat16)
    (cross_query, cross_key, cross_value), cross_mixed, cross_total = cross_forward(
        own_rows, other_rows, other_keys, attn_in
    )
    cross_out_grad = weight_grad(cross_mixed, grad_cross_out)
    grad_cross_mixed = project_back(grad_cross_out, attn_out[0]).astype(jnp.bfloat16)
    grad_cross_query, grad_cross_key, grad_cross_value = attend_backward(
        cross_query, cross_key, cross_value, other_keys, cross_total, grad_cross_mixed
    )
    grad_own = grad_resid_one + project_back(grad_cross_query, attn_in[0])
    grad_other = project_back(grad_cross_key, attn_in[1]) + project_back(
        grad_cross_value, attn_in[2]
    )
    in_grads = jnp.stack(
        [
            weight_grad(own_rows, grad_cross_query),
            weight_grad(other_rows, grad_cross_key),
            weight_grad(other_rows, grad_cross_value),
            weight_grad(hidden_low, grad_self_query),
            weight_grad(hidden_low, grad_self_key),
            weight_grad(hidden_low, grad_self_value),
        ]
    )
    out_grads = jnp.stack([cross_out_grad, self_out_grad])
    gain_grads = jnp.stack([gain_one, gain_two, gain_three])
    bias_grads = jnp.stack([bias_one, bias_two, bias_three])
    return (
        grad_own,
        grad_other,
        (in_grads, out_grads, up_grad, down_grad, gain_grads, bias_grads, grad_gate),
    )


def stream_params(gathered, stream):
    return (
        gathered[0][stream],
        gathered[1][stream],
        gathered[2][stream],
        gathered[3][stream],
        gathered[4][stream].astype(jnp.float32),
        gathered[5][stream].astype(jnp.float32),
        gathered[6][stream].astype(jnp.float32),
    )


def plain_path(
    text_a,
    visual_a,
    text_b,
    visual_b,
    text_len_a,
    visual_len_a,
    text_len_b,
    visual_len_b,
    cot_text_a,
    cot_visual_a,
    cot_text_b,
    cot_visual_b,
    attn_in,
    attn_out,
    ffn_up,
    ffn_down,
    norm_gain,
    norm_bias,
    gate_vector,
):
    gathered = (
        lax.all_gather(attn_in, "fsdp", axis=2, tiled=True),
        lax.all_gather(attn_out, "fsdp", axis=2, tiled=True),
        lax.all_gather(ffn_up, "fsdp", axis=1, tiled=True),
        lax.all_gather(ffn_down, "fsdp", axis=1, tiled=True),
        lax.all_gather(norm_gain, "fsdp", axis=2, tiled=True),
        lax.all_gather(norm_bias, "fsdp", axis=2, tiled=True),
        lax.all_gather(gate_vector, "fsdp", axis=1, tiled=True),
    )
    layouts = []
    for rows_text, rows_visual, len_text, len_visual, cot_text, cot_visual in (
        (text_a, visual_a, text_len_a, visual_len_a, cot_text_a, cot_visual_a),
        (text_b, visual_b, text_len_b, visual_len_b, cot_text_b, cot_visual_b),
    ):
        keys_text = jnp.arange(rows_text.shape[1], dtype=jnp.int32)[None, :] < len_text[:, None]
        keys_visual = (
            jnp.arange(rows_visual.shape[1], dtype=jnp.int32)[None, :] < len_visual[:, None]
        )
        stream_rows = (rows_text, rows_visual)
        stream_keys = (keys_text, keys_visual)
        stream_masks = (keys_text.astype(jnp.float32), keys_visual.astype(jnp.float32))
        outputs = []
        saved_list = []
        for stream in (0, 1):
            other_side = 1 - stream
            output, saved_rows = stream_forward(
                stream_rows[stream],
                stream_rows[other_side],
                stream_keys[stream],
                stream_keys[other_side],
                stream_masks[stream],
                stream_params(gathered, stream),
            )
            outputs.append(output.astype(jnp.bfloat16))
            saved_list.append(saved_rows)
        layouts.append(
            (stream_rows, stream_keys, stream_masks, (cot_text, cot_visual), outputs, saved_list)
        )
    back_weights = gathered
    input_grads = [[None, None], [None, None]]
    stream_grads = []
    for stream in (0, 1):
        other_side = 1 - stream
        params = stream_params(back_weights, stream)
        summed = None
        for layout_index in (0, 1):
            stream_rows, stream_keys, stream_masks, cotangents, outputs, saved_list = layouts[
                layout_index
            ]
            grad_own, grad_other, grads_here = stream_backward(
                stream_rows[stream],
                stream_rows[other_side],
                stream_keys[stream],
                stream_keys[other_side],
                stream_masks[stream],
                params,
                saved_list[stream],
                cotangents[stream].astype(jnp.float32),
            )
            for target, piece in ((stream, grad_own), (other_side, grad_other)):
                if input_grads[layout_index][target] is None:
                    input_grads[layout_index][target] = piece
                else:
                    input_grads[layout_index][target] = input_grads[layout_index][target] + piece
            if summed is None:
                summed = grads_here
            else:
                summed = tuple((left + right for left, right in zip(summed, grads_here)))
        stream_grads.append(summed)
    text_grads = stream_grads[0]
    visual_grads = stream_grads[1]
    row_dims = (1, 1, 0, 0, 1, 1, 0)
    packed = tuple(
        (
            jnp.concatenate([text_grads[index], visual_grads[index]], axis=row_dims[index])
            for index in range(7)
        )
    )
    shares = (
        lax.psum_scatter(packed[0], ("dp", "fsdp"), scatter_dimension=1, tiled=True),
        lax.psum_scatter(packed[1], ("dp", "fsdp"), scatter_dimension=1, tiled=True),
        lax.psum_scatter(packed[2], ("dp", "fsdp"), scatter_dimension=0, tiled=True),
        lax.psum_scatter(packed[3], ("dp", "fsdp"), scatter_dimension=0, tiled=True),
        lax.psum_scatter(packed[4], ("dp", "fsdp"), scatter_dimension=1, tiled=True),
        lax.psum_scatter(packed[5], ("dp", "fsdp"), scatter_dimension=1, tiled=True),
        lax.psum_scatter(packed[6], ("dp", "fsdp"), scatter_dimension=0, tiled=True),
    )
    joined = (
        lax.all_gather(shares[0].astype(jnp.bfloat16), "dp", axis=1, tiled=True).astype(
            jnp.float32
        ),
        lax.all_gather(shares[1].astype(jnp.bfloat16), "dp", axis=1, tiled=True).astype(
            jnp.float32
        ),
        lax.all_gather(shares[2].astype(jnp.bfloat16), "dp", axis=0, tiled=True).astype(
            jnp.float32
        ),
        lax.all_gather(shares[3].astype(jnp.bfloat16), "dp", axis=0, tiled=True).astype(
            jnp.float32
        ),
        lax.all_gather(shares[4].astype(jnp.bfloat16), "dp", axis=1, tiled=True).astype(
            jnp.float32
        ),
        lax.all_gather(shares[5].astype(jnp.bfloat16), "dp", axis=1, tiled=True).astype(
            jnp.float32
        ),
        lax.all_gather(shares[6].astype(jnp.bfloat16), "dp", axis=0, tiled=True).astype(
            jnp.float32
        ),
    )
    finals = tuple(
        (jnp.stack(jnp.split(joined[index], 2, axis=row_dims[index])) for index in range(7))
    )
    first_outputs = layouts[0][4]
    second_outputs = layouts[1][4]
    return (
        first_outputs[0],
        first_outputs[1],
        second_outputs[0],
        second_outputs[1],
        input_grads[0][0].astype(jnp.bfloat16),
        input_grads[0][1].astype(jnp.bfloat16),
        input_grads[1][0].astype(jnp.bfloat16),
        input_grads[1][1].astype(jnp.bfloat16),
        finals[0],
        finals[1],
        finals[2],
        finals[3],
        finals[4],
        finals[5],
        finals[6],
    )


class Geometry:
    def __init__(self, mesh, shapes):
        self.dp = mesh.shape["dp"]
        self.fsdp = mesh.shape["fsdp"]
        (self.la, self.lva), (self.lb, self.lvb) = (
            (shapes[0][1], shapes[1][1]),
            (shapes[2][1], shapes[3][1]),
        )
        self.d = shapes[0][2]
        self.rows = self.d // self.fsdp
        self.ff = shapes[14][2]
        self.pages = shapes[0][0]
        self.t0 = -(-(self.la + self.lb) // 16) * 16
        self.t1 = -(-(self.lva + self.lvb) // 16) * 16
        self.t = self.t0 + self.t1
        self.nz = self.fsdp // 4

    def fits(self):
        return (
            self.dp == 2
            and self.fsdp == 16
            and self.pages == 1
            and self.d == 16 * 48
            and self.ff == 4 * self.d
            and self.t0 >= self.t1
            and self.d == 64 * HEADS
        )


def layer_kernel(g, *refs):
    D, FF, R, T0, T1, T, NZ = g.d, g.ff, g.rows, g.t0, g.t1, g.t, g.nz
    ZR = D // NZ
    it = iter(refs)
    take = lambda n: [next(it) for _ in range(n)]
    lens = take(4)
    rows_in = take(4)
    cots_in = take(4)
    w_parts = take(4)
    (vec_in,) = take(1)
    outs = take(4)
    grads = take(4)
    ga, gu, gd, vec_out = take(4)
    ra, rg, rfa, rfg = take(4)
    W, VEC, vecs = take(3)
    S, A, DU, CQ, SQ, DO = take(6)
    RES, HID, DR, XH, RSTD, GP = take(6)
    p_refs = take(4)
    RZ, FB, VG, VR, VZ = take(5)
    (s_loc, s_vec, r_vec, sz, rz, sy, ry, sx, rx, sc, rc) = take(11)
    (s_ex, r_ex, s_own, s_st, s_zr, r_zr, s_rd, r_rd, s_vg, r_vg, s_vz, r_vz) = take(12)

    X, H1, OC, OS, H2 = 0, 1, 2, 3, 4
    DQC, DKC, DVC, DQS, DKS, DVS, DC, DS, DF = range(5, 14)
    span = (slice(0, T0), slice(T0, T))
    size = (T0, T1)

    x = lax.axis_index("dp")
    f = lax.axis_index("fsdp")
    z, y, c = f // 4, (f // 2) % 2, f % 2
    me = c * 4 + x * 2 + y

    def device(xx, zz, yy, cc):
        return (xx, zz * 4 + yy * 2 + cc)

    def role_device(r):
        return device((r // 2) % 2, z, r % 2, r // 4)

    def remote(src, dst, send, recv, dev):
        return pltpu.make_async_remote_copy(
            src_ref=src, dst_ref=dst, send_sem=send, recv_sem=recv, device_id=dev,
            device_id_type=MESH_ID,
        )

    barrier = pltpu.get_barrier_semaphore()
    for step in range(1, g.fsdp):
        pl.semaphore_signal(
            barrier, inc=1, device_id=(x, (f + step) % g.fsdp), device_id_type=MESH_ID
        )
    for r in range(4):
        pl.semaphore_signal(
            barrier, inc=1, device_id=device(1 - x, z, r // 2, r % 2), device_id_type=MESH_ID
        )
    pl.semaphore_wait(barrier, g.fsdp + 3)

    def wref(k, ff, r0, n):
        kk = k % 16
        down = kk // 12
        unit = kk + down * (12 + (4 * R * ff) // D - kk)
        row = R * ff + down * ((4 * R * ff) % D + R * (kk - 12) - R * ff) + r0
        return W.at[k // 16, unit, pl.ds(pl.multiple_of(row, 16), n)]

    def local_part(k):
        w_in, w_out, w_up, w_dn = w_parts
        s, k = k // 16, k % 16
        if k in (3, 7):
            return w_out.at[s, (k - 3) // 4]
        if k < 8:
            return w_in.at[s, (0, 1, 2, None, 3, 4, 5)[k]]
        if k < 12:
            return w_up.at[s, :, pl.ds(D * (k - 8), D)]
        return w_dn.at[s, pl.ds(R * (k - 12), R)]

    third = R // 3
    NK = 32
    AHEAD = 2
    GAP = 2
    LAG = AHEAD + (NZ + 1) * GAP
    for k in range(NK):
        cp = pltpu.make_async_copy(local_part(k), wref(k, f, 0, R), s_loc.at[k])
        cp.start()

    def vec_copy(step):
        return remote(
            vec_in, VEC.at[f], s_vec.at[step - 1], r_vec.at[step - 1],
            (x, (f + step) % g.fsdp),
        )

    def vec_wait(step):
        ref = VEC.at[(f + g.fsdp - step) % g.fsdp]
        remote(ref, ref, s_vec.at[step - 1], r_vec.at[step - 1], (x, f)).wait_recv()

    for step in range(1, g.fsdp):
        vec_copy(step).start()
    own_vec = pltpu.make_async_copy(vec_in, VEC.at[f], s_loc.at[NK])
    own_vec.start()

    def shard(zz, yy):
        return zz * 4 + yy * 2 + c

    def z_relay(k, way, dist):
        up = way == 0
        ref = wref(k, shard(z - dist if up else z + dist, y), third * x, 2 * third)
        lands = dist + 1 if up else NZ - 1 - dist
        return remote(
            ref, ref, sz.at[k, way, dist], rz.at[k, lands - 1],
            device(x, z + 1 if up else z - 1, y, c),
        )

    def z_wait(k, d):
        ref = wref(k, shard((z + NZ - d) % NZ, y), third * x, 2 * third)
        remote(ref, ref, sz.at[k, 0, 0], rz.at[k, d - 1], device(x, z, 1 - y, c)).wait_recv()

    def z_relay_when(way, dist):
        return (z >= dist) & (z + 1 < NZ) if way == 0 else (z + dist < NZ) & (z >= 1)

    def y_copy(k, d):
        ref = wref(k, shard((z + NZ - d) % NZ, y), third * x, 2 * third)
        return remote(ref, ref, sy.at[k, d], ry.at[k, d], device(x, z, 1 - y, c))

    def y_wait(k, d):
        ref = wref(k, shard((z + NZ - d) % NZ, 1 - y), third * x, 2 * third)
        remote(ref, ref, sy.at[k, d], ry.at[k, d], device(x, z, 1 - y, c)).wait_recv()

    def x_copy(k, d, e):
        ref = wref(k, shard((z + NZ - d) % NZ, (y + e) % 2), 2 * third * x, third)
        return remote(ref, ref, sx.at[k, 2 * d + e], rx.at[k, 2 * d + e], device(1 - x, z, y, c))

    def x_wait(k, d, e):
        ref = wref(k, shard((z + NZ - d) % NZ, (y + e) % 2), 2 * third * (1 - x), third)
        remote(ref, ref, sx.at[k, 2 * d + e], rx.at[k, 2 * d + e], device(1 - x, z, y, c)).wait_recv()

    def c_copy(k, d, e):
        ref = wref(k, shard((z + NZ - d) % NZ, (y + e) % 2), 0, R)
        return remote(ref, ref, sc.at[k, 2 * d + e], rc.at[k, 2 * d + e], device(x, z, y, 1 - c))

    def c_wait(k, d, e):
        other = ((z + NZ - d) % NZ) * 4 + ((y + e) % 2) * 2 + 1 - c
        ref = wref(k, other, 0, R)
        remote(ref, ref, sc.at[k, 2 * d + e], rc.at[k, 2 * d + e], device(x, z, y, 1 - c)).wait_recv()

    def own_start(k):
        ref = wref(k, f, 0, R)
        pltpu.make_async_copy(ref, ref, s_loc.at[k]).wait()
        for way in range(2):

            @pl.when(z_relay_when(way, 0))
            def _():
                z_relay(k, way, 0).start()

        y_copy(k, 0).start()
        c_copy(k, 0, 0).start()

    def z_stage(k, dist):
        for way in range(2):
            d = dist if way == 0 else NZ - dist

            @pl.when(z >= dist if way == 0 else z + dist < NZ)
            def _():
                z_wait(k, d)

                @pl.when((dist < NZ - 1) & (z + 1 < NZ if way == 0 else z >= 1))
                def _():
                    z_relay(k, way, dist).start()

                y_copy(k, d).start()
                x_copy(k, d, 0).start()

    def y_stage(k):
        def one(d):
            y_wait(k, d)
            x_copy(k, d, 1).start()

        loop(NZ, one)

    def x_stage(k):
        def one(i):
            d, e = (i + 1) % NZ, (i + 1) // NZ
            x_wait(k, d, e)
            c_copy(k, d, e).start()

        loop(2 * NZ - 1, one)

    def c_stage(k):
        loop(2 * NZ, lambda i: c_wait(k, i % NZ, i // NZ))

    def gather_step(t):
        def at(k, act):
            @pl.when((k >= 0) & (k < NK))
            def _():
                act(k)

        at(t, own_start)
        loop(
            NZ - 1,
            lambda i: at(t - AHEAD - i * GAP, lambda k: z_stage(k, i + 1)),
        )
        at(t - AHEAD - (NZ - 1) * GAP, y_stage)
        at(t - AHEAD - NZ * GAP, x_stage)
        at(t - LAG, c_stage)

    def gather_steps(lo, hi):
        def step(t, carry):
            gather_step(t)
            return carry

        lax.fori_loop(lo, hi, step, 0)

    gather_steps(0, 2)
    reached = [2]

    la, lva = g.la, g.lva

    def assemble(dst, parts):
        ta, va, tb, vb = parts
        dst[0:la] = ta[0].astype(F32)
        dst[la : la + g.lb] = tb[0].astype(F32)
        if T0 > la + g.lb:
            dst[la + g.lb : T0] = jnp.zeros((T0 - la - g.lb, D), F32)
        dst[T0 : T0 + lva] = va[0].astype(F32)
        dst[T0 + lva : T0 + lva + g.lvb] = vb[0].astype(F32)
        if T1 > lva + g.lvb:
            dst[T0 + lva + g.lvb : T] = jnp.zeros((T1 - lva - g.lvb, D), F32)

    assemble(HID, rows_in)
    S[X] = HID[...].astype(BF)
    assemble(DR, cots_in)

    def live(index, s):
        first, second = (la, g.lb) if s == 0 else (lva, g.lvb)
        na, nb = lens[s][0], lens[2 + s][0]
        return ((index < first) & (index < na)) | (
            (index >= first) & (index - first < nb) & (index - first < second)
        )

    def key_mask(qs, ks):
        shape = (size[qs], size[ks])
        qi = lax.broadcasted_iota(jnp.int32, shape, 0)
        ki = lax.broadcasted_iota(jnp.int32, shape, 1)
        q_first = la if qs == 0 else lva
        k_first = la if ks == 0 else lva
        same = ((qi < q_first) & (ki < k_first)) | ((qi >= q_first) & (ki >= k_first))
        return same & live(ki, ks)

    UA = (0, 1, 2, 4, 5, 6)
    UB = (3, 7)

    def wtile(s, u, i):
        return W[s, u, :, cols(i, 256)]

    def wrows(s, u, i):
        return W[s, u, cols(i, 256), :]

    NT = D // 256

    def cross_project(s):
        own, other = span[s], span[1 - s]

        def q_tile(i):
            CQ[0, own, cols(i, 256)] = dot(S[X, own], wtile(s, 0, i)).astype(BF)

        loop(NT, q_tile)

        def kv_tile(i):
            m = 1 + i // NT
            j = i % NT
            CQ[m, other, cols(j, 256)] = dot(S[X, other], wtile(s, m, j)).astype(BF)

        loop(2 * NT, kv_tile)

    def self_project(s):
        own = span[s]

        def tile(i):
            m = i // NT
            j = i % NT
            SQ[m, own, cols(j, 256)] = dot(S[H1, own], wtile(s, 4 + m, j)).astype(BF)

        loop(3 * NT, tile)

    def attend(src, base, s, ks, p_ref, o_index):
        own, keys = span[s], span[ks]

        def pair(p):
            lanes = cols(p, 128)
            mask = key_mask(s, ks)
            q, k, v = src[base, own, lanes], src[base + 1, keys, lanes], src[base + 2, keys, lanes]
            low = lax.broadcasted_iota(jnp.int32, q.shape, 1) < 64
            high = lax.broadcasted_iota(jnp.int32, q.shape, 1) >= 64
            mixed = []
            for half in range(2):
                qh = jnp.where(low if half == 0 else high, q, jnp.zeros_like(q))
                scores = jnp.where(mask, dot_rt(qh, k) * 0.125, NEG)
                top = jnp.max(scores, axis=-1, keepdims=True)
                expon = jnp.exp(scores - top)
                probs = expon / jnp.sum(expon, axis=-1, keepdims=True)
                p_ref[2 * p + half] = probs
                mixed.append(dot(probs.astype(BF), v))
            S[o_index, own, lanes] = jnp.where(low, mixed[0], mixed[1]).astype(BF)

        loop(HEADS // 2, pair)

    def attend_back(src, base, s, ks, p_ref, gq, gk, gv):
        own, keys = span[s], span[ks]

        def pair(p):
            lanes = cols(p, 128)
            q, k, v = src[base, own, lanes], src[base + 1, keys, lanes], src[base + 2, keys, lanes]
            do = DO[own, lanes]
            low_q = lax.broadcasted_iota(jnp.int32, q.shape, 1) < 64
            high_q = lax.broadcasted_iota(jnp.int32, q.shape, 1) >= 64
            low_k = lax.broadcasted_iota(jnp.int32, k.shape, 1) < 64
            dq, dk, dv = [], [], []
            for half in range(2):
                doh = jnp.where(low_q if half == 0 else high_q, do, jnp.zeros_like(do))
                probs = p_ref[2 * p + half]
                dp = dot_rt(doh, v)
                ds = (probs * (dp - jnp.sum(dp * probs, axis=-1, keepdims=True))).astype(BF)
                dq.append(dot(ds, k))
                dk.append(dot_lt(ds, q))
                dv.append(dot_lt(probs.astype(BF), do))
            S[gq, own, lanes] = (jnp.where(low_q, dq[0], dq[1]) * 0.125).astype(BF)
            S[gk, keys, lanes] = (jnp.where(low_k, dk[0], dk[1]) * 0.125).astype(BF)
            S[gv, keys, lanes] = jnp.where(low_k, dv[0], dv[1]).astype(BF)

        loop(HEADS // 2, pair)

    def out_project(o_index, which, s):
        own = span[s]

        def tile(i):
            RES[own, cols(i, 256)] = HID[own, cols(i, 256)] + dot(
                S[o_index, own], wtile(s, UB[which], i)
            )

        loop(NT, tile)

    RB = 16
    mean = lambda v: jnp.sum(v, axis=-1, keepdims=True) * (1.0 / D)

    def normalize(i, r):
        resid = RES[r]
        centre = resid - mean(resid)
        rstd = lax.rsqrt(mean(centre * centre) + 1e-05)
        return centre * rstd, rstd

    def rows_of(s, b):
        return pl.ds(pl.multiple_of((0, T0)[s] + b * RB, RB), RB)

    def norm_forward(i, h_index, s):
        def block(b):
            r = rows_of(s, b)
            xh, rstd = normalize(i, r)
            XH[i, r] = xh
            RSTD[i, r] = rstd
            hidden = xh * vecs[pl.ds(s * 3 + i, 1), :] + vecs[pl.ds(6 + s * 3 + i, 1), :]
            HID[r] = hidden
            S[h_index, r] = hidden.astype(BF)

        loop(size[s] // RB, block)

    def add_row(row, value):
        VG[pl.ds(row, 1), :] += jnp.sum(value, axis=0, keepdims=True)

    def norm_pull(i, s, r, dh, xh, rstd):
        add_row(s * 3 + i, dh * xh)
        add_row(6 + s * 3 + i, dh)
        dx = dh * vecs[pl.ds(s * 3 + i, 1), :]
        return rstd * (dx - mean(dx) - xh * mean(dx * xh))

    def norm_backward(i, g_index, s):
        def block(b):
            r = rows_of(s, b)
            dr = norm_pull(i, s, r, DR[r], XH[i, r], RSTD[i, r])
            DR[r] = dr
            S[g_index, r] = dr.astype(BF)

        loop(size[s] // RB, block)

    def tail(s):
        def block(b):
            r = rows_of(s, b)
            xh, rstd = normalize(2, r)
            gain = vecs[pl.ds(s * 3 + 2, 1), :]
            h3 = xh * gain + vecs[pl.ds(6 + s * 3 + 2, 1), :]
            gate = vecs[pl.ds(12 + s, 1), :]
            logit = jnp.sum(h3 * gate, axis=-1, keepdims=True)
            sig = 1.0 / (1.0 + jnp.exp(-logit))
            index = lax.broadcasted_iota(jnp.int32, (RB, 1), 0) + b * RB
            mask = jnp.where(live(index, s), 1.0, 0.0)
            weight = sig * mask
            HID[r] = h3 * weight
            dout = DR[r]
            dlogit = jnp.sum(dout * h3, axis=-1, keepdims=True) * weight * (1.0 - sig)
            add_row(12 + s, h3 * dlogit)
            dr = norm_pull(2, s, r, dout * weight + dlogit * gate, xh, rstd)
            DR[r] = dr
            S[DF, r] = dr.astype(BF)

        loop(size[s] // RB, block)
        o_ta, o_va, o_tb, o_vb = outs
        if s == 0:
            o_ta[0] = HID[0:la].astype(BF)
            o_tb[0] = HID[la : la + g.lb].astype(BF)
        else:
            o_va[0] = HID[T0 : T0 + lva].astype(BF)
            o_vb[0] = HID[T0 + lva : T0 + lva + g.lvb].astype(BF)

    def ffn_up(q, s):
        own = span[s]

        def tile(i):
            j = q * NT + i
            u = dot(S[H2, own], wtile(s, 8 + q, i))
            cdf = 0.5 + 0.5 * erf_of(u * 0.7071067811865476)
            A[own, cols(j, 256)] = (u * cdf).astype(BF)
            GP[own, cols(j, 256)] = cdf + u * (
                jnp.exp(u * u * -0.5) * 0.3989422804014327
            )

        loop(NT, tile)

    def ffn_down(s):
        own = span[s]

        def tile(i):
            total = HID[own, cols(i, 256)]
            for q in range(4):
                total = total + dot(A[own, D * q : D * q + D], wtile(s, 12 + q, i))
            RES[own, cols(i, 256)] = total

        loop(NT, tile)

    def ffn_down_back(s):
        own = span[s]

        def tile(j):
            da = dot_rt(S[DF, own], wrows(s, 12 + j // NT, j % NT))
            DU[own, cols(j, 256)] = (GP[own, cols(j, 256)] * da).astype(BF)

        loop(4 * NT, tile)

    def ffn_up_back(s):
        own = span[s]

        def tile(i):
            total = DR[own, cols(i, 256)]
            for q in range(4):
                total = total + dot_rt(DU[own, D * q : D * q + D], wrows(s, 8 + q, i))
            DR[own, cols(i, 256)] = total

        loop(NT, tile)

    def out_back(g_index, which, s):
        own = span[s]

        def tile(i):
            DO[own, cols(i, 256)] = dot_rt(
                S[g_index, own], wrows(s, UB[which], i)
            ).astype(BF)

        loop(NT, tile)

    def self_back(s):
        own = span[s]

        def tile(i):
            total = DR[own, cols(i, 256)]
            for m, gi in enumerate((DQS, DKS, DVS)):
                total = total + dot_rt(S[gi, own], wrows(s, 4 + m, i))
            DR[own, cols(i, 256)] = total

        loop(NT, tile)

    def cross_back(s):
        own = span[s]

        def tile(i):
            total = DR[own, cols(i, 256)] + dot_rt(S[DQC, own], wrows(s, 0, i))
            total = total + dot_rt(S[DKC, own], wrows(1 - s, 1, i))
            total = total + dot_rt(S[DVC, own], wrows(1 - s, 2, i))
            DR[own, cols(i, 256)] = total

        loop(NT, tile)
        g_ta, g_va, g_tb, g_vb = grads
        if s == 0:
            g_ta[0] = DR[0:la].astype(BF)
            g_tb[0] = DR[la : la + g.lb].astype(BF)
        else:
            g_va[0] = DR[T0 : T0 + lva].astype(BF)
            g_vb[0] = DR[T0 + lva : T0 + lva + g.lvb].astype(BF)

    sends = []

    def plane_send(r, src, dst, slot):
        @pl.when(me != r)
        def _():
            remote(src, dst, s_ex.at[slot, r], r_ex.at[slot, me], role_device(r)).start()

        @pl.when(me == r)
        def _():
            pltpu.make_async_copy(src, dst, s_own.at[slot]).start()

        sends.append((r, src, dst, slot))

    def finish_sends():
        for r, src, dst, slot in sends:

            @pl.when(me != r)
            def _():
                remote(src, dst, s_ex.at[slot, r], r_ex.at[slot, me], role_device(r)).wait_send()

    def plane_wait(slot, pick):
        for p in range(8):
            ref = pick(p)

            @pl.when(me != p)
            def _():
                remote(ref, ref, s_ex.at[slot, p], r_ex.at[slot, p], role_device(p)).wait_recv()

            @pl.when(me == p)
            def _():
                pltpu.make_async_copy(ref, ref, s_own.at[slot]).wait()

    A_OF = (X, X, X, OC, H1, H1, H1, OS)
    G_OF = (DQC, DKC, DVC, DC, DQS, DKS, DVS, DS)
    HB = D // 2

    def rows_for(r, s):
        t = 1 - s if r in (1, 2) else s
        return pl.ds((0, T0)[t], size[t])

    def send_left(r, s):
        rows = rows_for(r, s)
        plane_send(r, S.at[A_OF[r], rows], ra.at[me, rows], 7 * s)

    def send_right(r, s):
        rows = rows_for(r, s)
        plane_send(r, S.at[G_OF[r], rows], rg.at[me, rows], 7 * s + 1)

    def own_rows(s):
        return pl.ds((0, T0)[s], size[s])

    def send_ffn_left(r, q, s):
        rows = own_rows(s)
        if r < 4:
            plane_send(r, S.at[H2, rows], rfa.at[me, rows, pl.ds(0, D)], 7 * s + 3)
        else:
            plane_send(
                r, A.at[rows, pl.ds(D * q + HB * (r % 2), HB)],
                rfa.at[me, rows, pl.ds(HB * q, HB)], 7 * s + 3 + q,
            )

    def send_ffn_right(r, s):
        rows = own_rows(s)
        if r < 4:
            plane_send(r, DU.at[rows, pl.ds(D * r, D)], rfg.at[me, rows], 7 * s + 2)
        else:
            hh = (r // 2) % 2
            plane_send(
                r, S.at[DF, rows, pl.ds(HB * hh, HB)], rfg.at[me, rows, pl.ds(0, HB)], 7 * s + 2
            )

    flip = (((me + 1) // 2) % 2) * (1 - me // 4)

    def stage(s, rows, n, first, blocks):
        made = []
        for src, unit, col in blocks:
            for p in range(8):
                made.append(
                    pltpu.make_async_copy(
                        src.at[p, rows, pl.ds(col, D)],
                        W.at[s, unit + p // 4, pl.ds(n * (p % 4), n)],
                        s_st.at[first + len(made)],
                    )
                )
        for cp in made:
            cp.start()
        for cp in made:
            cp.wait()

    def stacked(s, unit, n, lanes):
        return jnp.concatenate(
            [W[s, unit + p // 4, n * (p % 4) : n * (p % 4) + n, lanes] for p in range(8)], axis=0
        )

    def weight_grad(s, n, dst):
        def tile(i):
            W[s, dst, cols(i, 256), :] = dot_lt(
                stacked(s, 8, n, cols(i, 256)), stacked(s, 12, n, slice(0, D))
            ).astype(BF)

        loop(NT, tile)

    def weight_grad_down(s, n, dst):
        def tile(q):
            out = dot_lt(
                stacked(s, 8 + 2 * (q // 2), n, cols(q % 2, HB)), stacked(s, 12, n, slice(0, HB))
            ).astype(BF)
            W[s, dst, pl.ds(pl.multiple_of(q * ZR, ZR), ZR), 0:HB] = out[0:ZR]
            W[s, dst, pl.ds(pl.multiple_of(q * ZR, ZR), ZR), HB:D] = out[ZR : 2 * ZR]

        loop(4, tile)

    def z_send(n, s, d):
        zz = (z + d) % NZ
        src = W.at[s, 14 + n, pl.ds(pl.multiple_of(zz * ZR, ZR), ZR)]
        return remote(
            src, RZ.at[n, s, d - 1], s_zr.at[n, s, d - 1], r_zr.at[n, s, d - 1],
            device(x, zz, y, c),
        )

    def z_collect(n, s):
        for d in range(1, NZ):
            z_send(n, s, d).wait_recv()

        def block(i):
            total = W[s, 14 + n, pl.ds(pl.multiple_of(z * ZR + i * 16, 16), 16)].astype(F32)
            for d in range(NZ - 1):
                total = total + RZ[n, s, d, cols(i, 16)].astype(F32)
            FB[n, s, cols(i, 16)] = total.astype(BF)

        loop(ZR // 16, block)

    def ffn_share(s):
        rows, n = own_rows(s), size[s]

        @pl.when(me < 4)
        def _():
            plane_wait(7 * s + 2, lambda p: rfg.at[p, rows])
            plane_wait(7 * s + 3, lambda p: rfa.at[p, rows, pl.ds(0, D)])

        @pl.when(me >= 4)
        def _():
            plane_wait(7 * s + 2, lambda p: rfg.at[p, rows, pl.ds(0, HB)])
            for q in range(4):
                plane_wait(7 * s + 3 + q, lambda p: rfa.at[p, rows, pl.ds(HB * q, HB)])

        stage(s, rows, n, 0, ((rfg, 12, 0), (rfa, 8, 0), (rfa, 10, D)))

        @pl.when(me < 4)
        def _():
            weight_grad(s, n, 15)

        @pl.when(me >= 4)
        def _():
            weight_grad_down(s, n, 15)

        for d in range(1, NZ):
            z_send(1, s, d).start()

    def attention_share(s):
        def branch(r):
            rows, n = rows_for(r, s), size[1 - s if r in (1, 2) else s]
            plane_wait(7 * s, lambda p: ra.at[p, rows])
            plane_wait(7 * s + 1, lambda p: rg.at[p, rows])
            stage(s, rows, n, 24, ((ra, 8, 0), (rg, 12, 0)))
            weight_grad(s, n, 14)

        @pl.when(flip == 0)
        def _():
            branch(0)

        @pl.when(flip == 1)
        def _():
            branch(1)

        for d in range(1, NZ):
            z_send(0, s, d).start()

    slot_of = me + 3 * (me // 3) * (1 - me // 4) - (me // 4) * (1 - me // 7)

    def attn_block(r, s):
        return FB.at[0, s, pl.ds(R * (2 * (r % 2) + r // 4), R)], ga.at[s, slot_of]

    def up_block(r, s):
        return (
            FB.at[1, s, pl.ds(R * (2 * (r % 2) + r // 4), R)],
            gu.at[s, :, pl.ds(pl.multiple_of(D * (me % 4), 128), D)],
        )

    def down_block(r, s):
        return (
            FB.at[1, s, :, pl.ds(HB * (r // 4), HB)],
            gd.at[s, :, pl.ds(pl.multiple_of(HB * ((me // 2) % 2), 128), HB)],
        )

    def spread(r, n, s, block, cond, act):
        src, dst = block(r, s)

        @pl.when(cond & (me != r))
        def _():
            cp = remote(src, dst, s_rd.at[2 * n + s, r], r_rd.at[2 * n + s, me], role_device(r))
            cp.start() if act == "start" else cp.wait_send()

        @pl.when(cond & (me == r))
        def _():
            cp = pltpu.make_async_copy(src, dst, s_own.at[14 + 2 * n + s])
            cp.start() if act == "start" else cp.wait()

    def spread_all(n, s, act):
        for r in range(8):
            if n == 0:
                spread(r, n, s, attn_block, me >= 0, act)
            else:
                spread(r, n, s, up_block, me < 4, act)
                spread(r, n, s, down_block, (me >= 4) & (me % 2 == r % 2), act)

    def spread_wait():
        def arrived(ref, n, s, p):
            remote(
                ref, ref, s_rd.at[2 * n + s, p], r_rd.at[2 * n + s, p], role_device(p)
            ).wait_recv()

        for p in range(8):

            @pl.when(me != p)
            def _():
                for s in range(2):
                    arrived(ga.at[s, p], 0, s, p)
                    if p < 4:
                        arrived(gu.at[s, :, pl.ds(D * p, D)], 1, s, p)

            if p >= 4:

                @pl.when((me != p) & (y == p % 2))
                def _():
                    for s in range(2):
                        arrived(gd.at[s, :, pl.ds(HB * (p % 2), HB)], 1, s, p)

    VG[...] = jnp.zeros_like(VG)
    for step in range(1, g.fsdp):
        vec_wait(step)
    own_vec.wait()
    total = jnp.zeros((16, D), F32)
    lane = lax.broadcasted_iota(jnp.int32, (128, D), 0)
    col = lax.broadcasted_iota(jnp.int32, (128, D), 1)
    for ff in range(g.fsdp):
        pick = ((col == lane + R * ff) & (lane < R)).astype(F32).astype(BF)
        total = total + dot(VEC[ff], pick)
    vecs[...] = total

    def gather_to(t):
        if t > reached[0]:
            gather_steps(reached[0], t)
            reached[0] = t

    def gather_more(n):
        gather_to(min(reached[0] + n, NK + LAG))

    def gather_sent(k):
        def hop(dist):
            for way in range(2):

                @pl.when(z_relay_when(way, dist))
                def _():
                    z_relay(k, way, dist).wait_send()

        loop(NZ - 1, hop)
        loop(NZ, lambda d: y_copy(k, d).wait_send())
        loop(2 * NZ, lambda i: c_copy(k, i % NZ, i // NZ).wait_send())
        loop(2 * NZ - 1, lambda i: x_copy(k, (i + 1) % NZ, (i + 1) // NZ).wait_send())

    for s in range(2):
        base = 16 * s + LAG + 1
        gather_to(base + 2)
        cross_project(s)
        gather_to(base + 3)
        attend(CQ, 0, s, 1 - s, p_refs[s], OC)
        if s == 1:
            gather_more(1)
            z_collect(1, 0)
            spread_all(1, 0, "start")
            gather_more(1)
        gather_to(base + 4)
        out_project(OC, 0, s)
        norm_forward(0, H1, s)
        if s == 1:
            gather_more(1)
        gather_to(base + 6)
        self_project(s)
        if s == 1:
            gather_more(1)
        gather_to(base + 7)
        attend(SQ, 0, s, s, p_refs[2 + s], OS)
        if s == 1:
            z_collect(0, 0)
            spread_all(0, 0, "start")
            gather_more(1)
        gather_to(base + 8)
        out_project(OS, 1, s)
        norm_forward(1, H2, s)
        for r in range(4):
            send_ffn_left(r, 0, s)
        for q in range(4):
            gather_to(base + 8 + q)
            ffn_up(q, s)
            for r in range(4, 8):
                send_ffn_left(r, q, s)
        gather_to(base + 15)
        ffn_down(s)
        gather_more(1)
        tail(s)
        for r in range(4, 8):
            send_ffn_right(r, s)
        gather_more(1)
        ffn_down_back(s)
        for r in range(4):
            send_ffn_right(r, s)
        for r in range(8):
            send_left(r, s)
        gather_more(1)
        ffn_up_back(s)
        norm_backward(1, DS, s)
        send_right(7, s)
        gather_more(1)
        out_back(DS, 1, s)
        attend_back(SQ, 0, s, s, p_refs[2 + s], DQS, DKS, DVS)
        for r in (4, 5, 6):
            send_right(r, s)
        gather_more(1)
        lax.fori_loop(16 * s, 16 * s + 16, lambda k, carry: (gather_sent(k), carry)[1], 0)
        ffn_share(s)
        gather_more(1)
        self_back(s)
        norm_backward(0, DC, s)
        send_right(3, s)
        gather_more(1)
        out_back(DC, 0, s)
        attend_back(CQ, 0, s, 1 - s, p_refs[s], DQC, DKC, DVC)
        for r in (0, 1, 2):
            send_right(r, s)
        gather_more(1)
        attention_share(s)

    def vg_copy(r):
        return remote(VG, VR.at[me], s_vg.at[r], r_vg.at[me], role_device(r))

    for r in range(8):

        @pl.when(me != r)
        def _():
            vg_copy(r).start()

    VR[me] = VG[...]
    cross_back(0)
    cross_back(1)

    for p in range(8):

        @pl.when(me != p)
        def _():
            ref = VR.at[p]
            remote(ref, ref, s_vg.at[p], r_vg.at[p], role_device(p)).wait_recv()

    total = VR[0]
    for p in range(1, 8):
        total = total + VR[p]
    VZ[z] = total

    def vz_copy(d):
        return remote(
            VZ.at[z], VZ.at[z], s_vz.at[d - 1], r_vz.at[d - 1], device(x, (z + d) % NZ, y, c)
        )

    for d in range(1, NZ):
        vz_copy(d).start()
    z_collect(1, 1)
    spread_all(1, 1, "start")
    for d in range(1, NZ):
        ref = VZ.at[(z + NZ - d) % NZ]
        remote(ref, ref, s_vz.at[d - 1], r_vz.at[d - 1], device(x, z, y, c)).wait_recv()
    total = VZ[0]
    for zz in range(1, NZ):
        total = total + VZ[zz]
    vec_out[...] = total
    z_collect(0, 1)
    spread_all(0, 1, "start")

    for step in range(1, g.fsdp):
        vec_copy(step).wait_send()
    finish_sends()
    for r in range(8):

        @pl.when(me != r)
        def _():
            vg_copy(r).wait_send()

    for d in range(1, NZ):
        vz_copy(d).wait_send()
        for n in range(2):
            for s in range(2):
                z_send(n, s, d).wait_send()
    spread_wait()
    for n in range(2):
        for s in range(2):
            spread_all(n, s, "wait")


def finish_kernel(g, *refs):
    rows, (ga, gu, gd, vectors) = refs[:8], refs[8:12]
    outs, (g_in, g_out, g_up, g_dn, g_gain, g_bias, g_gate) = refs[12:20], refs[20:]
    for src, dst in zip(rows, outs):
        dst[...] = src[...]

    for s in range(2):

        def unit(m):
            g_in[s, m] = ga[s, m].astype(F32)

        loop(6, unit)
        for m in range(2):
            g_out[s, m] = ga[s, 6 + m].astype(F32)
        g_up[s] = gu[s].astype(F32)
        g_dn[s] = gd[s].astype(F32)
    row = lax.broadcasted_iota(jnp.int32, (g.d, g.rows), 0)
    lane = lax.broadcasted_iota(jnp.int32, (g.d, g.rows), 1)
    pick = jnp.where(row == lane + lax.axis_index("fsdp") * g.rows, 1.0, 0.0)
    own = lax.dot_general(
        vectors[...], pick, (((1,), (0,)), ((), ())),
        precision=lax.Precision.HIGHEST, preferred_element_type=F32,
    )
    for s in range(2):
        for i in range(3):
            g_gain[s, i : i + 1] = own[3 * s + i : 3 * s + i + 1]
            g_bias[s, i : i + 1] = own[6 + 3 * s + i : 7 + 3 * s + i]
    g_gate[...] = own[12:14]


def kernel_path(g, *args):
    rows, lens, cots = args[0:4], args[4:8], args[8:12]
    weights = args[12:16]
    gain, bias, gate = args[16:19]
    D, FF, R, T, T0, T1, NZ = g.d, g.ff, g.rows, g.t, g.t0, g.t1, g.nz
    vec = jnp.concatenate([gain.reshape(6, R), bias.reshape(6, R), gate], axis=0)
    vec = jnp.pad(vec, ((0, 2), (0, 128 - R)))
    vmem = lambda *shape: pltpu.VMEM(shape[:-1], shape[-1])
    dma = lambda *shape: pltpu.SemaphoreType.DMA(shape)
    in_vmem = pl.BlockSpec(memory_space=pltpu.VMEM)
    in_any = pl.BlockSpec(memory_space=pl.ANY)
    in_smem = pl.BlockSpec(memory_space=pltpu.SMEM)
    row_shapes = [jax.ShapeDtypeStruct(r.shape, BF) for r in rows]
    out_shape = row_shapes * 2 + [
        jax.ShapeDtypeStruct((2, 8, R, D), BF),
        jax.ShapeDtypeStruct((2, R, FF), BF),
        jax.ShapeDtypeStruct((2, 4 * R, D), BF),
        jax.ShapeDtypeStruct((16, D), F32),
        jax.ShapeDtypeStruct((8, T, D), BF),
        jax.ShapeDtypeStruct((8, T, D), BF),
        jax.ShapeDtypeStruct((8, T, 2 * D), BF),
        jax.ShapeDtypeStruct((8, T, D), BF),
    ]
    scratch = [
        vmem(2, 16, D, D, BF),
        vmem(g.fsdp, 16, 128, BF),
        vmem(16, D, F32),
        vmem(14, T, D, BF),
        vmem(T, FF, BF),
        vmem(T, FF, BF),
        vmem(3, T, D, BF),
        vmem(3, T, D, BF),
        vmem(T, D, BF),
        vmem(T, D, F32),
        vmem(T, D, F32),
        vmem(T, D, F32),
        vmem(3, T, D, F32),
        vmem(3, T, 1, F32),
        vmem(T, FF, F32),
        vmem(HEADS, T0, T1, F32),
        vmem(HEADS, T1, T0, F32),
        vmem(HEADS, T0, T0, F32),
        vmem(HEADS, T1, T1, F32),
        vmem(2, 2, NZ - 1, D // NZ, D, BF),
        vmem(2, 2, D // NZ, D, BF),
        vmem(16, D, F32),
        vmem(8, 16, D, F32),
        vmem(NZ, 16, D, F32),
        dma(33),
        dma(g.fsdp - 1),
        dma(g.fsdp - 1),
        dma(32, 2, NZ - 1),
        dma(32, NZ - 1),
        dma(32, NZ),
        dma(32, NZ),
        dma(32, 2 * NZ),
        dma(32, 2 * NZ),
        dma(32, 2 * NZ),
        dma(32, 2 * NZ),
        dma(14, 8),
        dma(14, 8),
        dma(18),
        dma(40),
        dma(2, 2, NZ - 1),
        dma(2, 2, NZ - 1),
        dma(4, 8),
        dma(4, 8),
        dma(8),
        dma(8),
        dma(NZ - 1),
        dma(NZ - 1),
    ]
    results = pl.pallas_call(
        partial(layer_kernel, g),
        out_shape=out_shape,
        in_specs=[in_smem] * 4 + [in_vmem] * 8 + [in_any] * 5,
        out_specs=[in_vmem] * 8 + [in_any] * 3 + [in_vmem] + [in_any] * 4,
        scratch_shapes=scratch,
        compiler_params=pltpu.CompilerParams(
            collective_id=0, has_side_effects=True, vmem_limit_bytes=67043328
        ),
        name="layer",
    )(*lens, *rows, *cots, *weights, vec)
    grad_shapes = [
        jax.ShapeDtypeStruct((2, 6, R, D), F32),
        jax.ShapeDtypeStruct((2, 2, R, D), F32),
        jax.ShapeDtypeStruct((2, R, FF), F32),
        jax.ShapeDtypeStruct((2, 4 * R, D), F32),
        jax.ShapeDtypeStruct((2, 3, R), F32),
        jax.ShapeDtypeStruct((2, 3, R), F32),
        jax.ShapeDtypeStruct((2, R), F32),
    ]
    return tuple(
        pl.pallas_call(
            partial(finish_kernel, g),
            out_shape=row_shapes * 2 + grad_shapes,
            in_specs=[in_vmem] * 12,
            out_specs=[in_vmem] * 15,
            name="finish",
        )(*results[:12])
    )


def solution(mesh):
    def per_device(*args):
        g = Geometry(mesh, [a.shape for a in args])
        return kernel_path(g, *args) if g.fits() else plain_path(*args)

    in_specs = (
        P(("dp", "fsdp"), None, None),
        P(("dp", "fsdp"), None, None),
        P(("dp", "fsdp"), None, None),
        P(("dp", "fsdp"), None, None),
        P(("dp", "fsdp")),
        P(("dp", "fsdp")),
        P(("dp", "fsdp")),
        P(("dp", "fsdp")),
        P(("dp", "fsdp"), None, None),
        P(("dp", "fsdp"), None, None),
        P(("dp", "fsdp"), None, None),
        P(("dp", "fsdp"), None, None),
        P(None, None, "fsdp", None),
        P(None, None, "fsdp", None),
        P(None, "fsdp", None),
        P(None, "fsdp", None),
        P(None, None, "fsdp"),
        P(None, None, "fsdp"),
        P(None, "fsdp"),
    )
    out_specs = (
        P(("dp", "fsdp"), None, None),
        P(("dp", "fsdp"), None, None),
        P(("dp", "fsdp"), None, None),
        P(("dp", "fsdp"), None, None),
        P(("dp", "fsdp"), None, None),
        P(("dp", "fsdp"), None, None),
        P(("dp", "fsdp"), None, None),
        P(("dp", "fsdp"), None, None),
        P(None, None, "fsdp", None),
        P(None, None, "fsdp", None),
        P(None, "fsdp", None),
        P(None, "fsdp", None),
        P(None, None, "fsdp"),
        P(None, None, "fsdp"),
        P(None, "fsdp"),
    )
    return jax.shard_map(
        per_device, mesh=mesh, in_specs=in_specs, out_specs=out_specs, check_vma=False
    )
```

```python
from functools import partial
import math

import jax
import jax.numpy as jnp
from jax import lax
from jax.experimental import pallas as pl
from jax.experimental.pallas import tpu as pltpu
from jax.sharding import PartitionSpec as P

HEADS = 12
BF = jnp.bfloat16
F32 = jnp.float32
MESH_ID = pl.DeviceIdType.MESH
NEG = -1000000000.0


def dot(a, b):
    return lax.dot_general(a, b, (((1,), (0,)), ((), ())), preferred_element_type=F32)


def dot_rt(a, b):
    return lax.dot_general(a, b, (((1,), (1,)), ((), ())), preferred_element_type=F32)


def dot_lt(a, b):
    return lax.dot_general(a, b, (((0,), (0,)), ((), ())), preferred_element_type=F32)


def loop(count, body):
    def step(index, carry):
        body(index)
        return carry

    lax.fori_loop(0, count, step, 0)


def cols(index, size):
    return pl.ds(pl.multiple_of(index * size, size), size)


def erf_of(value):
    x = jnp.minimum(jnp.maximum(value, -3.832506856900711), 3.832506856900711)
    y = x * x
    top = jnp.full_like(y, 0.00022905065861350646)
    for c in (0.0034082910107109506, 0.050955695062380861, 0.18520832239976145, 1.128379143519084):
        top = top * y + c
    low = jnp.full_like(y, -1.1791602954361697e-7)
    for c in (
        0.000023547966471313185,
        0.0010179625278914885,
        0.014070470171167667,
        0.11098505178285362,
        0.49746925110067538,
        1.0,
    ):
        low = low * y + c
    return x * top / low


def project(rows, matrix):
    return jnp.einsum("pld,de->ple", rows, matrix, preferred_element_type=jnp.float32)


def project_back(grads, matrix):
    return jnp.einsum("ple,de->pld", grads, matrix, preferred_element_type=jnp.float32)


def weight_grad(rows, grads):
    return jnp.einsum("pld,ple->de", rows, grads, preferred_element_type=jnp.float32)


def layer_norm(resid, gain_row, bias_row):
    centre = resid - jnp.mean(resid, axis=-1, keepdims=True)
    spread = jnp.mean(centre * centre, axis=-1, keepdims=True)
    return centre * lax.rsqrt(spread + 1e-05) * gain_row + bias_row


def gate_tail(resid, gain_row, bias_row, gate_row, row_mask):
    hidden_three = layer_norm(resid, gain_row, bias_row)
    logit = jnp.einsum("pld,d->pl", hidden_three, gate_row, precision=lax.Precision.HIGHEST)
    return hidden_three * (jax.nn.sigmoid(logit) * row_mask)[..., None]


def exact_gelu(upward):
    return jax.nn.gelu(upward, approximate=False)


def split_heads(rows):
    return rows.reshape(rows.shape[0], rows.shape[1], HEADS, rows.shape[2] // HEADS)


def masked_scores(queries, key_rows, key_mask):
    score_scale = 1.0 / math.sqrt(queries.shape[2] // HEADS)
    scores = (
        jnp.einsum(
            "plhe,pmhe->phlm",
            split_heads(queries),
            split_heads(key_rows),
            preferred_element_type=jnp.float32,
        )
        * score_scale
    )
    return jnp.where(key_mask[:, None, None, :], scores, -1000000000.0)


def attend_forward(queries, key_rows, value_rows, key_mask):
    masked = masked_scores(queries, key_rows, key_mask)
    row_max = jnp.max(masked, axis=-1, keepdims=True)
    expon = jnp.exp(masked - row_max)
    row_sum = jnp.sum(expon, axis=-1, keepdims=True)
    probs = expon / row_sum
    log_total = row_max + jnp.log(row_sum)
    mixed = jnp.einsum(
        "phlm,pmhe->plhe",
        probs.astype(jnp.bfloat16),
        split_heads(value_rows),
        preferred_element_type=jnp.float32,
    )
    return (mixed.reshape(queries.shape).astype(jnp.bfloat16), log_total)


def attend_backward(queries, key_rows, value_rows, key_mask, log_total, grad_mixed):
    score_scale = 1.0 / math.sqrt(queries.shape[2] // HEADS)
    masked = masked_scores(queries, key_rows, key_mask)
    probs = jnp.where(key_mask[:, None, None, :], jnp.exp(masked - log_total), 0.0)
    grad_heads = split_heads(grad_mixed)
    grad_probs = jnp.einsum(
        "plhe,pmhe->phlm", grad_heads, split_heads(value_rows), preferred_element_type=jnp.float32
    )
    grad_scores = (
        probs * (grad_probs - jnp.sum(grad_probs * probs, axis=-1, keepdims=True))
    ).astype(jnp.bfloat16)
    grad_query = (
        jnp.einsum(
            "phlm,pmhe->plhe",
            grad_scores,
            split_heads(key_rows),
            preferred_element_type=jnp.float32,
        )
        * score_scale
    )
    grad_key = (
        jnp.einsum(
            "phlm,plhe->pmhe", grad_scores, split_heads(queries), preferred_element_type=jnp.float32
        )
        * score_scale
    )
    grad_value = jnp.einsum(
        "phlm,plhe->pmhe",
        probs.astype(jnp.bfloat16),
        grad_heads,
        preferred_element_type=jnp.float32,
    )
    return (
        grad_query.reshape(queries.shape).astype(jnp.bfloat16),
        grad_key.reshape(key_rows.shape).astype(jnp.bfloat16),
        grad_value.reshape(value_rows.shape).astype(jnp.bfloat16),
    )


def cross_forward(own_rows, other_rows, other_keys, attn_in):
    cross_query = project(own_rows, attn_in[0]).astype(jnp.bfloat16)
    cross_key = project(other_rows, attn_in[1]).astype(jnp.bfloat16)
    cross_value = project(other_rows, attn_in[2]).astype(jnp.bfloat16)
    cross_mixed, cross_total = attend_forward(cross_query, cross_key, cross_value, other_keys)
    return ((cross_query, cross_key, cross_value), cross_mixed, cross_total)


def stream_forward(own_rows, other_rows, own_keys, other_keys, row_mask, params):
    attn_in, attn_out, ffn_up, ffn_down, gains, biases, gate_row = params
    _, cross_mixed, _ = cross_forward(own_rows, other_rows, other_keys, attn_in)
    resid_one = own_rows.astype(jnp.float32) + project(cross_mixed, attn_out[0])
    hidden_one = layer_norm(resid_one, gains[0], biases[0])
    hidden_low = hidden_one.astype(jnp.bfloat16)
    self_query = project(hidden_low, attn_in[3]).astype(jnp.bfloat16)
    self_key = project(hidden_low, attn_in[4]).astype(jnp.bfloat16)
    self_value = project(hidden_low, attn_in[5]).astype(jnp.bfloat16)
    self_mixed, self_total = attend_forward(self_query, self_key, self_value, own_keys)
    resid_two = hidden_one + project(self_mixed, attn_out[1])
    hidden_two = layer_norm(resid_two, gains[1], biases[1])
    ffn_in = hidden_two.astype(jnp.bfloat16)
    upward = project(ffn_in, ffn_up)
    active = exact_gelu(upward).astype(jnp.bfloat16)
    resid_three = hidden_two + project(active, ffn_down)
    output = gate_tail(resid_three, gains[2], biases[2], gate_row, row_mask)
    saved_rows = (
        resid_one,
        hidden_low,
        self_query,
        self_key,
        self_value,
        self_total,
        self_mixed,
        resid_two,
        ffn_in,
        upward,
        active,
        resid_three,
    )
    return (output, saved_rows)


def stream_backward(
    own_rows, other_rows, own_keys, other_keys, row_mask, params, saved_rows, grad_out
):
    attn_in, attn_out, ffn_up, ffn_down, gains, biases, gate_row = params
    (
        resid_one,
        hidden_low,
        self_query,
        self_key,
        self_value,
        self_total,
        self_mixed,
        resid_two,
        ffn_in,
        upward,
        active,
        resid_three,
    ) = saved_rows
    _, tail_pull = jax.vjp(
        partial(gate_tail, row_mask=row_mask), resid_three, gains[2], biases[2], gate_row
    )
    grad_three, gain_three, bias_three, grad_gate = tail_pull(grad_out)
    grad_down_in = grad_three.astype(jnp.bfloat16)
    down_grad = weight_grad(active, grad_down_in)
    grad_active = project_back(grad_down_in, ffn_down)
    _, gelu_pull = jax.vjp(exact_gelu, upward)
    grad_upward = gelu_pull(grad_active)[0].astype(jnp.bfloat16)
    up_grad = weight_grad(ffn_in, grad_upward)
    grad_two = grad_three + project_back(grad_upward, ffn_up)
    _, norm_two_pull = jax.vjp(layer_norm, resid_two, gains[1], biases[1])
    grad_resid_two, gain_two, bias_two = norm_two_pull(grad_two)
    grad_self_out = grad_resid_two.astype(jnp.bfloat16)
    self_out_grad = weight_grad(self_mixed, grad_self_out)
    grad_self_mixed = project_back(grad_self_out, attn_out[1]).astype(jnp.bfloat16)
    grad_self_query, grad_self_key, grad_self_value = attend_backward(
        self_query, self_key, self_value, own_keys, self_total, grad_self_mixed
    )
    grad_one = (
        grad_resid_two
        + project_back(grad_self_query, attn_in[3])
        + project_back(grad_self_key, attn_in[4])
        + project_back(grad_self_value, attn_in[5])
    )
    _, norm_one_pull = jax.vjp(layer_norm, resid_one, gains[0], biases[0])
    grad_resid_one, gain_one, bias_one = norm_one_pull(grad_one)
    grad_cross_out = grad_resid_one.astype(jnp.bfloat16)
    (cross_query, cross_key, cross_value), cross_mixed, cross_total = cross_forward(
        own_rows, other_rows, other_keys, attn_in
    )
    cross_out_grad = weight_grad(cross_mixed, grad_cross_out)
    grad_cross_mixed = project_back(grad_cross_out, attn_out[0]).astype(jnp.bfloat16)
    grad_cross_query, grad_cross_key, grad_cross_value = attend_backward(
        cross_query, cross_key, cross_value, other_keys, cross_total, grad_cross_mixed
    )
    grad_own = grad_resid_one + project_back(grad_cross_query, attn_in[0])
    grad_other = project_back(grad_cross_key, attn_in[1]) + project_back(
        grad_cross_value, attn_in[2]
    )
    in_grads = jnp.stack(
        [
            weight_grad(own_rows, grad_cross_query),
            weight_grad(other_rows, grad_cross_key),
            weight_grad(other_rows, grad_cross_value),
            weight_grad(hidden_low, grad_self_query),
            weight_grad(hidden_low, grad_self_key),
            weight_grad(hidden_low, grad_self_value),
        ]
    )
    out_grads = jnp.stack([cross_out_grad, self_out_grad])
    gain_grads = jnp.stack([gain_one, gain_two, gain_three])
    bias_grads = jnp.stack([bias_one, bias_two, bias_three])
    return (
        grad_own,
        grad_other,
        (in_grads, out_grads, up_grad, down_grad, gain_grads, bias_grads, grad_gate),
    )


def stream_params(gathered, stream):
    return (
        gathered[0][stream],
        gathered[1][stream],
        gathered[2][stream],
        gathered[3][stream],
        gathered[4][stream].astype(jnp.float32),
        gathered[5][stream].astype(jnp.float32),
        gathered[6][stream].astype(jnp.float32),
    )


def plain_path(
    text_a,
    visual_a,
    text_b,
    visual_b,
    text_len_a,
    visual_len_a,
    text_len_b,
    visual_len_b,
    cot_text_a,
    cot_visual_a,
    cot_text_b,
    cot_visual_b,
    attn_in,
    attn_out,
    ffn_up,
    ffn_down,
    norm_gain,
    norm_bias,
    gate_vector,
):
    gathered = (
        lax.all_gather(attn_in, "fsdp", axis=2, tiled=True),
        lax.all_gather(attn_out, "fsdp", axis=2, tiled=True),
        lax.all_gather(ffn_up, "fsdp", axis=1, tiled=True),
        lax.all_gather(ffn_down, "fsdp", axis=1, tiled=True),
        lax.all_gather(norm_gain, "fsdp", axis=2, tiled=True),
        lax.all_gather(norm_bias, "fsdp", axis=2, tiled=True),
        lax.all_gather(gate_vector, "fsdp", axis=1, tiled=True),
    )
    layouts = []
    for rows_text, rows_visual, len_text, len_visual, cot_text, cot_visual in (
        (text_a, visual_a, text_len_a, visual_len_a, cot_text_a, cot_visual_a),
        (text_b, visual_b, text_len_b, visual_len_b, cot_text_b, cot_visual_b),
    ):
        keys_text = jnp.arange(rows_text.shape[1], dtype=jnp.int32)[None, :] < len_text[:, None]
        keys_visual = (
            jnp.arange(rows_visual.shape[1], dtype=jnp.int32)[None, :] < len_visual[:, None]
        )
        stream_rows = (rows_text, rows_visual)
        stream_keys = (keys_text, keys_visual)
        stream_masks = (keys_text.astype(jnp.float32), keys_visual.astype(jnp.float32))
        outputs = []
        saved_list = []
        for stream in (0, 1):
            other_side = 1 - stream
            output, saved_rows = stream_forward(
                stream_rows[stream],
                stream_rows[other_side],
                stream_keys[stream],
                stream_keys[other_side],
                stream_masks[stream],
                stream_params(gathered, stream),
            )
            outputs.append(output.astype(jnp.bfloat16))
            saved_list.append(saved_rows)
        layouts.append(
            (stream_rows, stream_keys, stream_masks, (cot_text, cot_visual), outputs, saved_list)
        )
    back_weights = gathered
    input_grads = [[None, None], [None, None]]
    stream_grads = []
    for stream in (0, 1):
        other_side = 1 - stream
        params = stream_params(back_weights, stream)
        summed = None
        for layout_index in (0, 1):
            stream_rows, stream_keys, stream_masks, cotangents, outputs, saved_list = layouts[
                layout_index
            ]
            grad_own, grad_other, grads_here = stream_backward(
                stream_rows[stream],
                stream_rows[other_side],
                stream_keys[stream],
                stream_keys[other_side],
                stream_masks[stream],
                params,
                saved_list[stream],
                cotangents[stream].astype(jnp.float32),
            )
            for target, piece in ((stream, grad_own), (other_side, grad_other)):
                if input_grads[layout_index][target] is None:
                    input_grads[layout_index][target] = piece
                else:
                    input_grads[layout_index][target] = input_grads[layout_index][target] + piece
            if summed is None:
                summed = grads_here
            else:
                summed = tuple((left + right for left, right in zip(summed, grads_here)))
        stream_grads.append(summed)
    text_grads = stream_grads[0]
    visual_grads = stream_grads[1]
    row_dims = (1, 1, 0, 0, 1, 1, 0)
    packed = tuple(
        (
            jnp.concatenate([text_grads[index], visual_grads[index]], axis=row_dims[index])
            for index in range(7)
        )
    )
    shares = (
        lax.psum_scatter(packed[0], ("dp", "fsdp"), scatter_dimension=1, tiled=True),
        lax.psum_scatter(packed[1], ("dp", "fsdp"), scatter_dimension=1, tiled=True),
        lax.psum_scatter(packed[2], ("dp", "fsdp"), scatter_dimension=0, tiled=True),
        lax.psum_scatter(packed[3], ("dp", "fsdp"), scatter_dimension=0, tiled=True),
        lax.psum_scatter(packed[4], ("dp", "fsdp"), scatter_dimension=1, tiled=True),
        lax.psum_scatter(packed[5], ("dp", "fsdp"), scatter_dimension=1, tiled=True),
        lax.psum_scatter(packed[6], ("dp", "fsdp"), scatter_dimension=0, tiled=True),
    )
    joined = (
        lax.all_gather(shares[0].astype(jnp.bfloat16), "dp", axis=1, tiled=True).astype(
            jnp.float32
        ),
        lax.all_gather(shares[1].astype(jnp.bfloat16), "dp", axis=1, tiled=True).astype(
            jnp.float32
        ),
        lax.all_gather(shares[2].astype(jnp.bfloat16), "dp", axis=0, tiled=True).astype(
            jnp.float32
        ),
        lax.all_gather(shares[3].astype(jnp.bfloat16), "dp", axis=0, tiled=True).astype(
            jnp.float32
        ),
        lax.all_gather(shares[4].astype(jnp.bfloat16), "dp", axis=1, tiled=True).astype(
            jnp.float32
        ),
        lax.all_gather(shares[5].astype(jnp.bfloat16), "dp", axis=1, tiled=True).astype(
            jnp.float32
        ),
        lax.all_gather(shares[6].astype(jnp.bfloat16), "dp", axis=0, tiled=True).astype(
            jnp.float32
        ),
    )
    finals = tuple(
        (jnp.stack(jnp.split(joined[index], 2, axis=row_dims[index])) for index in range(7))
    )
    first_outputs = layouts[0][4]
    second_outputs = layouts[1][4]
    return (
        first_outputs[0],
        first_outputs[1],
        second_outputs[0],
        second_outputs[1],
        input_grads[0][0].astype(jnp.bfloat16),
        input_grads[0][1].astype(jnp.bfloat16),
        input_grads[1][0].astype(jnp.bfloat16),
        input_grads[1][1].astype(jnp.bfloat16),
        finals[0],
        finals[1],
        finals[2],
        finals[3],
        finals[4],
        finals[5],
        finals[6],
    )


class Geometry:
    def __init__(self, mesh, shapes):
        self.dp = mesh.shape["dp"]
        self.fsdp = mesh.shape["fsdp"]
        (self.la, self.lva), (self.lb, self.lvb) = (
            (shapes[0][1], shapes[1][1]),
            (shapes[2][1], shapes[3][1]),
        )
        self.d = shapes[0][2]
        self.rows = self.d // self.fsdp
        self.ff = shapes[14][2]
        self.pages = shapes[0][0]
        self.t0 = -(-(self.la + self.lb) // 16) * 16
        self.t1 = -(-(self.lva + self.lvb) // 16) * 16
        self.t = self.t0 + self.t1
        self.nz = self.fsdp // 4

    def fits(self):
        return (
            self.dp == 2
            and self.fsdp == 16
            and self.pages == 1
            and self.d == 16 * 48
            and self.ff == 4 * self.d
            and self.t0 >= self.t1
            and self.d == 64 * HEADS
        )


def layer_kernel(g, *refs):
    D, FF, R, T0, T1, T, NZ = g.d, g.ff, g.rows, g.t0, g.t1, g.t, g.nz
    ZR = D // NZ
    it = iter(refs)
    take = lambda n: [next(it) for _ in range(n)]
    lens = take(4)
    rows_in = take(4)
    cots_in = take(4)
    w_parts = take(4)
    (vec_in,) = take(1)
    outs = take(4)
    grads = take(4)
    ga, gu, gd, vec_out = take(4)
    ra, rg, rfa, rfg = take(4)
    W, VEC, vecs = take(3)
    S, A, DU, CQ, SQ, DO = take(6)
    RES, HID, DR, XH, RSTD, GP = take(6)
    p_refs = take(4)
    RZ, FB, VG, VR, VZ = take(5)
    (s_loc, s_vec, r_vec, sz, rz, sy, ry, sx, rx, sc, rc) = take(11)
    (s_ex, r_ex, s_own, s_st, s_zr, r_zr, s_rd, r_rd, s_vg, r_vg, s_vz, r_vz) = take(12)

    X, H1, OC, OS, H2 = 0, 1, 2, 3, 4
    DQC, DKC, DVC, DQS, DKS, DVS, DC, DS, DF = range(5, 14)
    span = (slice(0, T0), slice(T0, T))
    size = (T0, T1)

    x = lax.axis_index("dp")
    f = lax.axis_index("fsdp")
    z, y, c = f // 4, (f // 2) % 2, f % 2
    me = c * 4 + x * 2 + y

    def device(xx, zz, yy, cc):
        return (xx, zz * 4 + yy * 2 + cc)

    def role_device(r):
        return device((r // 2) % 2, z, r % 2, r // 4)

    def remote(src, dst, send, recv, dev):
        return pltpu.make_async_remote_copy(
            src_ref=src, dst_ref=dst, send_sem=send, recv_sem=recv, device_id=dev,
            device_id_type=MESH_ID,
        )

    barrier = pltpu.get_barrier_semaphore()
    for step in range(1, g.fsdp):
        pl.semaphore_signal(
            barrier, inc=1, device_id=(x, (f + step) % g.fsdp), device_id_type=MESH_ID
        )
    for r in range(4):
        pl.semaphore_signal(
            barrier, inc=1, device_id=device(1 - x, z, r // 2, r % 2), device_id_type=MESH_ID
        )
    pl.semaphore_wait(barrier, g.fsdp + 3)

    def wref(k, ff, r0, n):
        kk = k % 16
        down = kk // 12
        unit = kk + down * (12 + (4 * R * ff) // D - kk)
        row = R * ff + down * ((4 * R * ff) % D + R * (kk - 12) - R * ff) + r0
        return W.at[k // 16, unit, pl.ds(pl.multiple_of(row, 16), n)]

    def local_part(k):
        w_in, w_out, w_up, w_dn = w_parts
        s, k = k // 16, k % 16
        if k in (3, 7):
            return w_out.at[s, (k - 3) // 4]
        if k < 8:
            return w_in.at[s, (0, 1, 2, None, 3, 4, 5)[k]]
        if k < 12:
            return w_up.at[s, :, pl.ds(D * (k - 8), D)]
        return w_dn.at[s, pl.ds(R * (k - 12), R)]

    third = R // 3
    NK = 32
    AHEAD = 2
    GAP = 2
    LAG = AHEAD + (NZ + 1) * GAP
    for k in range(NK):
        cp = pltpu.make_async_copy(local_part(k), wref(k, f, 0, R), s_loc.at[k])
        cp.start()

    def vec_copy(step):
        return remote(
            vec_in, VEC.at[f], s_vec.at[step - 1], r_vec.at[step - 1],
            (x, (f + step) % g.fsdp),
        )

    def vec_wait(step):
        ref = VEC.at[(f + g.fsdp - step) % g.fsdp]
        remote(ref, ref, s_vec.at[step - 1], r_vec.at[step - 1], (x, f)).wait_recv()

    for step in range(1, g.fsdp):
        vec_copy(step).start()
    own_vec = pltpu.make_async_copy(vec_in, VEC.at[f], s_loc.at[NK])
    own_vec.start()

    def shard(zz, yy):
        return zz * 4 + yy * 2 + c

    def z_relay(k, way, dist):
        up = way == 0
        ref = wref(k, shard(z - dist if up else z + dist, y), third * x, 2 * third)
        lands = dist + 1 if up else NZ - 1 - dist
        return remote(
            ref, ref, sz.at[k, way, dist], rz.at[k, lands - 1],
            device(x, z + 1 if up else z - 1, y, c),
        )

    def z_wait(k, d):
        ref = wref(k, shard((z + NZ - d) % NZ, y), third * x, 2 * third)
        remote(ref, ref, sz.at[k, 0, 0], rz.at[k, d - 1], device(x, z, 1 - y, c)).wait_recv()

    def z_relay_when(way, dist):
        return (z >= dist) & (z + 1 < NZ) if way == 0 else (z + dist < NZ) & (z >= 1)

    def y_copy(k, d):
        ref = wref(k, shard((z + NZ - d) % NZ, y), third * x, 2 * third)
        return remote(ref, ref, sy.at[k, d], ry.at[k, d], device(x, z, 1 - y, c))

    def y_wait(k, d):
        ref = wref(k, shard((z + NZ - d) % NZ, 1 - y), third * x, 2 * third)
        remote(ref, ref, sy.at[k, d], ry.at[k, d], device(x, z, 1 - y, c)).wait_recv()

    def x_copy(k, d, e):
        ref = wref(k, shard((z + NZ - d) % NZ, (y + e) % 2), 2 * third * x, third)
        return remote(ref, ref, sx.at[k, 2 * d + e], rx.at[k, 2 * d + e], device(1 - x, z, y, c))

    def x_wait(k, d, e):
        ref = wref(k, shard((z + NZ - d) % NZ, (y + e) % 2), 2 * third * (1 - x), third)
        remote(ref, ref, sx.at[k, 2 * d + e], rx.at[k, 2 * d + e], device(1 - x, z, y, c)).wait_recv()

    def c_copy(k, d, e):
        ref = wref(k, shard((z + NZ - d) % NZ, (y + e) % 2), 0, R)
        return remote(ref, ref, sc.at[k, 2 * d + e], rc.at[k, 2 * d + e], device(x, z, y, 1 - c))

    def c_wait(k, d, e):
        other = ((z + NZ - d) % NZ) * 4 + ((y + e) % 2) * 2 + 1 - c
        ref = wref(k, other, 0, R)
        remote(ref, ref, sc.at[k, 2 * d + e], rc.at[k, 2 * d + e], device(x, z, y, 1 - c)).wait_recv()

    def own_start(k):
        ref = wref(k, f, 0, R)
        pltpu.make_async_copy(ref, ref, s_loc.at[k]).wait()
        for way in range(2):

            @pl.when(z_relay_when(way, 0))
            def _():
                z_relay(k, way, 0).start()

        y_copy(k, 0).start()
        c_copy(k, 0, 0).start()

    def z_stage(k, dist):
        for way in range(2):
            d = dist if way == 0 else NZ - dist

            @pl.when(z >= dist if way == 0 else z + dist < NZ)
            def _():
                z_wait(k, d)

                @pl.when((dist < NZ - 1) & (z + 1 < NZ if way == 0 else z >= 1))
                def _():
                    z_relay(k, way, dist).start()

                y_copy(k, d).start()
                x_copy(k, d, 0).start()

    def y_stage(k):
        def one(d):
            y_wait(k, d)
            x_copy(k, d, 1).start()

        loop(NZ, one)

    def x_stage(k):
        def one(i):
            d, e = (i + 1) % NZ, (i + 1) // NZ
            x_wait(k, d, e)
            c_copy(k, d, e).start()

        loop(2 * NZ - 1, one)

    def c_stage(k):
        loop(2 * NZ, lambda i: c_wait(k, i % NZ, i // NZ))

    def gather_step(t):
        def at(k, act):
            @pl.when((k >= 0) & (k < NK))
            def _():
                act(k)

        at(t, own_start)
        loop(
            NZ - 1,
            lambda i: at(t - AHEAD - i * GAP, lambda k: z_stage(k, i + 1)),
        )
        at(t - AHEAD - (NZ - 1) * GAP, y_stage)
        at(t - AHEAD - NZ * GAP, x_stage)
        at(t - LAG, c_stage)

    def gather_steps(lo, hi):
        def step(t, carry):
            gather_step(t)
            return carry

        lax.fori_loop(lo, hi, step, 0)

    gather_steps(0, 2)
    reached = [2]

    la, lva = g.la, g.lva

    def assemble(dst, parts):
        ta, va, tb, vb = parts
        dst[0:la] = ta[0].astype(F32)
        dst[la : la + g.lb] = tb[0].astype(F32)
        if T0 > la + g.lb:
            dst[la + g.lb : T0] = jnp.zeros((T0 - la - g.lb, D), F32)
        dst[T0 : T0 + lva] = va[0].astype(F32)
        dst[T0 + lva : T0 + lva + g.lvb] = vb[0].astype(F32)
        if T1 > lva + g.lvb:
            dst[T0 + lva + g.lvb : T] = jnp.zeros((T1 - lva - g.lvb, D), F32)

    assemble(HID, rows_in)
    S[X] = HID[...].astype(BF)
    assemble(DR, cots_in)

    def live(index, s):
        first, second = (la, g.lb) if s == 0 else (lva, g.lvb)
        na, nb = lens[s][0], lens[2 + s][0]
        return ((index < first) & (index < na)) | (
            (index >= first) & (index - first < nb) & (index - first < second)
        )

    def key_mask(qs, ks):
        shape = (size[qs], size[ks])
        qi = lax.broadcasted_iota(jnp.int32, shape, 0)
        ki = lax.broadcasted_iota(jnp.int32, shape, 1)
        q_first = la if qs == 0 else lva
        k_first = la if ks == 0 else lva
        same = ((qi < q_first) & (ki < k_first)) | ((qi >= q_first) & (ki >= k_first))
        return same & live(ki, ks)

    UA = (0, 1, 2, 4, 5, 6)
    UB = (3, 7)

    def wtile(s, u, i):
        return W[s, u, :, cols(i, 256)]

    def wrows(s, u, i):
        return W[s, u, cols(i, 256), :]

    NT = D // 256

    def cross_project(s):
        own, other = span[s], span[1 - s]

        def q_tile(i):
            CQ[0, own, cols(i, 256)] = dot(S[X, own], wtile(s, 0, i)).astype(BF)

        loop(NT, q_tile)

        def kv_tile(i):
            m = 1 + i // NT
            j = i % NT
            CQ[m, other, cols(j, 256)] = dot(S[X, other], wtile(s, m, j)).astype(BF)

        loop(2 * NT, kv_tile)

    def self_project(s):
        own = span[s]

        def tile(i):
            m = i // NT
            j = i % NT
            SQ[m, own, cols(j, 256)] = dot(S[H1, own], wtile(s, 4 + m, j)).astype(BF)

        loop(3 * NT, tile)

    def attend(src, base, s, ks, p_ref, o_index):
        own, keys = span[s], span[ks]

        def pair(p):
            lanes = cols(p, 128)
            mask = key_mask(s, ks)
            q, k, v = src[base, own, lanes], src[base + 1, keys, lanes], src[base + 2, keys, lanes]
            low = lax.broadcasted_iota(jnp.int32, q.shape, 1) < 64
            high = lax.broadcasted_iota(jnp.int32, q.shape, 1) >= 64
            mixed = []
            for half in range(2):
                qh = jnp.where(low if half == 0 else high, q, jnp.zeros_like(q))
                scores = jnp.where(mask, dot_rt(qh, k) * 0.125, NEG)
                top = jnp.max(scores, axis=-1, keepdims=True)
                expon = jnp.exp(scores - top)
                probs = expon / jnp.sum(expon, axis=-1, keepdims=True)
                p_ref[2 * p + half] = probs
                mixed.append(dot(probs.astype(BF), v))
            S[o_index, own, lanes] = jnp.where(low, mixed[0], mixed[1]).astype(BF)

        loop(HEADS // 2, pair)

    def attend_back(src, base, s, ks, p_ref, gq, gk, gv):
        own, keys = span[s], span[ks]

        def pair(p):
            lanes = cols(p, 128)
            q, k, v = src[base, own, lanes], src[base + 1, keys, lanes], src[base + 2, keys, lanes]
            do = DO[own, lanes]
            low_q = lax.broadcasted_iota(jnp.int32, q.shape, 1) < 64
            high_q = lax.broadcasted_iota(jnp.int32, q.shape, 1) >= 64
            low_k = lax.broadcasted_iota(jnp.int32, k.shape, 1) < 64
            dq, dk, dv = [], [], []
            for half in range(2):
                doh = jnp.where(low_q if half == 0 else high_q, do, jnp.zeros_like(do))
                probs = p_ref[2 * p + half]
                dp = dot_rt(doh, v)
                ds = (probs * (dp - jnp.sum(dp * probs, axis=-1, keepdims=True))).astype(BF)
                dq.append(dot(ds, k))
                dk.append(dot_lt(ds, q))
                dv.append(dot_lt(probs.astype(BF), do))
            S[gq, own, lanes] = (jnp.where(low_q, dq[0], dq[1]) * 0.125).astype(BF)
            S[gk, keys, lanes] = (jnp.where(low_k, dk[0], dk[1]) * 0.125).astype(BF)
            S[gv, keys, lanes] = jnp.where(low_k, dv[0], dv[1]).astype(BF)

        loop(HEADS // 2, pair)

    def out_project(o_index, which, s):
        own = span[s]

        def tile(i):
            RES[own, cols(i, 256)] = HID[own, cols(i, 256)] + dot(
                S[o_index, own], wtile(s, UB[which], i)
            )

        loop(NT, tile)

    RB = 16
    mean = lambda v: jnp.sum(v, axis=-1, keepdims=True) * (1.0 / D)

    def normalize(i, r):
        resid = RES[r]
        centre = resid - mean(resid)
        rstd = lax.rsqrt(mean(centre * centre) + 1e-05)
        return centre * rstd, rstd

    def rows_of(s, b):
        return pl.ds(pl.multiple_of((0, T0)[s] + b * RB, RB), RB)

    def norm_forward(i, h_index, s):
        def block(b):
            r = rows_of(s, b)
            xh, rstd = normalize(i, r)
            XH[i, r] = xh
            RSTD[i, r] = rstd
            hidden = xh * vecs[pl.ds(s * 3 + i, 1), :] + vecs[pl.ds(6 + s * 3 + i, 1), :]
            HID[r] = hidden
            S[h_index, r] = hidden.astype(BF)

        loop(size[s] // RB, block)

    def add_row(row, value):
        VG[pl.ds(row, 1), :] += jnp.sum(value, axis=0, keepdims=True)

    def norm_pull(i, s, r, dh, xh, rstd):
        add_row(s * 3 + i, dh * xh)
        add_row(6 + s * 3 + i, dh)
        dx = dh * vecs[pl.ds(s * 3 + i, 1), :]
        return rstd * (dx - mean(dx) - xh * mean(dx * xh))

    def norm_backward(i, g_index, s):
        def block(b):
            r = rows_of(s, b)
            dr = norm_pull(i, s, r, DR[r], XH[i, r], RSTD[i, r])
            DR[r] = dr
            S[g_index, r] = dr.astype(BF)

        loop(size[s] // RB, block)

    def tail(s):
        def block(b):
            r = rows_of(s, b)
            xh, rstd = normalize(2, r)
            gain = vecs[pl.ds(s * 3 + 2, 1), :]
            h3 = xh * gain + vecs[pl.ds(6 + s * 3 + 2, 1), :]
            gate = vecs[pl.ds(12 + s, 1), :]
            logit = jnp.sum(h3 * gate, axis=-1, keepdims=True)
            sig = 1.0 / (1.0 + jnp.exp(-logit))
            index = lax.broadcasted_iota(jnp.int32, (RB, 1), 0) + b * RB
            mask = jnp.where(live(index, s), 1.0, 0.0)
            weight = sig * mask
            HID[r] = h3 * weight
            dout = DR[r]
            dlogit = jnp.sum(dout * h3, axis=-1, keepdims=True) * weight * (1.0 - sig)
            add_row(12 + s, h3 * dlogit)
            dr = norm_pull(2, s, r, dout * weight + dlogit * gate, xh, rstd)
            DR[r] = dr
            S[DF, r] = dr.astype(BF)

        loop(size[s] // RB, block)
        o_ta, o_va, o_tb, o_vb = outs
        if s == 0:
            o_ta[0] = HID[0:la].astype(BF)
            o_tb[0] = HID[la : la + g.lb].astype(BF)
        else:
            o_va[0] = HID[T0 : T0 + lva].astype(BF)
            o_vb[0] = HID[T0 + lva : T0 + lva + g.lvb].astype(BF)

    def ffn_up(q, s):
        own = span[s]

        def tile(i):
            j = q * NT + i
            u = dot(S[H2, own], wtile(s, 8 + q, i))
            cdf = 0.5 + 0.5 * erf_of(u * 0.7071067811865476)
            A[own, cols(j, 256)] = (u * cdf).astype(BF)
            GP[own, cols(j, 256)] = cdf + u * (
                jnp.exp(u * u * -0.5) * 0.3989422804014327
            )

        loop(NT, tile)

    def ffn_down(s):
        own = span[s]

        def tile(i):
            total = HID[own, cols(i, 256)]
            for q in range(4):
                total = total + dot(A[own, D * q : D * q + D], wtile(s, 12 + q, i))
            RES[own, cols(i, 256)] = total

        loop(NT, tile)

    def ffn_down_back(s, q):
        own = span[s]

        def tile(i):
            j = q * NT + i
            da = dot_rt(S[DF, own], wrows(s, 12 + q, i))
            DU[own, cols(j, 256)] = (GP[own, cols(j, 256)] * da).astype(BF)

        loop(NT, tile)

    def ffn_up_back(s):
        own = span[s]

        def tile(i):
            total = DR[own, cols(i, 256)]
            for q in range(4):
                total = total + dot_rt(DU[own, D * q : D * q + D], wrows(s, 8 + q, i))
            DR[own, cols(i, 256)] = total

        loop(NT, tile)

    def out_back(g_index, which, s):
        own = span[s]

        def tile(i):
            DO[own, cols(i, 256)] = dot_rt(
                S[g_index, own], wrows(s, UB[which], i)
            ).astype(BF)

        loop(NT, tile)

    def self_back(s):
        own = span[s]

        def tile(i):
            total = DR[own, cols(i, 256)]
            for m, gi in enumerate((DQS, DKS, DVS)):
                total = total + dot_rt(S[gi, own], wrows(s, 4 + m, i))
            DR[own, cols(i, 256)] = total

        loop(NT, tile)

    def cross_back(s):
        own = span[s]

        def tile(i):
            total = DR[own, cols(i, 256)] + dot_rt(S[DQC, own], wrows(s, 0, i))
            total = total + dot_rt(S[DKC, own], wrows(1 - s, 1, i))
            total = total + dot_rt(S[DVC, own], wrows(1 - s, 2, i))
            DR[own, cols(i, 256)] = total

        loop(NT, tile)
        g_ta, g_va, g_tb, g_vb = grads
        if s == 0:
            g_ta[0] = DR[0:la].astype(BF)
            g_tb[0] = DR[la : la + g.lb].astype(BF)
        else:
            g_va[0] = DR[T0 : T0 + lva].astype(BF)
            g_vb[0] = DR[T0 + lva : T0 + lva + g.lvb].astype(BF)

    sends = []

    def plane_send(r, src, dst, slot):
        @pl.when(me != r)
        def _():
            remote(src, dst, s_ex.at[slot, r], r_ex.at[slot, me], role_device(r)).start()

        @pl.when(me == r)
        def _():
            pltpu.make_async_copy(src, dst, s_own.at[slot]).start()

        sends.append((r, src, dst, slot))

    def finish_sends():
        for r, src, dst, slot in sends:

            @pl.when(me != r)
            def _():
                remote(src, dst, s_ex.at[slot, r], r_ex.at[slot, me], role_device(r)).wait_send()

    def plane_wait(slot, pick):
        for p in range(8):
            ref = pick(p)

            @pl.when(me != p)
            def _():
                remote(ref, ref, s_ex.at[slot, p], r_ex.at[slot, p], role_device(p)).wait_recv()

            @pl.when(me == p)
            def _():
                pltpu.make_async_copy(ref, ref, s_own.at[slot]).wait()

    A_OF = (X, X, X, OC, H1, H1, H1, OS)
    G_OF = (DQC, DKC, DVC, DC, DQS, DKS, DVS, DS)
    HB = D // 2

    def rows_for(r, s):
        t = 1 - s if r in (1, 2) else s
        return pl.ds((0, T0)[t], size[t])

    def send_left(r, s):
        rows = rows_for(r, s)
        plane_send(r, S.at[A_OF[r], rows], ra.at[me, rows], 7 * s)

    def send_right(r, s):
        rows = rows_for(r, s)
        plane_send(r, S.at[G_OF[r], rows], rg.at[me, rows], 7 * s + 1)

    def own_rows(s):
        return pl.ds((0, T0)[s], size[s])

    def send_ffn_left(r, q, s):
        rows = own_rows(s)
        if r < 4:
            plane_send(r, S.at[H2, rows], rfa.at[me, rows, pl.ds(0, D)], 7 * s + 3)
        else:
            plane_send(
                r, A.at[rows, pl.ds(D * q + HB * (r % 2), HB)],
                rfa.at[me, rows, pl.ds(HB * q, HB)], 7 * s + 3 + q,
            )

    def send_ffn_right(r, s):
        rows = own_rows(s)
        if r < 4:
            plane_send(r, DU.at[rows, pl.ds(D * r, D)], rfg.at[me, rows], 7 * s + 2)
        else:
            hh = (r // 2) % 2
            plane_send(
                r, S.at[DF, rows, pl.ds(HB * hh, HB)], rfg.at[me, rows, pl.ds(0, HB)], 7 * s + 2
            )

    flip = (((me + 1) // 2) % 2) * (1 - me // 4)

    def stage(s, rows, n, first, blocks):
        made = []
        for src, unit, col in blocks:
            for p in range(8):
                made.append(
                    pltpu.make_async_copy(
                        src.at[p, rows, pl.ds(col, D)],
                        W.at[s, unit + p // 4, pl.ds(n * (p % 4), n)],
                        s_st.at[first + len(made)],
                    )
                )
        for cp in made:
            cp.start()
        for cp in made:
            cp.wait()

    def stacked(s, unit, n, lanes):
        return jnp.concatenate(
            [W[s, unit + p // 4, n * (p % 4) : n * (p % 4) + n, lanes] for p in range(8)], axis=0
        )

    def weight_grad(s, n, dst):
        def tile(i):
            W[s, dst, cols(i, 256), :] = dot_lt(
                stacked(s, 8, n, cols(i, 256)), stacked(s, 12, n, slice(0, D))
            ).astype(BF)

        loop(NT, tile)

    def weight_grad_down(s, n, dst):
        def tile(q):
            out = dot_lt(
                stacked(s, 8 + 2 * (q // 2), n, cols(q % 2, HB)), stacked(s, 12, n, slice(0, HB))
            ).astype(BF)
            W[s, dst, pl.ds(pl.multiple_of(q * ZR, ZR), ZR), 0:HB] = out[0:ZR]
            W[s, dst, pl.ds(pl.multiple_of(q * ZR, ZR), ZR), HB:D] = out[ZR : 2 * ZR]

        loop(4, tile)

    def z_send(n, s, d):
        zz = (z + d) % NZ
        src = W.at[s, 14 + n, pl.ds(pl.multiple_of(zz * ZR, ZR), ZR)]
        return remote(
            src, RZ.at[n, s, d - 1], s_zr.at[n, s, d - 1], r_zr.at[n, s, d - 1],
            device(x, zz, y, c),
        )

    def z_collect(n, s):
        for d in range(1, NZ):
            z_send(n, s, d).wait_recv()

        def block(i):
            total = W[s, 14 + n, pl.ds(pl.multiple_of(z * ZR + i * 16, 16), 16)].astype(F32)
            for d in range(NZ - 1):
                total = total + RZ[n, s, d, cols(i, 16)].astype(F32)
            FB[n, s, cols(i, 16)] = total.astype(BF)

        loop(ZR // 16, block)

    def ffn_share(s):
        rows, n = own_rows(s), size[s]

        @pl.when(me < 4)
        def _():
            plane_wait(7 * s + 2, lambda p: rfg.at[p, rows])
            plane_wait(7 * s + 3, lambda p: rfa.at[p, rows, pl.ds(0, D)])

        @pl.when(me >= 4)
        def _():
            plane_wait(7 * s + 2, lambda p: rfg.at[p, rows, pl.ds(0, HB)])
            for q in range(4):
                plane_wait(7 * s + 3 + q, lambda p: rfa.at[p, rows, pl.ds(HB * q, HB)])

        stage(s, rows, n, 0, ((rfg, 12, 0), (rfa, 8, 0), (rfa, 10, D)))

        @pl.when(me < 4)
        def _():
            weight_grad(s, n, 15)

        @pl.when(me >= 4)
        def _():
            weight_grad_down(s, n, 15)

        for d in range(1, NZ):
            z_send(1, s, d).start()

    def attention_share(s):
        def branch(r):
            rows, n = rows_for(r, s), size[1 - s if r in (1, 2) else s]
            plane_wait(7 * s, lambda p: ra.at[p, rows])
            plane_wait(7 * s + 1, lambda p: rg.at[p, rows])
            stage(s, rows, n, 24, ((ra, 8, 0), (rg, 12, 0)))
            weight_grad(s, n, 14)

        @pl.when(flip == 0)
        def _():
            branch(0)

        @pl.when(flip == 1)
        def _():
            branch(1)

        for d in range(1, NZ):
            z_send(0, s, d).start()

    slot_of = me + 3 * (me // 3) * (1 - me // 4) - (me // 4) * (1 - me // 7)

    def attn_block(r, s):
        return FB.at[0, s, pl.ds(R * (2 * (r % 2) + r // 4), R)], ga.at[s, slot_of]

    def up_block(r, s):
        return (
            FB.at[1, s, pl.ds(R * (2 * (r % 2) + r // 4), R)],
            gu.at[s, :, pl.ds(pl.multiple_of(D * (me % 4), 128), D)],
        )

    def down_block(r, s):
        return (
            FB.at[1, s, :, pl.ds(HB * (r // 4), HB)],
            gd.at[s, :, pl.ds(pl.multiple_of(HB * ((me // 2) % 2), 128), HB)],
        )

    def spread(r, n, s, block, cond, act):
        src, dst = block(r, s)

        @pl.when(cond & (me != r))
        def _():
            cp = remote(src, dst, s_rd.at[2 * n + s, r], r_rd.at[2 * n + s, me], role_device(r))
            cp.start() if act == "start" else cp.wait_send()

        @pl.when(cond & (me == r))
        def _():
            cp = pltpu.make_async_copy(src, dst, s_own.at[14 + 2 * n + s])
            cp.start() if act == "start" else cp.wait()

    def spread_all(n, s, act):
        for r in range(8):
            if n == 0:
                spread(r, n, s, attn_block, me >= 0, act)
            else:
                spread(r, n, s, up_block, me < 4, act)
                spread(r, n, s, down_block, (me >= 4) & (me % 2 == r % 2), act)

    def spread_wait():
        def arrived(ref, n, s, p):
            remote(
                ref, ref, s_rd.at[2 * n + s, p], r_rd.at[2 * n + s, p], role_device(p)
            ).wait_recv()

        for p in range(8):

            @pl.when(me != p)
            def _():
                for s in range(2):
                    arrived(ga.at[s, p], 0, s, p)
                    if p < 4:
                        arrived(gu.at[s, :, pl.ds(D * p, D)], 1, s, p)

            if p >= 4:

                @pl.when((me != p) & (y == p % 2))
                def _():
                    for s in range(2):
                        arrived(gd.at[s, :, pl.ds(HB * (p % 2), HB)], 1, s, p)

    VG[...] = jnp.zeros_like(VG)
    for step in range(1, g.fsdp):
        vec_wait(step)
    own_vec.wait()
    total = jnp.zeros((16, D), F32)
    lane = lax.broadcasted_iota(jnp.int32, (128, D), 0)
    col = lax.broadcasted_iota(jnp.int32, (128, D), 1)
    for ff in range(g.fsdp):
        pick = ((col == lane + R * ff) & (lane < R)).astype(F32).astype(BF)
        total = total + dot(VEC[ff], pick)
    vecs[...] = total

    def gather_to(t):
        if t > reached[0]:
            gather_steps(reached[0], t)
            reached[0] = t

    def gather_more(n):
        gather_to(min(reached[0] + n, NK + LAG))

    def gather_sent(k):
        def hop(dist):
            for way in range(2):

                @pl.when(z_relay_when(way, dist))
                def _():
                    z_relay(k, way, dist).wait_send()

        loop(NZ - 1, hop)
        loop(NZ, lambda d: y_copy(k, d).wait_send())
        loop(2 * NZ, lambda i: c_copy(k, i % NZ, i // NZ).wait_send())
        loop(2 * NZ - 1, lambda i: x_copy(k, (i + 1) % NZ, (i + 1) // NZ).wait_send())

    for s in range(2):
        base = 16 * s + LAG + 1
        gather_to(base + 2)
        cross_project(s)
        gather_to(base + 3)
        attend(CQ, 0, s, 1 - s, p_refs[s], OC)
        if s == 1:
            gather_more(1)
            z_collect(1, 0)
            spread_all(1, 0, "start")
            gather_more(1)
        gather_to(base + 4)
        out_project(OC, 0, s)
        norm_forward(0, H1, s)
        if s == 1:
            gather_more(1)
        gather_to(base + 6)
        self_project(s)
        if s == 1:
            gather_more(1)
        gather_to(base + 7)
        attend(SQ, 0, s, s, p_refs[2 + s], OS)
        if s == 1:
            z_collect(0, 0)
            spread_all(0, 0, "start")
            gather_more(1)
        gather_to(base + 8)
        out_project(OS, 1, s)
        norm_forward(1, H2, s)
        for r in range(4):
            send_ffn_left(r, 0, s)
        for q in range(4):
            gather_to(base + 8 + q)
            ffn_up(q, s)
            for r in range(4, 8):
                send_ffn_left(r, q, s)
        gather_to(base + 15)
        ffn_down(s)
        gather_more(1)
        tail(s)
        for r in range(4, 8):
            send_ffn_right(r, s)
        gather_more(1)
        for r in range(4):
            ffn_down_back(s, r)
            send_ffn_right(r, s)
        for r in range(8):
            send_left(r, s)
        gather_more(1)
        ffn_up_back(s)
        norm_backward(1, DS, s)
        send_right(7, s)
        gather_more(1)
        out_back(DS, 1, s)
        lax.fori_loop(16 * s, 16 * s + 16, lambda k, carry: (gather_sent(k), carry)[1], 0)
        ffn_share(s)
        attend_back(SQ, 0, s, s, p_refs[2 + s], DQS, DKS, DVS)
        for r in (4, 5, 6):
            send_right(r, s)
        gather_more(1)
        gather_more(1)
        self_back(s)
        norm_backward(0, DC, s)
        send_right(3, s)
        gather_more(1)
        out_back(DC, 0, s)
        attend_back(CQ, 0, s, 1 - s, p_refs[s], DQC, DKC, DVC)
        for r in (0, 1, 2):
            send_right(r, s)
        gather_more(1)
        attention_share(s)

    def vg_copy(r):
        return remote(VG, VR.at[me], s_vg.at[r], r_vg.at[me], role_device(r))

    for r in range(8):

        @pl.when(me != r)
        def _():
            vg_copy(r).start()

    VR[me] = VG[...]
    cross_back(0)
    cross_back(1)

    for p in range(8):

        @pl.when(me != p)
        def _():
            ref = VR.at[p]
            remote(ref, ref, s_vg.at[p], r_vg.at[p], role_device(p)).wait_recv()

    total = VR[0]
    for p in range(1, 8):
        total = total + VR[p]
    VZ[z] = total

    def vz_copy(d):
        return remote(
            VZ.at[z], VZ.at[z], s_vz.at[d - 1], r_vz.at[d - 1], device(x, (z + d) % NZ, y, c)
        )

    for d in range(1, NZ):
        vz_copy(d).start()
    z_collect(1, 1)
    spread_all(1, 1, "start")
    for d in range(1, NZ):
        ref = VZ.at[(z + NZ - d) % NZ]
        remote(ref, ref, s_vz.at[d - 1], r_vz.at[d - 1], device(x, z, y, c)).wait_recv()
    total = VZ[0]
    for zz in range(1, NZ):
        total = total + VZ[zz]
    vec_out[...] = total
    z_collect(0, 1)
    spread_all(0, 1, "start")

    for step in range(1, g.fsdp):
        vec_copy(step).wait_send()
    finish_sends()
    for r in range(8):

        @pl.when(me != r)
        def _():
            vg_copy(r).wait_send()

    for d in range(1, NZ):
        vz_copy(d).wait_send()
        for n in range(2):
            for s in range(2):
                z_send(n, s, d).wait_send()
    spread_wait()
    for n in range(2):
        for s in range(2):
            spread_all(n, s, "wait")


def finish_kernel(g, *refs):
    rows, (ga, gu, gd, vectors) = refs[:8], refs[8:12]
    outs, (g_in, g_out, g_up, g_dn, g_gain, g_bias, g_gate) = refs[12:20], refs[20:]
    for src, dst in zip(rows, outs):
        dst[...] = src[...]

    for s in range(2):

        def unit(m):
            g_in[s, m] = ga[s, m].astype(F32)

        loop(6, unit)
        for m in range(2):
            g_out[s, m] = ga[s, 6 + m].astype(F32)
        g_up[s] = gu[s].astype(F32)
        g_dn[s] = gd[s].astype(F32)
    row = lax.broadcasted_iota(jnp.int32, (g.d, g.rows), 0)
    lane = lax.broadcasted_iota(jnp.int32, (g.d, g.rows), 1)
    pick = jnp.where(row == lane + lax.axis_index("fsdp") * g.rows, 1.0, 0.0)
    own = lax.dot_general(
        vectors[...], pick, (((1,), (0,)), ((), ())),
        precision=lax.Precision.HIGHEST, preferred_element_type=F32,
    )
    for s in range(2):
        for i in range(3):
            g_gain[s, i : i + 1] = own[3 * s + i : 3 * s + i + 1]
            g_bias[s, i : i + 1] = own[6 + 3 * s + i : 7 + 3 * s + i]
    g_gate[...] = own[12:14]


def kernel_path(g, *args):
    rows, lens, cots = args[0:4], args[4:8], args[8:12]
    weights = args[12:16]
    gain, bias, gate = args[16:19]
    D, FF, R, T, T0, T1, NZ = g.d, g.ff, g.rows, g.t, g.t0, g.t1, g.nz
    vec = jnp.concatenate([gain.reshape(6, R), bias.reshape(6, R), gate], axis=0)
    vec = jnp.pad(vec, ((0, 2), (0, 128 - R)))
    vmem = lambda *shape: pltpu.VMEM(shape[:-1], shape[-1])
    dma = lambda *shape: pltpu.SemaphoreType.DMA(shape)
    in_vmem = pl.BlockSpec(memory_space=pltpu.VMEM)
    in_any = pl.BlockSpec(memory_space=pl.ANY)
    in_smem = pl.BlockSpec(memory_space=pltpu.SMEM)
    row_shapes = [jax.ShapeDtypeStruct(r.shape, BF) for r in rows]
    out_shape = row_shapes * 2 + [
        jax.ShapeDtypeStruct((2, 8, R, D), BF),
        jax.ShapeDtypeStruct((2, R, FF), BF),
        jax.ShapeDtypeStruct((2, 4 * R, D), BF),
        jax.ShapeDtypeStruct((16, D), F32),
        jax.ShapeDtypeStruct((8, T, D), BF),
        jax.ShapeDtypeStruct((8, T, D), BF),
        jax.ShapeDtypeStruct((8, T, 2 * D), BF),
        jax.ShapeDtypeStruct((8, T, D), BF),
    ]
    scratch = [
        vmem(2, 16, D, D, BF),
        vmem(g.fsdp, 16, 128, BF),
        vmem(16, D, F32),
        vmem(14, T, D, BF),
        vmem(T, FF, BF),
        vmem(T, FF, BF),
        vmem(3, T, D, BF),
        vmem(3, T, D, BF),
        vmem(T, D, BF),
        vmem(T, D, F32),
        vmem(T, D, F32),
        vmem(T, D, F32),
        vmem(3, T, D, F32),
        vmem(3, T, 1, F32),
        vmem(T, FF, F32),
        vmem(HEADS, T0, T1, F32),
        vmem(HEADS, T1, T0, F32),
        vmem(HEADS, T0, T0, F32),
        vmem(HEADS, T1, T1, F32),
        vmem(2, 2, NZ - 1, D // NZ, D, BF),
        vmem(2, 2, D // NZ, D, BF),
        vmem(16, D, F32),
        vmem(8, 16, D, F32),
        vmem(NZ, 16, D, F32),
        dma(33),
        dma(g.fsdp - 1),
        dma(g.fsdp - 1),
        dma(32, 2, NZ - 1),
        dma(32, NZ - 1),
        dma(32, NZ),
        dma(32, NZ),
        dma(32, 2 * NZ),
        dma(32, 2 * NZ),
        dma(32, 2 * NZ),
        dma(32, 2 * NZ),
        dma(14, 8),
        dma(14, 8),
        dma(18),
        dma(40),
        dma(2, 2, NZ - 1),
        dma(2, 2, NZ - 1),
        dma(4, 8),
        dma(4, 8),
        dma(8),
        dma(8),
        dma(NZ - 1),
        dma(NZ - 1),
    ]
    results = pl.pallas_call(
        partial(layer_kernel, g),
        out_shape=out_shape,
        in_specs=[in_smem] * 4 + [in_vmem] * 8 + [in_any] * 5,
        out_specs=[in_vmem] * 8 + [in_any] * 3 + [in_vmem] + [in_any] * 4,
        scratch_shapes=scratch,
        compiler_params=pltpu.CompilerParams(
            collective_id=0, has_side_effects=True, vmem_limit_bytes=67043328
        ),
        name="layer",
    )(*lens, *rows, *cots, *weights, vec)
    grad_shapes = [
        jax.ShapeDtypeStruct((2, 6, R, D), F32),
        jax.ShapeDtypeStruct((2, 2, R, D), F32),
        jax.ShapeDtypeStruct((2, R, FF), F32),
        jax.ShapeDtypeStruct((2, 4 * R, D), F32),
        jax.ShapeDtypeStruct((2, 3, R), F32),
        jax.ShapeDtypeStruct((2, 3, R), F32),
        jax.ShapeDtypeStruct((2, R), F32),
    ]
    return tuple(
        pl.pallas_call(
            partial(finish_kernel, g),
            out_shape=row_shapes * 2 + grad_shapes,
            in_specs=[in_vmem] * 12,
            out_specs=[in_vmem] * 15,
            name="finish",
        )(*results[:12])
    )


def solution(mesh):
    def per_device(*args):
        g = Geometry(mesh, [a.shape for a in args])
        return kernel_path(g, *args) if g.fits() else plain_path(*args)

    in_specs = (
        P(("dp", "fsdp"), None, None),
        P(("dp", "fsdp"), None, None),
        P(("dp", "fsdp"), None, None),
        P(("dp", "fsdp"), None, None),
        P(("dp", "fsdp")),
        P(("dp", "fsdp")),
        P(("dp", "fsdp")),
        P(("dp", "fsdp")),
        P(("dp", "fsdp"), None, None),
        P(("dp", "fsdp"), None, None),
        P(("dp", "fsdp"), None, None),
        P(("dp", "fsdp"), None, None),
        P(None, None, "fsdp", None),
        P(None, None, "fsdp", None),
        P(None, "fsdp", None),
        P(None, "fsdp", None),
        P(None, None, "fsdp"),
        P(None, None, "fsdp"),
        P(None, "fsdp"),
    )
    out_specs = (
        P(("dp", "fsdp"), None, None),
        P(("dp", "fsdp"), None, None),
        P(("dp", "fsdp"), None, None),
        P(("dp", "fsdp"), None, None),
        P(("dp", "fsdp"), None, None),
        P(("dp", "fsdp"), None, None),
        P(("dp", "fsdp"), None, None),
        P(("dp", "fsdp"), None, None),
        P(None, None, "fsdp", None),
        P(None, None, "fsdp", None),
        P(None, "fsdp", None),
        P(None, "fsdp", None),
        P(None, None, "fsdp"),
        P(None, None, "fsdp"),
        P(None, "fsdp"),
    )
    return jax.shard_map(
        per_device, mesh=mesh, in_specs=in_specs, out_specs=out_specs, check_vma=False
    )
```
